32 devices in a mesh: seq: 4 (over y, core), fsdp: 8 (over z, x).
Axes of the slice: x: 2, y: 2, z: 4, core: 2. Of those that a mesh axis runs over, the one named last changes fastest.
Arguments:
- tokens: bfloat16 [2, 8, 512, 2048], P(None, 'fsdp', 'seq'), may hold values from -6 to 6
- norm_gains: float32 [2, 2048], replicated, may hold values from 0.5 to 1.5
- w_query: bfloat16 [2048, 2048], P('fsdp', 'seq'), may hold values from -0.125 to 0.125
- w_key: bfloat16 [2048, 2048], P('fsdp', 'seq'), may hold values from -0.125 to 0.125
- w_value: bfloat16 [2048, 4096], P('fsdp', 'seq'), may hold values from -0.125 to 0.125
- w_gate: bfloat16 [2048, 4096], P('fsdp', 'seq'), may hold values from -0.125 to 0.125
- w_out: bfloat16 [4096, 2048], P('seq', 'fsdp'), may hold values from -0.1875 to 0.1875
- w_up: bfloat16 [2048, 4096], P('fsdp', 'seq'), may hold values from -0.125 to 0.125
- w_down: bfloat16 [4096, 2048], P('seq', 'fsdp'), may hold values from -0.125 to 0.125
- segments: int32 [2, 8, 512], P(None, 'fsdp'), may hold values from 0 to 3, never falling along the last dimension, each value on 1 to 256 neighbouring positions
- d_output: bfloat16 [2, 8, 512, 2048], P(None, 'fsdp', 'seq'), may hold values from -6 to 6
Outputs:
- output: bfloat16 [2, 8, 512, 2048], P(None, 'fsdp', 'seq')
- d_input: float32 [2, 8, 512, 2048], P(None, 'fsdp', 'seq')
- grad_norms: float32 [2, 2048], replicated
- grad_query: float32 [2048, 2048], P('fsdp', 'seq')
- grad_key: float32 [2048, 2048], P('fsdp', 'seq')
- grad_value: float32 [2048, 4096], P('fsdp', 'seq')
- grad_gate: float32 [2048, 4096], P('fsdp', 'seq')
- grad_out: float32 [4096, 2048], P('seq', 'fsdp')
- grad_up: float32 [2048, 4096], P('fsdp', 'seq')
- grad_down: float32 [4096, 2048], P('seq', 'fsdp')
The draws below stay inside these ranges and needn't reach their ends.
Inputs may be any that keep to these rules, and one draw needn't show every extreme that they name: `segments`: within a sequence the document numbers never fall; each document has 1 to 256 positions, and one has exactly 256.
All inputs are finite; a program needn't handle non-finite values.
Results may differ from the reference program's by a relative error of at most 0.02.
Values may be sent and summed in bfloat16 or wider, within the bound.
No kernel may reach another device: no remote copies, remote signals or barrier semaphores. Data moves between devices by JAX's collectives and lax.ppermute only.
A program may use at most 192 MiB of HBM per device.

```python
import math
import jax
import jax.numpy as jnp
import numpy as np
from jax import lax

D = 2048
HEADS = 8
KEY_HEAD = 256
VAL_HEAD = 512
FF = 4096
LEN = 512
MICRO = 2
DK = 2048
DV = 4096
SEQS = 8


def block_levels(rng, dims, cuts, low, high):
    level, own = 1.0, jax.random.fold_in(rng, 6)
    for position, parts in cuts:
        heights = jnp.exp(jax.random.uniform(jax.random.fold_in(own, position), (parts,), jnp.float32, low / len(cuts), high / len(cuts)))
        level = level * jnp.repeat(heights, dims[position] // parts).reshape([-1 if axis == position else 1 for axis in range(len(dims))])
    return level


def profile(count, total, reach, slope):
    weights = [(1 << 20) // math.isqrt(standing ** slope) + 1 for standing in range(2, count + 1)]
    rest, counts = total - reach - (count - 1), [1] * (count - 1)
    while rest > 0:
        candidates = [i for i in range(count - 1) if counts[i] < reach]
        whole, remaining = sum([weights[i] for i in candidates]), rest
        for i in candidates:
            more = min(reach - counts[i], max(1, remaining * weights[i] // whole), rest)
            counts[i] = counts[i] + more
            rest = rest - more
    return np.array([reach] + counts)


def ragged(own_key, amount, total, bound, lean):
    if amount == 2:
        one = jax.random.randint(own_key, (), max(1, total - bound), min(bound, total - 1) + 1)
        return jnp.stack([one, total - one])
    lengths = jnp.asarray(profile(amount, total, bound, lean), jnp.int32)
    pairs = (amount - 1) // 2
    giver, receiver = lengths[1:1 + 2 * pairs:2], lengths[2:2 + 2 * pairs:2]
    margin = jnp.minimum(giver - 1, bound - receiver)
    moved = jax.random.randint(jax.random.fold_in(own_key, 1), (pairs,), 0, 1 << 20) % (margin + 1)
    lengths = lengths.at[1:1 + 2 * pairs:2].set(giver - moved).at[2:2 + 2 * pairs:2].set(receiver + moved)
    return lengths[jax.random.permutation(jax.random.fold_in(own_key, 2), amount)]


def normal_values(own_key, shape, deviation, limit, shards=(), held_as=jnp.bfloat16):
    values = jax.random.normal(own_key, shape, jnp.float32) * deviation
    if len(shards) > 0:
        values = block_levels(own_key, shape, shards, -0.22, 0.18) * values
    return jnp.clip(values, min=-limit, max=limit).astype(held_as)


def setup_inputs(seed: int = 0) -> dict:
    arg_keys = jax.random.split(jax.random.key(seed), 12)
    tokens = normal_values(arg_keys[0], (MICRO, SEQS, LEN, D), 1.0, 6.0, ((1, 8), (2, 4)))
    norm_gains = jnp.clip(1.0 + 0.1 * jax.random.normal(arg_keys[1], (2, D), jnp.float32), 0.5, 1.5)
    w_query = normal_values(arg_keys[2], (D, DK), D ** -0.5, 0.125, ((0, 8), (1, 4)))
    w_key = normal_values(arg_keys[3], (D, DK), D ** -0.5, 0.125, ((0, 8), (1, 4)))
    w_value = normal_values(arg_keys[4], (D, DV), D ** -0.5, 0.125, ((0, 8), (1, 4)))
    w_gate = normal_values(arg_keys[5], (D, DV), D ** -0.5, 0.125, ((0, 8), (1, 4)))
    w_out = normal_values(arg_keys[6], (DV, D), (DV // 4) ** -0.5, 0.1875, ((0, 4), (1, 8)))
    w_up = normal_values(arg_keys[7], (D, FF), D ** -0.5, 0.125, ((0, 8), (1, 4)))
    w_down = normal_values(arg_keys[8], (FF, D), (FF // 2) ** -0.5, 0.125, ((0, 4), (1, 8)))
    segments = jax.vmap(lambda own: jnp.searchsorted(jnp.cumsum(ragged(own, max(LEN // 128, 3), LEN, LEN // 2, 2)), jnp.arange(LEN), side="right"))(jax.random.split(arg_keys[9], MICRO * SEQS)).reshape((MICRO, SEQS, LEN)).astype(jnp.int32)
    d_output = normal_values(arg_keys[10], (MICRO, SEQS, LEN, D), 1.0, 6.0, ((1, 8), (2, 4)))
    return dict(tokens=tokens, norm_gains=norm_gains, w_query=w_query, w_key=w_key, w_value=w_value, w_gate=w_gate, w_out=w_out, w_up=w_up, w_down=w_down, segments=segments, d_output=d_output)


@jax.custom_vjp
def low(v):
    return lax.optimization_barrier(v.astype(jnp.bfloat16)).astype(jnp.float32)

@jax.custom_vjp
def low_back(v):
    return v

def low_keep(v):
    return (low(v), None)

def low_pass(kept, grad):
    return (grad,)

def back_keep(v):
    return (v, None)

def back_low(kept, grad):
    return (low(grad),)
low.defvjp(low_keep, low_pass)
low_back.defvjp(back_keep, back_low)
eps_norm = 1e-05
eps_group = 1.0

def dense(left, right):
    return jnp.dot(left, right, precision=lax.Precision.HIGHEST, preferred_element_type=jnp.float32)

def layer_norm(inputs, gain_row):
    center = inputs - lax.optimization_barrier(jnp.mean(inputs, axis=-1, keepdims=True))
    scaled = center * lax.rsqrt(lax.optimization_barrier(jnp.mean(center * center, axis=-1, keepdims=True)) + eps_norm)
    return scaled * gain_row

def rotation_tables(length, head_dim):
    half_dim = head_dim // 2
    positions = jnp.arange(length, dtype=jnp.float32)[:, None]
    frequency = jnp.exp(-jnp.log(10000.0) * 2.0 * jnp.arange(half_dim, dtype=jnp.float32) / head_dim)
    angles = positions * frequency[None, :]
    return (jnp.cos(angles), jnp.sin(angles))

def rotate(inputs, cos_table, sin_table):
    half_dim = inputs.shape[-1] // 2
    first_half = inputs[..., :half_dim]
    second_half = inputs[..., half_dim:]
    cos_part = cos_table[:, None, :]
    sin_part = sin_table[:, None, :]
    return jnp.concatenate([first_half * cos_part - second_half * sin_part, second_half * cos_part + first_half * sin_part], axis=-1)

def decay_masks(segment_row, head_ids):
    length = segment_row.shape[0]
    positions = jnp.arange(length, dtype=jnp.int32)
    distance = positions[:, None] - positions[None, :]
    allowed = (distance >= 0) & (segment_row[:, None] == segment_row[None, :])
    log_decay = jnp.log1p(-jnp.exp2(-5.0 - head_ids.astype(jnp.float32)))
    steps_back = jnp.maximum(distance, 0).astype(jnp.float32)
    score_scale = 1.0 / jnp.sqrt(jnp.float32(KEY_HEAD))
    return jnp.where(allowed[None], jnp.exp(steps_back[None] * log_decay[:, None, None]) * score_scale, 0.0)

def retain_one(query_rot, key_rot, values, segment_row):
    decay = decay_masks(segment_row, jnp.arange(HEADS, dtype=jnp.int32))
    scores = low_back(jnp.einsum('nhk,mhk->hnm', query_rot, key_rot, precision=lax.Precision.HIGHEST))
    weights = low(scores * decay)
    return low_back(jnp.einsum('hnm,mhv->nhv', weights, values, precision=lax.Precision.HIGHEST))

def forward(tokens, norm_gains, w_query, w_key, w_value, w_gate, w_out, w_up, w_down, segments):
    seq_count, length, model_width = tokens.shape
    rows_all = seq_count * length
    flat_tokens = tokens.reshape(rows_all, model_width)
    normed_in = low(layer_norm(flat_tokens, norm_gains[0]))
    cos_table, sin_table = rotation_tables(length, KEY_HEAD)
    query = low_back(dense(normed_in, w_query)).reshape(seq_count, length, HEADS, KEY_HEAD)
    key_raw = low_back(dense(normed_in, w_key)).reshape(seq_count, length, HEADS, KEY_HEAD)
    query_rot = low(rotate(query, cos_table, sin_table))
    key_rot = low(rotate(key_raw, cos_table, sin_table))
    values = low(low_back(dense(normed_in, w_value))).reshape(seq_count, length, HEADS, VAL_HEAD)
    gate_raw = low_back(dense(normed_in, w_gate))
    retained = lax.map(jax.checkpoint(lambda pieces: retain_one(*pieces)), (query_rot, key_rot, values, segments))
    mean_square = lax.optimization_barrier(jnp.mean(retained * retained, axis=-1, keepdims=True))
    group_normed = (retained * lax.rsqrt(mean_square + eps_group)).reshape(rows_all, DV)
    gated = low(jax.nn.silu(gate_raw) * group_normed)
    mixed = low_back(dense(gated, w_out))
    resid_mid = flat_tokens + mixed
    normed_mid = low(layer_norm(resid_mid, norm_gains[1]))
    up_input = low_back(dense(normed_mid, w_up))
    activated = low(jax.nn.gelu(up_input, approximate=True))
    ffn_out = low_back(dense(activated, w_down))
    return (resid_mid + ffn_out).reshape(seq_count, length, model_width)

def reference(tokens, norm_gains, w_query, w_key, w_value, w_gate, w_out, w_up, w_down, segments, d_output):
    params = tuple((matrix.astype(jnp.float32) for matrix in (norm_gains, w_query, w_key, w_value, w_gate, w_out, w_up, w_down)))

    def micro_step(running, pieces):
        batch_tokens, batch_segments, batch_grad = pieces

        def apply_layer(inputs, *weights):
            return forward(inputs, *weights, batch_segments)
        outputs, pullback = jax.vjp(apply_layer, batch_tokens.astype(jnp.float32), *params)
        gradients = pullback(batch_grad.astype(jnp.float32))
        updated = tuple((accumulated + increment for accumulated, increment in zip(running, gradients[1:])))
        return (updated, (outputs.astype(jnp.bfloat16), gradients[0]))
    zero_grads = tuple((jnp.zeros_like(matrix) for matrix in params))
    totals, (output, d_input) = lax.scan(micro_step, zero_grads, (tokens, segments, d_output))
    return (output, d_input, totals[0], totals[1], totals[2], totals[3], totals[4], totals[5], totals[6], totals[7])
```

```python
import jax
import jax.numpy as jnp
from jax import lax
from jax.sharding import PartitionSpec as P

KEY_HEAD = 256
VAL_HEAD = 512
eps_norm = 1e-05
eps_group = 1.0
BF = jnp.bfloat16
F32 = jnp.float32
AXES = ("seq", "fsdp")


def mm(left, right):
    return jnp.dot(left, right, preferred_element_type=F32)


def mm_t(left, right):
    return lax.dot_general(left, right, (((1,), (1,)), ((), ())), preferred_element_type=F32)


def mm_tok(left, right):
    return lax.dot_general(left, right, (((0,), (0,)), ((), ())), preferred_element_type=F32)


class Grid:
    def __init__(self, n_seq, n_fsdp):
        self.n_seq, self.n_fsdp = n_seq, n_fsdp
        self.ny, self.nz = n_seq // 2, n_fsdp // 2
        self.masks = [0]
        bit = self.nz // 2
        self.z_bits = []
        while bit:
            self.z_bits.append(bit)
            self.masks = self.masks + [m ^ bit for m in self.masks]
            bit //= 2
        self.y_bits = []
        bit = self.ny // 2
        while bit:
            self.y_bits.append(bit)
            bit //= 2

    def pairs(self, move):
        found = []
        for y in range(self.ny):
            for c in range(2):
                for z in range(self.nz):
                    for x in range(2):
                        y2, c2, z2, x2 = move(y, c, z, x)
                        src = (y * 2 + c) * self.n_fsdp + z * 2 + x
                        dst = (y2 * 2 + c2) * self.n_fsdp + z2 * 2 + x2
                        if src != dst:
                            found.append((src, dst))
        return found

    def send(self, value, move):
        return lax.ppermute(value, AXES, self.pairs(move))

    def flip_z(self, value, bit):
        return self.send(value, lambda y, c, z, x: (y, c, z ^ bit, x))

    def flip_c(self, value):
        return self.send(value, lambda y, c, z, x: (y, 1 - c, z, x))

    def flip_y(self, value, bit):
        return self.send(value, lambda y, c, z, x: (y ^ bit, c, z, x))

    def flip_x(self, value):
        return self.send(value, lambda y, c, z, x: (y, c, z, 1 - x))

    def swap(self, value, same):
        other = self.send(value, lambda y, c, z, x: (y, x, z, c))
        return jnp.where(same, value, other)


def gather_weight(grid, shard):
    held = shard
    for bit in grid.z_bits:
        held = jnp.concatenate([held, grid.flip_z(held, bit)], axis=0)
    return jnp.concatenate([held, grid.flip_c(held)], axis=0)


def scatter_grad(grid, grad, same):
    half = grad.shape[0] // 2
    held = grad[:half] + grid.flip_c(grad[half:].astype(BF)).astype(F32)
    for bit in reversed(grid.z_bits):
        half = held.shape[0] // 2
        held = held[:half] + grid.flip_z(held[half:].astype(BF), bit).astype(F32)
    return held


def gather_tokens(grid, block):
    held = block
    for bit in grid.y_bits:
        held = jnp.concatenate([held, grid.flip_y(held, bit)], axis=0)
    return jnp.concatenate([held, grid.flip_x(held)], axis=0)


def scatter_tokens(grid, partial):
    half = partial.shape[0] // 2
    held = partial[:half] + grid.flip_x(partial[half:].astype(BF)).astype(F32)
    for bit in reversed(grid.y_bits):
        half = held.shape[0] // 2
        held = held[:half] + grid.flip_y(held[half:].astype(BF), bit).astype(F32)
    return held


def layer_norm_parts(inputs, gain_row):
    center = inputs - jnp.mean(inputs, axis=-1, keepdims=True)
    inverse = lax.rsqrt(jnp.mean(center * center, axis=-1, keepdims=True) + eps_norm)
    scaled = center * inverse
    return (scaled * gain_row, scaled, inverse)


def layer_norm_back(incoming, scaled, inverse, gain_row):
    upstream = incoming * gain_row
    centered_grad = (
        upstream
        - jnp.mean(upstream, axis=-1, keepdims=True)
        - scaled * jnp.mean(upstream * scaled, axis=-1, keepdims=True)
    )
    return (centered_grad * inverse, jnp.sum(incoming * scaled, axis=0))


def rotate(inputs, cos_table, sin_table, sign):
    pieces = []
    half = KEY_HEAD // 2
    for start in range(0, inputs.shape[-1], KEY_HEAD):
        first = inputs[:, start : start + half]
        second = inputs[:, start + half : start + KEY_HEAD]
        pieces.append(first * cos_table - sign * (second * sin_table))
        pieces.append(second * cos_table + sign * (first * sin_table))
    return jnp.concatenate(pieces, axis=-1)


def decay_masks(segment_row, positions, head_ids):
    distance = positions[:, None] - positions[None, :]
    allowed = (distance >= 0) & (segment_row[:, None] == segment_row[None, :])
    log_decay = jnp.log1p(-jnp.exp2(-5.0 - head_ids.astype(F32)))
    steps_back = jnp.maximum(distance, 0).astype(F32)
    score_scale = 1.0 / jnp.sqrt(F32(KEY_HEAD))
    return jnp.where(
        allowed[None], jnp.exp(steps_back[None] * log_decay[:, None, None]) * score_scale, 0.0
    )


def make_on_device(grid):
    n_slots = grid.n_fsdp

    def on_device(
        tokens, norm_gains, w_query, w_key, w_value, w_gate, w_out, w_up, w_down, segments, d_output
    ):
        micro = tokens.shape[0]
        piece = tokens.shape[2]
        width = tokens.shape[3]
        col = width // n_slots
        heads_here = w_query.shape[1] // KEY_HEAD
        dk = heads_here * KEY_HEAD
        seq_id = lax.axis_index("seq")
        fsdp_id = lax.axis_index("fsdp")
        y, c = seq_id // 2, seq_id % 2
        z, x = fsdp_id // 2, fsdp_id % 2
        same = x == c
        place = y * 2 + x
        head_ids = place * heads_here + jnp.arange(heads_here, dtype=jnp.int32)

        slot_block = [2 * (z ^ m) + (c ^ p) for p in range(2) for m in grid.masks]
        back = jnp.asarray([grid.masks.index(m) for m in range(grid.nz)], jnp.int32)
        block_slot = [
            (p ^ c) * grid.nz + back[zb ^ z] for zb in range(grid.nz) for p in range(2)
        ]

        def pick(value, blocks):
            return jnp.concatenate(
                [lax.dynamic_slice_in_dim(value, b * col, col, axis=-1) for b in blocks], axis=-1
            )

        shards = [
            jnp.concatenate([w_query, w_key], axis=1),
            w_value,
            w_gate,
            w_out.T,
            w_up,
            w_down.T,
        ]
        toks = grid.swap(tokens.reshape(micro * piece, width), same)
        segs = grid.swap(segments.reshape(micro, -1), same)
        shards = [grid.swap(s, same) for s in shards]
        full_qk, full_v, full_g, full_o, full_u, full_d = [gather_weight(grid, s) for s in shards]
        cots = grid.swap(d_output.reshape(micro * piece, width), same)

        gains = pick(norm_gains, slot_block)
        gain_in, gain_mid = gains[0], gains[1]
        xin = pick(toks, slot_block).astype(F32)
        cot_own = pick(cots, slot_block)

        y_masks = [0]
        for bit in grid.y_bits:
            y_masks = y_masks + [m ^ bit for m in y_masks]
        ranks = [2 * (y ^ m) + (x ^ p) for p in range(2) for m in y_masks]
        positions = jnp.concatenate(
            [r * piece + jnp.arange(piece, dtype=jnp.int32) for r in ranks]
        )
        half = KEY_HEAD // 2
        frequency = jnp.exp(
            -jnp.log(10000.0) * 2.0 * jnp.arange(half, dtype=F32) / KEY_HEAD
        )
        angles = positions.astype(F32)[:, None] * frequency[None, :]
        cos_table, sin_table = jnp.cos(angles), jnp.sin(angles)
        segs_order = [
            jnp.concatenate(
                [lax.dynamic_slice_in_dim(segs[b], r * piece, piece) for r in ranks]
            )
            for b in range(micro)
        ]

        def rows(value, b):
            return value[b * piece : (b + 1) * piece]

        normed, scaled_in, inverse_in = layer_norm_parts(xin, gain_in)
        normed = normed.astype(BF)
        saved = []
        outs = []
        for b in range(micro):
            h1 = gather_tokens(grid, rows(normed, b))
            qk = mm(h1, full_qk)
            qr = rotate(qk[:, :dk], cos_table, sin_table, 1.0).astype(BF)
            kr = rotate(qk[:, dk:], cos_table, sin_table, 1.0).astype(BF)
            values = mm(h1, full_v).astype(BF)
            gate = mm(h1, full_g)
            decay = decay_masks(segs_order[b], positions, head_ids)
            weights, retained = [], []
            for h in range(heads_here):
                ks = slice(h * KEY_HEAD, (h + 1) * KEY_HEAD)
                vs = slice(h * VAL_HEAD, (h + 1) * VAL_HEAD)
                w = (mm_t(qr[:, ks], kr[:, ks]) * decay[h]).astype(BF)
                weights.append(w)
                retained.append(mm(w, values[:, vs]))
            rgroup = [
                lax.rsqrt(jnp.mean(r * r, axis=-1, keepdims=True) + eps_group) for r in retained
            ]
            ynorm = jnp.concatenate([r * g for r, g in zip(retained, rgroup)], axis=-1)
            sig = jax.nn.sigmoid(gate)
            swish = gate * sig
            gated = (swish * ynorm).astype(BF)
            mixed = scatter_tokens(grid, mm_t(gated, full_o))
            x1 = rows(xin, b) + mixed
            normed_mid, scaled_mid, inverse_mid = layer_norm_parts(x1, gain_mid)
            h2 = gather_tokens(grid, normed_mid.astype(BF))
            up = mm(h2, full_u)
            act, gelu_pull = jax.vjp(lambda t: jax.nn.gelu(t, approximate=True), up)
            act = act.astype(BF)
            ffn = scatter_tokens(grid, mm_t(act, full_d))
            outs.append((x1 + ffn).astype(BF))
            saved.append(
                (h1, qr, kr, values, gate, sig, swish, decay, weights, rgroup, ynorm, gated)
                + (scaled_mid, inverse_mid, h2, gelu_pull, act)
            )

        sums = [None] * 6
        gain_grads = None
        d_inputs = []
        stage = []
        for b in range(micro):
            act, gelu_pull, h2 = saved[b][16], saved[b][15], saved[b][14]
            cot = gather_tokens(grid, rows(cot_own, b))
            g_down = mm_tok(cot, act)
            d_act = mm(cot, full_d)
            d_up = gelu_pull(d_act)[0].astype(BF)
            g_up = mm_tok(h2, d_up)
            d_h2 = scatter_tokens(grid, mm_t(d_up, full_u))
            stage.append((g_down, g_up, d_h2))
        rest = []
        for b in range(micro):
            (h1, qr, kr, values, gate, sig, swish, decay, weights, rgroup, ynorm, gated) = saved[b][:12]
            scaled_mid, inverse_mid = saved[b][12:14]
            g_down, g_up, d_h2 = stage[b]
            d_ln, gain_mid_grad = layer_norm_back(d_h2, scaled_mid, inverse_mid, gain_mid)
            d_x1 = rows(cot_own, b).astype(F32) + d_ln
            d_mix = gather_tokens(grid, d_x1.astype(BF))
            d_gated = mm(d_mix, full_o)
            g_out = mm_tok(d_mix, gated)
            d_gate = (d_gated * ynorm * sig * (1.0 + gate * (1.0 - sig))).astype(BF)
            d_yn = d_gated * swish
            d_q, d_k, d_v = [], [], []
            for h in range(heads_here):
                ks = slice(h * KEY_HEAD, (h + 1) * KEY_HEAD)
                vs = slice(h * VAL_HEAD, (h + 1) * VAL_HEAD)
                dy_h, yn_h = d_yn[:, vs], ynorm[:, vs]
                d_ret = (
                    (dy_h - yn_h * jnp.mean(dy_h * yn_h, axis=-1, keepdims=True)) * rgroup[h]
                ).astype(BF)
                d_w = mm_t(d_ret, values[:, vs])
                d_v.append(mm_tok(weights[h], d_ret).astype(BF))
                d_s = (d_w * decay[h]).astype(BF)
                d_q.append(mm(d_s, kr[:, ks]))
                d_k.append(mm_tok(d_s, qr[:, ks]))
            d_qk = rotate(
                jnp.concatenate(d_q + d_k, axis=-1), cos_table, sin_table, -1.0
            ).astype(BF)
            d_v = jnp.concatenate(d_v, axis=-1)
            d_h1 = mm_t(d_qk, full_qk) + mm_t(d_v, full_v) + mm_t(d_gate, full_g)
            d_h1 = scatter_tokens(grid, d_h1)
            d_ln1, gain_in_grad = layer_norm_back(
                d_h1, rows(scaled_in, b), rows(inverse_in, b), gain_in
            )
            d_inputs.append(d_x1 + d_ln1)
            grads = (
                mm_tok(h1, d_qk),
                mm_tok(h1, d_v),
                mm_tok(h1, d_gate),
                g_out,
                g_up,
                g_down,
            )
            sums = [g if s is None else s + g for s, g in zip(sums, grads)]
            both = jnp.stack([gain_in_grad, gain_mid_grad])
            gain_grads = both if gain_grads is None else gain_grads + both

        def finish(value):
            moved = grid.send(value.astype(BF), lambda y, c, z, x: (y, x, z, c))
            return jnp.where(same, value, moved.astype(value.dtype))

        done = [finish(scatter_grad(grid, g, same)) for g in sums]
        grad_norms = lax.psum(pick(gain_grads, block_slot), AXES)
        output = finish(pick(jnp.concatenate(outs), block_slot))
        d_input = finish(pick(jnp.concatenate(d_inputs), block_slot))
        shape = (micro, 1, piece, width)
        return (
            output.reshape(shape),
            d_input.reshape(shape),
            grad_norms,
            done[0][:, :dk],
            done[0][:, dk:],
            done[1],
            done[2],
            done[3].T,
            done[4],
            done[5].T,
        )

    return on_device


def solution(mesh):
    grid = Grid(mesh.shape["seq"], mesh.shape["fsdp"])
    rows = P("fsdp", "seq")
    cols = P("seq", "fsdp")
    tok = P(None, "fsdp", "seq", None)
    return jax.shard_map(
        make_on_device(grid),
        mesh=mesh,
        in_specs=(tok, P(), rows, rows, rows, rows, cols, rows, cols, P(None, "fsdp", None), tok),
        out_specs=(tok, tok, P(), rows, rows, rows, rows, cols, rows, cols),
        check_vma=False,
    )
```

```python
import functools

import jax
import jax.numpy as jnp
from jax import lax
from jax.experimental import pallas as pl
from jax.experimental.pallas import tpu as pltpu
from jax.sharding import PartitionSpec as P

KEY_HEAD = 256
VAL_HEAD = 512
ROT = KEY_HEAD // 2
eps_norm = 1e-05
eps_group = 1.0
BF = jnp.bfloat16
F32 = jnp.float32
AXES = ("seq", "fsdp")
ANY = pl.BlockSpec(memory_space=pl.ANY)


def nn(left, right):
    return jnp.dot(left, right, preferred_element_type=F32)


def nt(left, right):
    return lax.dot_general(left, right, (((1,), (1,)), ((), ())), preferred_element_type=F32)


def tn(left, right):
    return lax.dot_general(left, right, (((0,), (0,)), ((), ())), preferred_element_type=F32)


def after(value, *first):
    return lax.optimization_barrier((value, *first))[0]


class Grid:
    def __init__(self, n_seq, n_fsdp):
        assert n_seq == 4 and n_fsdp % 2 == 0
        self.n_fsdp, self.nz = n_fsdp, n_fsdp // 2
        self.lines = [[z * 2 + x for z in range(self.nz)] for x in range(2)]

    def send(self, value, move):
        found = []
        for y in range(2):
            for c in range(2):
                for z in range(self.nz):
                    for x in range(2):
                        y2, c2, z2, x2 = move(y, c, z, x)
                        src = (y * 2 + c) * self.n_fsdp + z * 2 + x
                        dst = (y2 * 2 + c2) * self.n_fsdp + z2 * 2 + x2
                        if src != dst:
                            found.append((src, dst))
        return lax.ppermute(value, AXES, found)

    def flip_z(self, value, bit):
        return self.send(value, lambda y, c, z, x: (y, c, z ^ bit, x))

    def flip_c(self, value):
        return self.send(value, lambda y, c, z, x: (y, 1 - c, z, x))

    def flip_y(self, value):
        return self.send(value, lambda y, c, z, x: (1 - y, c, z, x))

    def flip_x(self, value):
        return self.send(value, lambda y, c, z, x: (y, c, z, 1 - x))

    def first(self, b, value):
        return self.flip_y(value) if b == 0 else self.flip_x(value)

    def second(self, b, value):
        return self.flip_x(value) if b == 0 else self.flip_y(value)

    def swap(self, value, same):
        other = self.send(value.astype(BF), lambda y, c, z, x: (y, x, z, c))
        return jnp.where(same, value, other.astype(value.dtype))

    def gather_line(self, shard):
        return lax.all_gather(shard, "fsdp", axis=0, tiled=True, axis_index_groups=self.lines)

    def scatter_line(self, value):
        return lax.psum_scatter(
            value, "fsdp", scatter_dimension=0, tiled=True, axis_index_groups=self.lines
        )

    def gather_tokens(self, b, block):
        other = self.first(b, block)
        return (block, other, self.second(b, jnp.concatenate([block, other], axis=0)))

    def scatter_tokens(self, b, sent, kept):
        n = kept.shape[0] // 2
        got = self.second(b, sent).astype(F32)
        more = self.first(b, (kept[n:] + got[n:]).astype(BF)).astype(F32)
        return kept[:n] + got[:n] + more

    def total(self, value):
        for flip in (self.flip_y, self.flip_x, self.flip_c):
            value = value + flip(value)
        if self.nz & (self.nz - 1):
            return lax.psum(value, "fsdp", axis_index_groups=self.lines)
        bit = 1
        while bit < self.nz:
            value = value + self.flip_z(value, bit)
            bit *= 2
        return value


def call(body, grid, ins, outs, shapes, scratch=(), flops=0, moved=0):
    return pl.pallas_call(
        body,
        out_shape=shapes,
        grid=grid,
        in_specs=ins,
        out_specs=outs,
        scratch_shapes=list(scratch),
        cost_estimate=pl.CostEstimate(flops=flops, bytes_accessed=moved, transcendentals=0),
        compiler_params=pltpu.CompilerParams(vmem_limit_bytes=48 << 20),
    )


def shape(rows, cols, dtype=BF):
    return jax.ShapeDtypeStruct((rows, cols), dtype)


def spec(rows, cols, index):
    return pl.BlockSpec((rows, cols), index)


def fetch(pieces, target, sems):
    copies, row = [], 0
    for i, piece in enumerate(pieces):
        rows = piece.shape[0]
        copies.append(pltpu.make_async_copy(piece, target.at[pl.ds(row, rows)], sems.at[i]))
        row += rows
    for copy in copies:
        copy.start()
    for copy in copies:
        copy.wait()


def assemble(pieces):
    n = len(pieces)

    def body(*refs):
        fetch(refs[:n], refs[n], refs[n + 1])

    rows = sum(p.shape[0] for p in pieces)
    cols = pieces[0].shape[1]
    return pl.pallas_call(
        body,
        out_shape=shape(rows, cols),
        in_specs=[ANY] * n,
        out_specs=ANY,
        scratch_shapes=[pltpu.SemaphoreType.DMA((n,))],
        cost_estimate=pl.CostEstimate(
            flops=0, bytes_accessed=4 * rows * cols, transcendentals=0
        ),
    )(*pieces)


def rotated(first, second, cos_part, sin_part):
    return (first * cos_part - second * sin_part, second * cos_part + first * sin_part)


def project_qkv(pieces, w_own, w_oth, cos_table, sin_table, rotate_cols):
    n = len(pieces)
    rows = sum(p.shape[0] for p in pieces)
    width = pieces[0].shape[1]
    half, cols = w_own.shape
    tile, chunk = 512, 256

    def body(*refs):
        a, b, cos_ref, sin_ref, h_ref, o_ref, sems = refs[n:]
        j = pl.program_id(0)

        @pl.when(j == 0)
        def _():
            fetch(refs[:n], h_ref, sems)

        turn = j * tile < rotate_cols

        def step(i, _):
            at = pl.ds(pl.multiple_of(i * chunk, chunk), chunk)
            acc = nn(h_ref[at, :half], a[...]) + nn(h_ref[at, half:], b[...])
            cos_part = jnp.where(turn, cos_ref[at, :], 1.0)
            sin_part = jnp.where(turn, sin_ref[at, :], 0.0)
            for s in range(0, tile, KEY_HEAD):
                u, v = rotated(
                    acc[:, s : s + ROT], acc[:, s + ROT : s + KEY_HEAD], cos_part, sin_part
                )
                o_ref[at, s : s + ROT] = u.astype(BF)
                o_ref[at, s + ROT : s + KEY_HEAD] = v.astype(BF)
            return 0

        lax.fori_loop(0, rows // chunk, step, 0)

    return call(
        body,
        (cols // tile,),
        [ANY] * n
        + [spec(half, tile, lambda j: (0, j))] * 2
        + [spec(rows, ROT, lambda j: (0, 0))] * 2,
        [spec(rows, width, lambda j: (0, 0)), spec(rows, tile, lambda j: (0, j))],
        [shape(rows, width), shape(rows, cols)],
        [pltpu.SemaphoreType.DMA((n,))],
        2 * rows * width * cols,
        2 * (2 * rows * width + width * cols + rows * cols),
    )(*pieces, w_own, w_oth, cos_table, sin_table)


def decay_chunk(col_ref, row_ref, at, log_gamma):
    pos_n, seg_n = col_ref[at, 0:1], col_ref[at, 1:2]
    pos_m, seg_m = row_ref[0:1, :], row_ref[1:2, :]
    distance = pos_n - pos_m
    allowed = (distance >= 0.0) & (seg_n == seg_m)
    value = jnp.exp(jnp.maximum(distance, 0.0) * log_gamma) * (KEY_HEAD**-0.5)
    return jnp.where(allowed, value, 0.0)


def sigmoid(value):
    return 1.0 / (1.0 + jnp.exp(-value))


def retain(b, h1, qkv, w1_own, w1_oth, col_info, row_info, log_gamma, heads):
    width = h1.shape[1]
    half = width // 2
    rows = h1.shape[0] // 2
    dv = heads * VAL_HEAD
    chunk = 256

    def body(h_ref, ga, gb, oa, ob, q_ref, k_ref, v_ref, col_ref, row_ref, lg_ref,
             gate_ref, gated_ref, sent_ref, kept_ref, acc_ref):
        h = pl.program_id(0)
        log_g = lg_ref[h]

        def step(i, _):
            at = pl.ds(pl.multiple_of(i * chunk, chunk), chunk)
            gate = nn(h_ref[at, :half], ga[...]) + nn(h_ref[at, half:], gb[...])
            gate_ref[at, :] = gate
            decay = decay_chunk(col_ref, row_ref, at, log_g)
            weights = (nt(q_ref[at, :], k_ref[...]) * decay).astype(BF)
            kept = nn(weights, v_ref[...])
            scale = lax.rsqrt(jnp.mean(kept * kept, axis=-1, keepdims=True) + eps_group)
            gated = (gate * sigmoid(gate) * (kept * scale)).astype(BF)
            gated_ref[at, :] = gated
            left, right = nt(gated, oa[...]), nt(gated, ob[...])

            @pl.when(h == 0)
            def _():
                acc_ref[at, :half] = left
                acc_ref[at, half:] = right

            @pl.when(h != 0)
            def _():
                acc_ref[at, :half] = acc_ref[at, :half] + left
                acc_ref[at, half:] = acc_ref[at, half:] + right

            return 0

        lax.fori_loop(0, rows // chunk, step, 0)

        @pl.when(h == heads - 1)
        def _():
            kept_ref[...] = acc_ref[: rows // 2, :]
            sent_ref[...] = acc_ref[rows // 2 :, :].astype(BF)

    gate_spec = spec(half, VAL_HEAD, lambda h: (0, h))
    out_spec = spec(half, VAL_HEAD, lambda h: (0, heads + h))
    return call(
        body,
        (heads,),
        [
            spec(rows, width, lambda h: (b, 0)),
            gate_spec,
            gate_spec,
            out_spec,
            out_spec,
            spec(rows, KEY_HEAD, lambda h: (b, h)),
            spec(rows, KEY_HEAD, lambda h: (b, heads + h)),
            spec(rows, VAL_HEAD, lambda h: (b, heads + h)),
            spec(rows, 128, lambda h: (b, 0)),
            spec(8, rows, lambda h: (b, 0)),
            pl.BlockSpec(memory_space=pltpu.SMEM),
        ],
        [
            spec(rows, VAL_HEAD, lambda h: (0, h)),
            spec(rows, VAL_HEAD, lambda h: (0, h)),
            spec(rows // 2, width, lambda h: (0, 0)),
            spec(rows // 2, width, lambda h: (0, 0)),
        ],
        [
            shape(rows, dv, F32),
            shape(rows, dv),
            shape(rows // 2, width),
            shape(rows // 2, width, F32),
        ],
        [pltpu.VMEM((rows, width), F32)],
        4 * rows * width * dv + 2 * rows * rows * heads * (KEY_HEAD + VAL_HEAD),
        2 * rows * width + 4 * width * dv + 8 * rows * dv + 3 * rows * width,
    )(h1, w1_own, w1_oth, w1_own, w1_oth, qkv, qkv, qkv, col_info, row_info, log_gamma)


ROOT_2_PI = 0.7978845608028654


def feed_up(pieces, w2_own, w2_oth, hidden):
    n = len(pieces)
    rows = sum(p.shape[0] for p in pieces)
    width = pieces[0].shape[1]
    half = width // 2
    tile, chunk = 512, 256

    def body(*refs):
        a, b, h_ref, act_ref, slope_ref, sems = refs[n:]

        @pl.when(pl.program_id(0) == 0)
        def _():
            fetch(refs[:n], h_ref, sems)

        def step(i, _):
            at = pl.ds(pl.multiple_of(i * chunk, chunk), chunk)
            up = nn(h_ref[at, :half], a[...]) + nn(h_ref[at, half:], b[...])
            square = up * up
            bent = jnp.tanh(ROOT_2_PI * (up + 0.044715 * square * up))
            act_ref[at, :] = (0.5 * up * (1.0 + bent)).astype(BF)
            inner = ROOT_2_PI * (1.0 + 3.0 * 0.044715 * square)
            slope = 0.5 * (1.0 + bent) + 0.5 * up * (1.0 - bent * bent) * inner
            slope_ref[at, :] = slope
            return 0

        lax.fori_loop(0, rows // chunk, step, 0)

    return call(
        body,
        (hidden // tile,),
        [ANY] * n + [spec(half, tile, lambda j: (0, j))] * 2,
        [spec(rows, width, lambda j: (0, 0))] + [spec(rows, tile, lambda j: (0, j))] * 2,
        [shape(rows, width), shape(rows, hidden), shape(rows, hidden, F32)],
        [pltpu.SemaphoreType.DMA((n,))],
        2 * rows * width * hidden,
        4 * rows * width + 2 * width * hidden + 6 * rows * hidden,
    )(*pieces, w2_own, w2_oth)


def feed_down(act, w2_own, w2_oth, hidden):
    rows = act.shape[0]
    half = w2_own.shape[0]
    width = 2 * half
    tile, chunk = 512, 256
    steps = hidden // tile

    def body(act_ref, a, b, sent_ref, kept_ref, acc_ref):
        j = pl.program_id(0)

        def step(i, _):
            at = pl.ds(pl.multiple_of(i * chunk, chunk), chunk)
            left, right = nt(act_ref[at, :], a[...]), nt(act_ref[at, :], b[...])

            @pl.when(j == 0)
            def _():
                acc_ref[at, :half] = left
                acc_ref[at, half:] = right

            @pl.when(j != 0)
            def _():
                acc_ref[at, :half] = acc_ref[at, :half] + left
                acc_ref[at, half:] = acc_ref[at, half:] + right

            return 0

        lax.fori_loop(0, rows // chunk, step, 0)

        @pl.when(j == steps - 1)
        def _():
            kept_ref[...] = acc_ref[: rows // 2, :]
            sent_ref[...] = acc_ref[rows // 2 :, :].astype(BF)

    return call(
        body,
        (steps,),
        [spec(rows, tile, lambda j: (0, j))]
        + [spec(half, tile, lambda j: (0, steps + j))] * 2,
        [spec(rows // 2, width, lambda j: (0, 0))] * 2,
        [shape(rows // 2, width), shape(rows // 2, width, F32)],
        [pltpu.VMEM((rows, width), F32)],
        2 * rows * width * hidden,
        2 * rows * hidden + 2 * width * hidden + 3 * rows * width,
    )(act, w2_own, w2_oth)


def feed_back(b, cot, slope, w2_own, w2_oth, hidden):
    width = cot.shape[1]
    half = width // 2
    rows = slope.shape[0]
    tile, chunk = 512, 256
    steps = hidden // tile

    def body(cot_ref, slope_ref, da, db, ua, ub, dup_ref, sent_ref, kept_ref, acc_ref):
        j = pl.program_id(0)

        def step(i, _):
            at = pl.ds(pl.multiple_of(i * chunk, chunk), chunk)
            d_act = nn(cot_ref[at, :half], da[...]) + nn(cot_ref[at, half:], db[...])
            d_up = (d_act * slope_ref[at, :]).astype(BF)
            dup_ref[at, :] = d_up
            left, right = nt(d_up, ua[...]), nt(d_up, ub[...])

            @pl.when(j == 0)
            def _():
                acc_ref[at, :half] = left
                acc_ref[at, half:] = right

            @pl.when(j != 0)
            def _():
                acc_ref[at, :half] = acc_ref[at, :half] + left
                acc_ref[at, half:] = acc_ref[at, half:] + right

            return 0

        lax.fori_loop(0, rows // chunk, step, 0)

        @pl.when(j == steps - 1)
        def _():
            kept_ref[...] = acc_ref[: rows // 2, :]
            sent_ref[...] = acc_ref[rows // 2 :, :].astype(BF)

    return call(
        body,
        (steps,),
        [spec(rows, width, lambda j: (b, 0)), spec(rows, tile, lambda j: (0, j))]
        + [spec(half, tile, lambda j: (0, steps + j))] * 2
        + [spec(half, tile, lambda j: (0, j))] * 2,
        [spec(rows, tile, lambda j: (0, j))] + [spec(rows // 2, width, lambda j: (0, 0))] * 2,
        [shape(rows, hidden), shape(rows // 2, width), shape(rows // 2, width, F32)],
        [pltpu.VMEM((rows, width), F32)],
        4 * rows * width * hidden,
        5 * rows * width + 4 * width * hidden + 6 * rows * hidden,
    )(cot, slope, w2_own, w2_oth, w2_own, w2_oth)


def retain_back(b, pieces, gate, qkv, weights, col_info, row_info, cos_table, sin_table,
                log_gamma, heads):
    w0_own, w0_oth, w1_own, w1_oth = weights
    n = len(pieces)
    rows = sum(p.shape[0] for p in pieces)
    width = pieces[0].shape[1]
    half = width // 2
    dk, dv = heads * KEY_HEAD, heads * VAL_HEAD
    chunk = 256

    def body(*refs):
        (oa, ob, ga, gb, va, vb, qa, qb, ka, kb, gate_ref, q_ref, k_ref, v_ref, col_ref, row_ref,
         cos_ref, sin_ref, lg_ref, mix_ref, dgate_ref, dq_ref, dk_ref, dv_ref, sent_ref, kept_ref,
         acc_ref, dk_acc, dv_acc, sems) = refs[n:]
        h = pl.program_id(0)
        log_g = lg_ref[h]

        @pl.when(h == 0)
        def _():
            fetch(refs[:n], mix_ref, sems)

        def step(i, _):
            at = pl.ds(pl.multiple_of(i * chunk, chunk), chunk)
            d_gated = nn(mix_ref[at, :half], oa[...]) + nn(mix_ref[at, half:], ob[...])
            decay = decay_chunk(col_ref, row_ref, at, log_g)
            weights = (nt(q_ref[at, :], k_ref[...]) * decay).astype(BF)
            kept = nn(weights, v_ref[...])
            scale = lax.rsqrt(jnp.mean(kept * kept, axis=-1, keepdims=True) + eps_group)
            y_norm = kept * scale
            gate = gate_ref[at, :]
            sig = sigmoid(gate)
            d_gate = d_gated * y_norm * sig * (1.0 + gate * (1.0 - sig))
            dgate_ref[at, :] = d_gate.astype(BF)
            d_y = d_gated * (gate * sig)
            d_ret = (
                scale * (d_y - y_norm * jnp.mean(d_y * y_norm, axis=-1, keepdims=True))
            ).astype(BF)
            d_weights = nt(d_ret, v_ref[...])
            d_scores = (d_weights * decay).astype(BF)
            d_v = tn(weights, d_ret)
            d_k = tn(d_scores, q_ref[at, :])
            d_q = nn(d_scores, k_ref[...])
            u, v = rotated(d_q[:, :ROT], d_q[:, ROT:], cos_ref[at, :], -sin_ref[at, :])
            dq_ref[at, :ROT] = u.astype(BF)
            dq_ref[at, ROT:] = v.astype(BF)

            @pl.when(i == 0)
            def _():
                dk_acc[...] = d_k
                dv_acc[...] = d_v

            @pl.when(i != 0)
            def _():
                dk_acc[...] = dk_acc[...] + d_k
                dv_acc[...] = dv_acc[...] + d_v

            return 0

        lax.fori_loop(0, rows // chunk, step, 0)
        dv_ref[...] = dv_acc[...].astype(BF)
        u, v = rotated(dk_acc[:, :ROT], dk_acc[:, ROT:], cos_ref[...], -sin_ref[...])
        dk_ref[:, :ROT] = u.astype(BF)
        dk_ref[:, ROT:] = v.astype(BF)

        def back(i, _):
            at = pl.ds(pl.multiple_of(i * chunk, chunk), chunk)
            pairs = ((qa, ka, va, ga), (qb, kb, vb, gb))
            for side, (wq, wk, wv, wg) in enumerate(pairs):
                cols = slice(side * half, (side + 1) * half)
                part = (
                    nt(dq_ref[at, :], wq[...])
                    + nt(dk_ref[at, :], wk[...])
                    + nt(dv_ref[at, :], wv[...])
                    + nt(dgate_ref[at, :], wg[...])
                )

                @pl.when(h == 0)
                def _():
                    acc_ref[at, cols] = part

                @pl.when(h != 0)
                def _():
                    acc_ref[at, cols] = acc_ref[at, cols] + part

            return 0

        lax.fori_loop(0, rows // chunk, back, 0)

        @pl.when(h == heads - 1)
        def _():
            kept_ref[...] = acc_ref[: rows // 2, :]
            sent_ref[...] = acc_ref[rows // 2 :, :].astype(BF)

    wide = [spec(half, VAL_HEAD, lambda h: (0, heads + h))] * 2
    gate_w = [spec(half, VAL_HEAD, lambda h: (0, h))] * 2
    q_w = [spec(half, KEY_HEAD, lambda h: (0, h))] * 2
    k_w = [spec(half, KEY_HEAD, lambda h: (0, heads + h))] * 2
    per_head = spec(rows, VAL_HEAD, lambda h: (0, h))
    per_key = spec(rows, KEY_HEAD, lambda h: (0, h))
    whole = spec(rows // 2, width, lambda h: (0, 0))
    return call(
        body,
        (heads,),
        [ANY] * n
        + wide
        + gate_w
        + wide
        + q_w
        + k_w
        + [
            per_head,
            spec(rows, KEY_HEAD, lambda h: (b, h)),
            spec(rows, KEY_HEAD, lambda h: (b, heads + h)),
            spec(rows, VAL_HEAD, lambda h: (b, heads + h)),
            spec(rows, 128, lambda h: (b, 0)),
            spec(8, rows, lambda h: (b, 0)),
            spec(rows, ROT, lambda h: (b, 0)),
            spec(rows, ROT, lambda h: (b, 0)),
            pl.BlockSpec(memory_space=pltpu.SMEM),
        ],
        [
            spec(rows, width, lambda h: (0, 0)),
            per_head,
            per_key,
            per_key,
            per_head,
            whole,
            whole,
        ],
        [
            shape(rows, width),
            shape(rows, dv),
            shape(rows, dk),
            shape(rows, dk),
            shape(rows, dv),
            shape(rows // 2, width),
            shape(rows // 2, width, F32),
        ],
        [
            pltpu.VMEM((rows, width), F32),
            pltpu.VMEM((rows, KEY_HEAD), F32),
            pltpu.VMEM((rows, VAL_HEAD), F32),
            pltpu.SemaphoreType.DMA((n,)),
        ],
        2 * rows * width * (2 * dk + 3 * dv) + 2 * rows * rows * heads * 5 * VAL_HEAD,
        2 * width * (2 * dk + 3 * dv) + 12 * rows * dv + 7 * rows * width,
    )(
        *pieces, w1_own, w1_oth, w1_own, w1_oth, w0_own, w0_oth, w0_own, w0_oth, w0_own, w0_oth,
        gate, qkv, qkv, qkv, col_info, row_info, cos_table, sin_table, log_gamma,
    )


def weight_grad(side, lefts, rights, received=None):
    micro = len(lefts)
    groups = len(rights)
    width = lefts[0][0].shape[1]
    half = width // 2
    tile = 512
    tiles = half // tile
    sizes = [r[0].shape[1] for r in rights]
    cols = sum(sizes)
    flat = [r for group in rights for r in group]

    def body(*refs):
        left = refs[:micro]
        right = refs[micro : micro + len(flat)]
        o_ref = refs[-1]
        start = 0
        for g in range(groups):
            at = slice(start, start + sizes[g])
            acc = tn(left[0][...], right[g * micro][...])
            for b in range(1, micro):
                acc = acc + tn(left[b][...], right[g * micro + b][...])
            if received is not None:
                acc = acc + refs[-2][:, at].astype(F32)
            o_ref[:, at] = acc.astype(BF)
            start += sizes[g]

    rows = rights[0][0].shape[0]
    left_args = [array for array, _ in lefts]
    ins = [spec(rows, tile, lambda i, b=b: (b, side * tiles + i)) for _, b in lefts]
    ins = ins + [spec(r.shape[0], r.shape[1], lambda i: (0, 0)) for r in flat]
    args = left_args + flat
    if received is not None:
        ins.append(spec(tile, cols, lambda i: (i, 0)))
        args.append(received)
    return call(
        body,
        (tiles,),
        ins,
        spec(tile, cols, lambda i: (i, 0)),
        shape(half, cols),
        (),
        2 * micro * rows * half * cols,
        2 * (micro * rows * (half + cols) + half * cols),
    )(*args)


def layer_norm_parts(inputs, gain_row):
    center = inputs - jnp.mean(inputs, axis=-1, keepdims=True)
    inverse = lax.rsqrt(jnp.mean(center * center, axis=-1, keepdims=True) + eps_norm)
    scaled = center * inverse
    return (scaled * gain_row, scaled, inverse)


def layer_norm_back(incoming, scaled, inverse, gain_row):
    upstream = incoming * gain_row
    centered_grad = (
        upstream
        - jnp.mean(upstream, axis=-1, keepdims=True)
        - scaled * jnp.mean(upstream * scaled, axis=-1, keepdims=True)
    )
    return (centered_grad * inverse, jnp.sum(incoming * scaled, axis=0))


def make_on_device(grid):
    n_slots = grid.n_fsdp

    def on_device(
        tokens, norm_gains, w_query, w_key, w_value, w_gate, w_out, w_up, w_down, segments, d_output
    ):
        micro, _, piece, width = tokens.shape
        assert micro == 2
        own, length = micro * piece, 4 * piece
        col = width // n_slots
        dk, dv = w_query.shape[1], w_value.shape[1]
        heads = dk // KEY_HEAD
        hidden = w_up.shape[1]
        seq_id = lax.axis_index("seq")
        fsdp_id = lax.axis_index("fsdp")
        y, c = seq_id // 2, seq_id % 2
        x = fsdp_id % 2
        same = x == c
        both = range(micro)

        def to_local(value):
            v = value.reshape(-1, grid.nz, 2, col)
            a, b = v[:, :, 0].reshape(-1, width // 2), v[:, :, 1].reshape(-1, width // 2)
            return jnp.where(
                c == 0, jnp.concatenate([a, b], axis=1), jnp.concatenate([b, a], axis=1)
            )

        def to_natural(value):
            a, b = value[:, : width // 2], value[:, width // 2 :]
            a, b = a.reshape(-1, grid.nz, 1, col), b.reshape(-1, grid.nz, 1, col)
            v = jnp.where(
                c == 0, jnp.concatenate([a, b], axis=2), jnp.concatenate([b, a], axis=2)
            )
            return v.reshape(-1, width)

        w0 = grid.swap(jnp.concatenate([w_query, w_key, w_value], axis=1), same)
        toks = grid.swap(after(tokens.reshape(own, width), w0), same)
        segs = grid.swap(segments.reshape(micro, length).astype(F32), same)
        w0_own = grid.gather_line(w0)
        w1 = grid.swap(after(jnp.concatenate([w_gate, w_out.T], axis=1), toks), same)
        w1_own = grid.gather_line(w1)
        gains = to_local(norm_gains)
        gain_in, gain_mid = gains[0], gains[1]
        xin = to_local(toks).astype(F32)
        normed, scaled_in, inverse_in = layer_norm_parts(xin, gain_in)
        normed = normed.astype(BF)

        def rows(value, b):
            return value[b * piece : (b + 1) * piece]

        h1_pieces = [grid.gather_tokens(b, rows(normed, b)) for b in both]
        w0_oth = grid.flip_c(w0_own)
        w2 = grid.swap(after(jnp.concatenate([w_up, w_down.T], axis=1), w0_oth), same)
        w2_own = grid.gather_line(w2)

        ranks = [
            [2 * (y ^ i) + (x ^ j) for i, j in ((0, 0), (1, 0), (0, 1), (1, 1))],
            [2 * (y ^ i) + (x ^ j) for i, j in ((0, 0), (0, 1), (1, 0), (1, 1))],
        ]
        positions = jnp.stack(
            [jnp.concatenate([r * piece + jnp.arange(piece) for r in ranks[b]]) for b in both]
        ).astype(F32)
        seg_rows = jnp.stack(
            [
                jnp.concatenate(
                    [lax.dynamic_slice_in_dim(segs[b], r * piece, piece) for r in ranks[b]]
                )
                for b in both
            ]
        )
        frequency = jnp.exp(-jnp.log(10000.0) * 2.0 * jnp.arange(ROT, dtype=F32) / KEY_HEAD)
        angles = positions.reshape(-1, 1) * frequency[None, :]
        cos_table, sin_table = jnp.cos(angles), jnp.sin(angles)
        lanes = jnp.arange(128)[None, :]
        col_info = jnp.where(
            lanes == 0,
            positions.reshape(-1, 1),
            jnp.where(lanes == 1, seg_rows.reshape(-1, 1), 0.0),
        )
        row_info = jnp.stack([positions, seg_rows] + [jnp.zeros_like(positions)] * 6, axis=1)
        row_info = row_info.reshape(8 * micro, length)
        head_ids = (y * 2 + x) * heads + jnp.arange(heads, dtype=jnp.int32)
        log_gamma = jnp.log1p(-jnp.exp2(-5.0 - head_ids.astype(F32)))

        h1, qkv = project_qkv(
            [p for b in both for p in h1_pieces[b]], w0_own, w0_oth, cos_table, sin_table, 2 * dk
        )
        cots = grid.swap(after(d_output.reshape(own, width), qkv), same)
        cot_own = to_local(cots)
        cot_pieces = [grid.gather_tokens(b, rows(cot_own, b)) for b in both]
        cot = assemble([p for b in both for p in cot_pieces[b]])
        w1_oth = grid.flip_c(after(w1_own, cot))
        gate, gated, mixed = [], [], []
        for b in both:
            g, d, sent, kept = retain(
                b, h1, qkv, w1_own, w1_oth, col_info, row_info, log_gamma, heads
            )
            gate.append(g)
            gated.append(d)
            mixed.append(grid.scatter_tokens(b, sent, kept))
        x1, scaled_mid, inverse_mid, h2, act, slope = [], [], [], [], [], []
        w2_oth = grid.flip_c(w2_own)
        for b in both:
            x1.append(rows(xin, b) + mixed[b])
            out, scaled, inverse = layer_norm_parts(x1[b], gain_mid)
            scaled_mid.append(scaled)
            inverse_mid.append(inverse)
            h, a, s = feed_up(grid.gather_tokens(b, out.astype(BF)), w2_own, w2_oth, hidden)
            h2.append(h)
            act.append(a)
            slope.append(s)

        cot_rows = [(cot, b) for b in both]
        moved = grid.flip_c(weight_grad(1, cot_rows, [act]))
        d_up, d_h2 = [], []
        for b in both:
            d, sent, kept = feed_back(b, cot, slope[b], w2_own, w2_oth, hidden)
            d_up.append(d)
            d_h2.append(grid.scatter_tokens(b, sent, kept))
        h2_rows = [(h, 0) for h in h2]
        g_down = grid.scatter_line(weight_grad(0, cot_rows, [act], moved))
        moved = grid.flip_c(weight_grad(1, h2_rows, [d_up]))
        g_up = grid.scatter_line(weight_grad(0, h2_rows, [d_up], moved))

        d_x1, mix_pieces, gain_mid_grad = [], [], 0.0
        for b in both:
            d_ln, part = layer_norm_back(d_h2[b], scaled_mid[b], inverse_mid[b], gain_mid)
            gain_mid_grad = gain_mid_grad + part
            d_x1.append(rows(cot_own, b).astype(F32) + d_ln)
            mix_pieces.append(grid.gather_tokens(b, d_x1[b].astype(BF)))

        d_mix, d_gate, d_q, d_k, d_v, d_h1 = [], [], [], [], [], []
        for b in both:
            m, g, q, k, v, sent, kept = retain_back(
                b, mix_pieces[b], gate[b], qkv, (w0_own, w0_oth, w1_own, w1_oth), col_info,
                row_info, cos_table, sin_table, log_gamma, heads,
            )
            d_mix.append(m)
            d_gate.append(g)
            d_q.append(q)
            d_k.append(k)
            d_v.append(v)
            d_h1.append(grid.scatter_tokens(b, sent, kept))
        h1_rows = [(h1, b) for b in both]
        mix_rows = [(m, 0) for m in d_mix]
        moved = grid.flip_c(weight_grad(1, mix_rows, [gated]))
        g_out = grid.scatter_line(weight_grad(0, mix_rows, [gated], moved))
        moved = grid.flip_c(weight_grad(1, h1_rows, [d_gate, d_v]))
        g_gv = grid.scatter_line(weight_grad(0, h1_rows, [d_gate, d_v], moved))
        moved = grid.flip_c(weight_grad(1, h1_rows, [d_q, d_k]))
        g_qk = grid.scatter_line(weight_grad(0, h1_rows, [d_q, d_k], moved))

        outs = []
        for b in both:
            sent, kept = feed_down(act[b], w2_own, w2_oth, hidden)
            outs.append((x1[b] + grid.scatter_tokens(b, sent, kept)).astype(BF))

        d_inputs, gain_in_grad = [], 0.0
        for b in both:
            d_ln, part = layer_norm_back(
                d_h1[b], rows(scaled_in, b), rows(inverse_in, b), gain_in
            )
            gain_in_grad = gain_in_grad + part
            d_inputs.append(d_x1[b] + d_ln)
        grad_norms = grid.total(to_natural(jnp.stack([gain_in_grad, gain_mid_grad])))
        g_down, g_up, g_out, g_gv, g_qk = [
            grid.swap(g, same).astype(F32) for g in (g_down, g_up, g_out, g_gv, g_qk)
        ]
        output = grid.swap(to_natural(jnp.concatenate(outs)), same)
        d_input = grid.swap(to_natural(jnp.concatenate(d_inputs)), same)
        whole = (micro, 1, piece, width)
        return (
            output.reshape(whole),
            d_input.reshape(whole),
            grad_norms,
            g_qk[:, :dk],
            g_qk[:, dk:],
            g_gv[:, dv:],
            g_gv[:, :dv],
            g_out.T,
            g_up,
            g_down.T,
        )

    return on_device


def solution(mesh):
    grid = Grid(mesh.shape["seq"], mesh.shape["fsdp"])
    rows = P("fsdp", "seq")
    cols = P("seq", "fsdp")
    tok = P(None, "fsdp", "seq", None)
    return jax.shard_map(
        make_on_device(grid),
        mesh=mesh,
        in_specs=(tok, P(), rows, rows, rows, rows, cols, rows, cols, P(None, "fsdp", None), tok),
        out_specs=(tok, tok, P(), rows, rows, rows, rows, cols, rows, cols),
        check_vma=False,
    )
```

```python
import jax
import jax.numpy as jnp
from jax import lax
from jax.experimental import pallas as pl
from jax.experimental.pallas import tpu as pltpu
from jax.sharding import PartitionSpec as P

KEY_HEAD = 256
VAL_HEAD = 512
ROT = KEY_HEAD // 2
eps_norm = 1e-05
eps_group = 1.0
BF = jnp.bfloat16
F32 = jnp.float32
AXES = ("seq", "fsdp")
ANY = pl.BlockSpec(memory_space=pl.ANY)


def nn(left, right):
    return jnp.dot(left, right, preferred_element_type=F32)


def nt(left, right):
    return lax.dot_general(left, right, (((1,), (1,)), ((), ())), preferred_element_type=F32)


def tn(left, right):
    return lax.dot_general(left, right, (((0,), (0,)), ((), ())), preferred_element_type=F32)


def after(value, *first):
    return lax.optimization_barrier((value, *first))[0]


class Grid:
    def __init__(self, n_seq, n_fsdp):
        assert n_seq == 4 and n_fsdp % 2 == 0
        self.n_fsdp, self.nz = n_fsdp, n_fsdp // 2
        self.lines = [[z * 2 + x for z in range(self.nz)] for x in range(2)]
        self.groups = [
            [(y * 2 + c) * n_fsdp + z * 2 + x for z in range(self.nz) for c in range(2)]
            for y in range(2)
            for x in range(2)
        ]

    def send(self, value, move):
        found = []
        for y in range(2):
            for c in range(2):
                for z in range(self.nz):
                    for x in range(2):
                        y2, c2, z2, x2 = move(y, c, z, x)
                        src = (y * 2 + c) * self.n_fsdp + z * 2 + x
                        dst = (y2 * 2 + c2) * self.n_fsdp + z2 * 2 + x2
                        if src != dst:
                            found.append((src, dst))
        return lax.ppermute(value, AXES, found)

    def flip_z(self, value, bit):
        return self.send(value, lambda y, c, z, x: (y, c, z ^ bit, x))

    def flip_c(self, value):
        return self.send(value, lambda y, c, z, x: (y, 1 - c, z, x))

    def flip_y(self, value):
        return self.send(value, lambda y, c, z, x: (1 - y, c, z, x))

    def flip_x(self, value):
        return self.send(value, lambda y, c, z, x: (y, c, z, 1 - x))

    def first(self, b, value):
        return self.flip_y(value) if b == 0 else self.flip_x(value)

    def second(self, b, value):
        return self.flip_x(value) if b == 0 else self.flip_y(value)

    def swap(self, value):
        return self.send(value.astype(BF), lambda y, c, z, x: (y, x, z, c))

    def gather_weight(self, shard):
        return lax.all_gather(shard, AXES, axis=0, tiled=True, axis_index_groups=self.groups)

    def scatter_grad(self, value):
        return lax.psum_scatter(
            value, AXES, scatter_dimension=0, tiled=True, axis_index_groups=self.groups
        )

    def total(self, value):
        for flip in (self.flip_y, self.flip_x, self.flip_c):
            value = value + flip(value)
        if self.nz & (self.nz - 1):
            return lax.psum(value, "fsdp", axis_index_groups=self.lines)
        bit = 1
        while bit < self.nz:
            value = value + self.flip_z(value, bit)
            bit *= 2
        return value


def call(body, grid, ins, outs, shapes, scratch=(), flops=0, moved=0):
    return pl.pallas_call(
        body,
        out_shape=shapes,
        grid=grid,
        in_specs=ins,
        out_specs=outs,
        scratch_shapes=list(scratch),
        cost_estimate=pl.CostEstimate(
            flops=flops // 50, bytes_accessed=moved // 50, transcendentals=0
        ),
        compiler_params=pltpu.CompilerParams(vmem_limit_bytes=48 << 20),
    )


def shape(rows, cols, dtype=BF):
    return jax.ShapeDtypeStruct((rows, cols), dtype)


def spec(rows, cols, index):
    return pl.BlockSpec((rows, cols), index)


def fetch(pieces, target, sems):
    copies, row = [], 0
    for i, piece in enumerate(pieces):
        rows = piece.shape[0]
        copies.append(pltpu.make_async_copy(piece, target.at[pl.ds(row, rows)], sems.at[i]))
        row += rows
    for copy in copies:
        copy.start()
    for copy in copies:
        copy.wait()


def assemble(pieces):
    n = len(pieces)

    def body(*refs):
        fetch(refs[:n], refs[n], refs[n + 1])

    rows = sum(p.shape[0] for p in pieces)
    cols = pieces[0].shape[1]
    return pl.pallas_call(
        body,
        out_shape=shape(rows, cols),
        in_specs=[ANY] * n,
        scratch_shapes=[pltpu.SemaphoreType.DMA((n,))],
        cost_estimate=pl.CostEstimate(
            flops=0, bytes_accessed=4 * rows * cols, transcendentals=0
        ),
    )(*pieces)


def rotated(first, second, cos_part, sin_part):
    return (first * cos_part - second * sin_part, second * cos_part + first * sin_part)


def project(pieces, weight, cos_table, sin_table, rotate_cols, gate_cols):
    n = len(pieces)
    rows = sum(p.shape[0] for p in pieces)
    width = pieces[0].shape[1]
    cols = weight.shape[1]
    tile, chunk = 512, 512
    first = (cols - gate_cols) // tile

    def body(*refs):
        w_ref, cos_ref, sin_ref, h_ref, o_ref, gate_ref, sems = refs[n:]
        j = pl.program_id(0)

        @pl.when(j == 0)
        def _():
            fetch(refs[:n], h_ref, sems)

        turn = j * tile < rotate_cols

        def step(i, _):
            at = pl.ds(pl.multiple_of(i * chunk, chunk), chunk)
            acc = nn(h_ref[at, :], w_ref[...])

            @pl.when(j < first)
            def _():
                cos_part = jnp.where(turn, cos_ref[at, :], 1.0)
                sin_part = jnp.where(turn, sin_ref[at, :], 0.0)
                for s in range(0, tile, KEY_HEAD):
                    u, v = rotated(
                        acc[:, s : s + ROT], acc[:, s + ROT : s + KEY_HEAD], cos_part, sin_part
                    )
                    o_ref[at, s : s + ROT] = u.astype(BF)
                    o_ref[at, s + ROT : s + KEY_HEAD] = v.astype(BF)

            @pl.when(j >= first)
            def _():
                gate_ref[at, :] = acc

            return 0

        lax.fori_loop(0, rows // chunk, step, 0)

    return call(
        body,
        (cols // tile,),
        [ANY] * n
        + [spec(width, tile, lambda j: (0, j))]
        + [spec(rows, ROT, lambda j: (0, 0))] * 2,
        [
            spec(rows, width, lambda j: (0, 0)),
            spec(rows, tile, lambda j: (0, jnp.minimum(j, first - 1))),
            spec(rows, tile, lambda j: (0, jnp.maximum(j - first, 0))),
        ],
        [shape(rows, width), shape(rows, cols - gate_cols), shape(rows, gate_cols, F32)],
        [pltpu.SemaphoreType.DMA((n,))],
        2 * rows * width * cols,
        2 * (2 * rows * width + width * cols + rows * cols),
    )(*pieces, weight, cos_table, sin_table)


def decay_chunk(col_ref, row_ref, at, log_gamma):
    pos_n, seg_n = col_ref[at, 0:1], col_ref[at, 1:2]
    pos_m, seg_m = row_ref[0:1, :], row_ref[1:2, :]
    distance = pos_n - pos_m
    allowed = (distance >= 0.0) & (seg_n == seg_m)
    value = jnp.exp(jnp.maximum(distance, 0.0) * log_gamma) * (KEY_HEAD**-0.5)
    return jnp.where(allowed, value, 0.0)


def sigmoid(value):
    return 1.0 / (1.0 + jnp.exp(-value))


def retain(qkv, gate, col_info, row_info, log_gamma, heads, micro):
    rows = qkv.shape[0] // micro
    dv = heads * VAL_HEAD
    chunk = 256

    def body(q_ref, k_ref, v_ref, gate_ref, col_ref, row_ref, lg_ref, gated_ref):
        log_g = lg_ref[pl.program_id(1)]

        def step(i, _):
            at = pl.ds(pl.multiple_of(i * chunk, chunk), chunk)
            decay = decay_chunk(col_ref, row_ref, at, log_g)
            weights = (nt(q_ref[at, :], k_ref[...]) * decay).astype(BF)
            kept = nn(weights, v_ref[...])
            scale = lax.rsqrt(jnp.mean(kept * kept, axis=-1, keepdims=True) + eps_group)
            gate = gate_ref[at, :]
            gated_ref[at, :] = (gate * sigmoid(gate) * (kept * scale)).astype(BF)
            return 0

        lax.fori_loop(0, rows // chunk, step, 0)

    return call(
        body,
        (micro, heads),
        [
            spec(rows, KEY_HEAD, lambda b, h: (b, h)),
            spec(rows, KEY_HEAD, lambda b, h: (b, heads + h)),
            spec(rows, VAL_HEAD, lambda b, h: (b, heads + h)),
            spec(rows, VAL_HEAD, lambda b, h: (b, h)),
            spec(rows, 128, lambda b, h: (b, 0)),
            spec(8, rows, lambda b, h: (b, 0)),
            pl.BlockSpec(memory_space=pltpu.SMEM),
        ],
        spec(rows, VAL_HEAD, lambda b, h: (b, h)),
        shape(micro * rows, dv),
        (),
        2 * micro * rows * rows * heads * (KEY_HEAD + VAL_HEAD),
        10 * micro * rows * dv,
    )(qkv, qkv, qkv, gate, col_info, row_info, log_gamma)


ROOT_2_PI = 0.7978845608028654


def feed_up(pieces, weight, hidden):
    n = len(pieces)
    rows = sum(p.shape[0] for p in pieces)
    width = pieces[0].shape[1]
    tile, chunk = 512, 512

    def body(*refs):
        w_ref, h_ref, act_ref, slope_ref, sems = refs[n:]

        @pl.when(pl.program_id(0) == 0)
        def _():
            fetch(refs[:n], h_ref, sems)

        def step(i, _):
            at = pl.ds(pl.multiple_of(i * chunk, chunk), chunk)
            up = nn(h_ref[at, :], w_ref[...])
            square = up * up
            bent = jnp.tanh(ROOT_2_PI * (up + 0.044715 * square * up))
            act_ref[at, :] = (0.5 * up * (1.0 + bent)).astype(BF)
            inner = ROOT_2_PI * (1.0 + 3.0 * 0.044715 * square)
            slope = 0.5 * (1.0 + bent) + 0.5 * up * (1.0 - bent * bent) * inner
            slope_ref[at, :] = slope
            return 0

        lax.fori_loop(0, rows // chunk, step, 0)

    return call(
        body,
        (hidden // tile,),
        [ANY] * n + [spec(width, tile, lambda j: (0, j))],
        [spec(rows, width, lambda j: (0, 0))] + [spec(rows, tile, lambda j: (0, j))] * 2,
        [shape(rows, width), shape(rows, hidden), shape(rows, hidden, F32)],
        [pltpu.SemaphoreType.DMA((n,))],
        2 * rows * width * hidden,
        4 * rows * width + 2 * width * hidden + 6 * rows * hidden,
    )(*pieces, weight)


def project_back(b, value, rows, weight, first_col):
    hidden = value.shape[1]
    width = weight.shape[0]
    tile, chunk = 512, 512
    steps, first = hidden // tile, first_col // tile

    def body(in_ref, w_ref, sent_ref, kept_ref, acc_ref):
        j = pl.program_id(0)

        def step(i, _):
            at = pl.ds(pl.multiple_of(i * chunk, chunk), chunk)
            add_back(j, acc_ref, at, nt(in_ref[at, :], w_ref[...]))
            return 0

        lax.fori_loop(0, rows // chunk, step, 0)
        hand_out(j == steps - 1, acc_ref, sent_ref, kept_ref)

    return call(
        body,
        (steps,),
        [spec(rows, tile, lambda j: (b, j))]
        + [spec(width, tile, lambda j: (0, first + j))],
        [spec(rows // 2, width, lambda j: (0, 0))] * 2,
        [shape(rows // 2, width), shape(rows // 2, width, F32)],
        [pltpu.VMEM((rows, width), F32)],
        2 * rows * width * hidden,
        2 * rows * hidden + 2 * width * hidden + 3 * rows * width,
    )(value, weight)


def add_back(j, acc_ref, at, part):
    @pl.when(j == 0)
    def _():
        acc_ref[at, :] = part

    @pl.when(j != 0)
    def _():
        acc_ref[at, :] = acc_ref[at, :] + part


def hand_out(last, acc_ref, sent_ref, kept_ref):
    rows = acc_ref.shape[0]

    @pl.when(last)
    def _():
        kept_ref[...] = acc_ref[: rows // 2, :]
        sent_ref[...] = acc_ref[rows // 2 :, :].astype(BF)


def feed_back(b, cot, slope, weight, hidden):
    width = cot.shape[1]
    rows = slope.shape[0]
    tile, chunk = 512, 512
    steps = hidden // tile

    def body(cot_ref, slope_ref, down_ref, up_ref, dup_ref, sent_ref, kept_ref, acc_ref):
        j = pl.program_id(0)

        def step(i, _):
            at = pl.ds(pl.multiple_of(i * chunk, chunk), chunk)
            d_act = nn(cot_ref[at, :], down_ref[...])
            d_up = (d_act * slope_ref[at, :]).astype(BF)
            dup_ref[at, :] = d_up
            add_back(j, acc_ref, at, nt(d_up, up_ref[...]))
            return 0

        lax.fori_loop(0, rows // chunk, step, 0)
        hand_out(j == steps - 1, acc_ref, sent_ref, kept_ref)

    return call(
        body,
        (steps,),
        [spec(rows, width, lambda j: (b, 0)), spec(rows, tile, lambda j: (0, j))]
        + [spec(width, tile, lambda j: (0, steps + j)), spec(width, tile, lambda j: (0, j))],
        [spec(rows, tile, lambda j: (0, j))] + [spec(rows // 2, width, lambda j: (0, 0))] * 2,
        [shape(rows, hidden), shape(rows // 2, width), shape(rows // 2, width, F32)],
        [pltpu.VMEM((rows, width), F32)],
        4 * rows * width * hidden,
        5 * rows * width + 4 * width * hidden + 6 * rows * hidden,
    )(cot, slope, weight, weight)


def retain_back(b, d_mix, gate, qkv, weights, col_info, row_info, cos_table, sin_table,
                log_gamma, heads):
    w0, w1 = weights
    rows = d_mix.shape[0] // 2
    width = d_mix.shape[1]
    dk, dv = heads * KEY_HEAD, heads * VAL_HEAD
    chunk = 256

    def body(mix_ref, wo, wg, wv, wq, wk, gate_ref, q_ref, k_ref, v_ref, col_ref, row_ref,
             cos_ref, sin_ref, lg_ref, dgate_ref, dq_ref, dk_ref, dv_ref, sent_ref, kept_ref,
             acc_ref, dk_acc, dv_acc):
        h = pl.program_id(0)
        log_g = lg_ref[h]

        def step(i, _):
            at = pl.ds(pl.multiple_of(i * chunk, chunk), chunk)
            d_gated = nn(mix_ref[at, :], wo[...])
            decay = decay_chunk(col_ref, row_ref, at, log_g)
            weights = (nt(q_ref[at, :], k_ref[...]) * decay).astype(BF)
            kept = nn(weights, v_ref[...])
            scale = lax.rsqrt(jnp.mean(kept * kept, axis=-1, keepdims=True) + eps_group)
            y_norm = kept * scale
            gate = gate_ref[at, :]
            sig = sigmoid(gate)
            d_gate = d_gated * y_norm * sig * (1.0 + gate * (1.0 - sig))
            dgate_ref[at, :] = d_gate.astype(BF)
            d_y = d_gated * (gate * sig)
            d_ret = (
                scale * (d_y - y_norm * jnp.mean(d_y * y_norm, axis=-1, keepdims=True))
            ).astype(BF)
            d_weights = nt(d_ret, v_ref[...])
            d_scores = (d_weights * decay).astype(BF)
            d_v = tn(weights, d_ret)
            d_k = tn(d_scores, q_ref[at, :])
            d_q = nn(d_scores, k_ref[...])
            u, v = rotated(d_q[:, :ROT], d_q[:, ROT:], cos_ref[at, :], -sin_ref[at, :])
            dq_ref[at, :ROT] = u.astype(BF)
            dq_ref[at, ROT:] = v.astype(BF)

            @pl.when(i == 0)
            def _():
                dk_acc[...] = d_k
                dv_acc[...] = d_v

            @pl.when(i != 0)
            def _():
                dk_acc[...] = dk_acc[...] + d_k
                dv_acc[...] = dv_acc[...] + d_v

            return 0

        lax.fori_loop(0, rows // chunk, step, 0)
        dv_ref[...] = dv_acc[...].astype(BF)
        u, v = rotated(dk_acc[:, :ROT], dk_acc[:, ROT:], cos_ref[...], -sin_ref[...])
        dk_ref[:, :ROT] = u.astype(BF)
        dk_ref[:, ROT:] = v.astype(BF)

        def back(i, _):
            at = pl.ds(pl.multiple_of(i * chunk, chunk), chunk)
            part = (
                nt(dq_ref[at, :], wq[...])
                + nt(dk_ref[at, :], wk[...])
                + nt(dv_ref[at, :], wv[...])
                + nt(dgate_ref[at, :], wg[...])
            )
            add_back(h, acc_ref, at, part)
            return 0

        lax.fori_loop(0, rows // chunk, back, 0)
        hand_out(h == heads - 1, acc_ref, sent_ref, kept_ref)

    per_head = spec(rows, VAL_HEAD, lambda h: (0, h))
    per_key = spec(rows, KEY_HEAD, lambda h: (0, h))
    whole = spec(rows // 2, width, lambda h: (0, 0))
    return call(
        body,
        (heads,),
        [
            spec(rows, width, lambda h: (b, 0)),
            spec(width, VAL_HEAD, lambda h: (0, h)),
            spec(width, VAL_HEAD, lambda h: (0, 2 * heads + h)),
            spec(width, VAL_HEAD, lambda h: (0, heads + h)),
            spec(width, KEY_HEAD, lambda h: (0, h)),
            spec(width, KEY_HEAD, lambda h: (0, heads + h)),
            spec(rows, VAL_HEAD, lambda h: (b, h)),
            spec(rows, KEY_HEAD, lambda h: (b, h)),
            spec(rows, KEY_HEAD, lambda h: (b, heads + h)),
            spec(rows, VAL_HEAD, lambda h: (b, heads + h)),
            spec(rows, 128, lambda h: (b, 0)),
            spec(8, rows, lambda h: (b, 0)),
            spec(rows, ROT, lambda h: (b, 0)),
            spec(rows, ROT, lambda h: (b, 0)),
            pl.BlockSpec(memory_space=pltpu.SMEM),
        ],
        [
            per_head,
            per_key,
            per_key,
            per_head,
            whole,
            whole,
        ],
        [
            shape(rows, dv),
            shape(rows, dk),
            shape(rows, dk),
            shape(rows, dv),
            shape(rows // 2, width),
            shape(rows // 2, width, F32),
        ],
        [
            pltpu.VMEM((rows, width), F32),
            pltpu.VMEM((rows, KEY_HEAD), F32),
            pltpu.VMEM((rows, VAL_HEAD), F32),
        ],
        2 * rows * width * (2 * dk + 3 * dv) + 2 * rows * rows * heads * 5 * VAL_HEAD,
        2 * width * (2 * dk + 3 * dv) + 12 * rows * dv + 7 * rows * width,
    )(
        d_mix, w1, w0, w0, w0, w0,
        gate, qkv, qkv, qkv, col_info, row_info, cos_table, sin_table, log_gamma,
    )


def weight_grad(lefts, rights):
    micro = len(lefts)
    groups = len(rights)
    width = lefts[0][0].shape[1]
    tile = 512
    sizes = [r[0][0].shape[1] for r in rights]
    cols = sum(sizes)
    flat = [r for group in rights for r in group]

    def body(*refs):
        left = refs[:micro]
        right = refs[micro : micro + len(flat)]
        o_ref = refs[-1]
        start = 0
        for g in range(groups):
            at = slice(start, start + sizes[g])
            acc = tn(left[0][...], right[g * micro][...])
            for b in range(1, micro):
                acc = acc + tn(left[b][...], right[g * micro + b][...])
            o_ref[:, at] = acc.astype(BF)
            start += sizes[g]

    rows = lefts[0][2]
    args = [array for array, _, _ in lefts] + [array for array, _, _ in flat]
    ins = [spec(rows, tile, lambda i, b=b: (b, i)) for _, b, _ in lefts]
    ins = ins + [spec(rows, r.shape[1], lambda i, b=b: (b, 0)) for r, b, _ in flat]
    return call(
        body,
        (width // tile,),
        ins,
        spec(tile, cols, lambda i: (i, 0)),
        shape(width, cols),
        (),
        2 * micro * rows * width * cols,
        2 * (micro * rows * (width + cols) + width * cols),
    )(*args)


def layer_norm_parts(inputs, gain_row):
    center = inputs - jnp.mean(inputs, axis=-1, keepdims=True)
    inverse = lax.rsqrt(jnp.mean(center * center, axis=-1, keepdims=True) + eps_norm)
    scaled = center * inverse
    return (scaled * gain_row, scaled, inverse)


def layer_norm_back(incoming, scaled, inverse, gain_row):
    upstream = incoming * gain_row
    centered_grad = (
        upstream
        - jnp.mean(upstream, axis=-1, keepdims=True)
        - scaled * jnp.mean(upstream * scaled, axis=-1, keepdims=True)
    )
    return (centered_grad * inverse, jnp.sum(incoming * scaled, axis=0))


def make_on_device(grid):
    def on_device(
        tokens, norm_gains, w_query, w_key, w_value, w_gate, w_out, w_up, w_down, segments, d_output
    ):
        micro, _, piece, width = tokens.shape
        assert micro == 2
        own, length = micro * piece, 4 * piece
        dk, dv = w_query.shape[1], w_value.shape[1]
        heads = dk // KEY_HEAD
        hidden = w_up.shape[1]
        seq_id = lax.axis_index("seq")
        fsdp_id = lax.axis_index("fsdp")
        y, c = seq_id // 2, seq_id % 2
        x = fsdp_id % 2
        same = x == c
        both = range(micro)

        last = []

        def hold(value):
            return after(value, *last)

        def mark(value):
            last[:] = [value]
            return value

        def settle(value, moved):
            return mark(jnp.where(same, value, hold(moved).astype(value.dtype)))

        def rows(value, b):
            return value[b * piece : (b + 1) * piece]

        def pair(block, moved):
            return mark(jnp.concatenate([block, hold(moved)], axis=0))

        def reduce_second(b, kept, got):
            got = hold(got).astype(F32)
            kept = kept + got
            return kept[:piece], grid.first(b, mark(kept[piece:].astype(BF)))

        w0 = mark(jnp.concatenate([w_query, w_key, w_value, w_gate], axis=1))
        w0_moved = grid.swap(w0)
        toks = tokens.reshape(own, width)
        toks_moved = grid.swap(toks)
        segs = segments.reshape(micro, length).astype(F32)
        segs_moved = grid.swap(segs)
        w1 = mark(hold(w_out).T)
        w2 = mark(jnp.concatenate([w_up, hold(w_down).T], axis=1))

        ranks = [
            [2 * (y ^ i) + (x ^ j) for i, j in ((0, 0), (1, 0), (0, 1), (1, 1))],
            [2 * (y ^ i) + (x ^ j) for i, j in ((0, 0), (0, 1), (1, 0), (1, 1))],
        ]
        positions = jnp.stack(
            [jnp.concatenate([r * piece + jnp.arange(piece) for r in ranks[b]]) for b in both]
        ).astype(F32)
        frequency = jnp.exp(-jnp.log(10000.0) * 2.0 * jnp.arange(ROT, dtype=F32) / KEY_HEAD)
        angles = hold(positions).reshape(-1, 1) * frequency[None, :]
        cos_table, sin_table = jnp.cos(angles), jnp.sin(angles)
        mark(cos_table)
        head_ids = (y * 2 + x) * heads + jnp.arange(heads, dtype=jnp.int32)
        log_gamma = jnp.log1p(-jnp.exp2(-5.0 - head_ids.astype(F32)))
        gain_in, gain_mid = norm_gains[0], norm_gains[1]

        w0 = settle(w0, w0_moved)
        w0_full = grid.gather_weight(w0)
        toks = settle(toks, toks_moved)
        xin = toks.astype(F32)
        normed, scaled_in, inverse_in = layer_norm_parts(xin, gain_in)
        normed = mark(normed.astype(BF))
        h1_own = [rows(normed, b) for b in both]
        h1_first = [grid.first(b, h1_own[b]) for b in both]
        w1_moved = grid.swap(hold(w1))
        segs = settle(segs, segs_moved)
        seg_rows = jnp.stack(
            [
                jnp.concatenate(
                    [lax.dynamic_slice_in_dim(segs[b], r * piece, piece) for r in ranks[b]]
                )
                for b in both
            ]
        )
        lanes = jnp.arange(128)[None, :]
        col_info = jnp.where(
            lanes == 0,
            positions.reshape(-1, 1),
            jnp.where(lanes == 1, seg_rows.reshape(-1, 1), 0.0),
        )
        row_info = jnp.stack([positions, seg_rows] + [jnp.zeros_like(positions)] * 6, axis=1)
        row_info = mark(row_info.reshape(8 * micro, length))
        h1_second = [grid.second(b, pair(h1_own[b], h1_first[b])) for b in both]
        w1 = settle(w1, w1_moved)
        w1_full = grid.gather_weight(w1)
        cots = d_output.reshape(own, width)
        cots_moved = grid.swap(hold(cots))
        w2_moved = grid.swap(hold(w2))
        cots = settle(cots, cots_moved)
        cot_own = [rows(cots, b) for b in both]
        cot_first = [grid.first(b, cot_own[b]) for b in both]
        w2 = settle(w2, w2_moved)
        w2_full = grid.gather_weight(w2)
        cot_second = [grid.second(b, pair(cot_own[b], cot_first[b])) for b in both]

        h1, qkv, gate = project(
            [p for b in both for p in (h1_own[b], h1_first[b], h1_second[b])],
            hold(w0_full), cos_table, sin_table, 2 * dk, dv,
        )
        mark(qkv)
        cot = mark(
            assemble([p for b in both for p in (cot_own[b], cot_first[b], hold(cot_second[b]))])
        )
        gated = mark(retain(hold(qkv), gate, col_info, row_info, log_gamma, heads, micro))
        sums = []
        for b in both:
            sent, kept = project_back(b, hold(gated), length, w1_full, 0)
            mark(sent)
            sums.append((kept, grid.second(b, sent)))
        sums = [reduce_second(b, *sums[b]) for b in both]
        x1, mid, scaled_mid, inverse_mid, mid_first = [], [], [], [], []
        for b in both:
            x1.append(rows(xin, b) + (sums[b][0] + hold(sums[b][1]).astype(F32)))
            out, scaled, inverse = layer_norm_parts(x1[b], gain_mid)
            mid.append(mark(out.astype(BF)))
            scaled_mid.append(scaled)
            inverse_mid.append(inverse)
            mid_first.append(grid.first(b, mid[b]))
        mid_second = [grid.second(b, pair(mid[b], mid_first[b])) for b in both]
        h2, act, slope = [], [], []
        for b in both:
            h, a, s = feed_up(
                (mid[b], mid_first[b], hold(mid_second[b])), w2_full, hidden
            )
            mark(a)
            h2.append(h)
            act.append(a)
            slope.append(s)

        def blocks(value):
            if isinstance(value, list):
                return [(v, 0, length) for v in value]
            return [(value, b, length) for b in both]

        def grad(left, rights):
            left = hold(left) if not isinstance(left, list) else [hold(v) for v in left]
            sent = mark(weight_grad(blocks(left), [blocks(r) for r in rights]))
            return grid.scatter_grad(sent)

        d_up, sums = [], []
        g_down = grad(cot, [act])
        for b in both:
            d, sent, kept = feed_back(b, hold(cot), slope[b], w2_full, hidden)
            mark(sent)
            d_up.append(d)
            sums.append((kept, grid.second(b, sent)))
        g_up = grad(h2, [d_up])
        sums = [reduce_second(b, *sums[b]) for b in both]
        d_x1, mix_first, gain_mid_grad = [], [], 0.0
        for b in both:
            d_h2 = sums[b][0] + hold(sums[b][1]).astype(F32)
            d_ln, part = layer_norm_back(d_h2, scaled_mid[b], inverse_mid[b], gain_mid)
            gain_mid_grad = gain_mid_grad + part
            d_x1.append(cot_own[b].astype(F32) + d_ln)
            mix_first.append((mark(d_x1[b].astype(BF)),))
            mix_first[b] = mix_first[b] + (grid.first(b, mix_first[b][0]),)
        down = []
        sent, kept = project_back(0, hold(act[0]), length, w2_full, hidden)
        mark(sent)
        down.append((kept, sent))
        mix = [(v, f, grid.second(b, pair(v, f))) for b, (v, f) in enumerate(mix_first)]
        sent, kept = project_back(0, hold(act[1]), length, w2_full, hidden)
        mark(sent)
        down.append((kept, sent))
        d_mix = mark(assemble([p for b in both for p in mix[b][:2] + (hold(mix[b][2]),)]))
        g_out = grad(d_mix, [gated])
        g_down_moved = grid.swap(hold(g_down))
        d_gate, d_q, d_k, d_v, sums = [], [], [], [], []
        for b in both:
            g, q, k, v, sent, kept = retain_back(
                b, hold(d_mix), gate, qkv, (w0_full, w1_full), col_info, row_info, cos_table,
                sin_table, log_gamma, heads,
            )
            mark(sent)
            d_gate.append(g)
            d_q.append(q)
            d_k.append(k)
            d_v.append(v)
            sums.append((kept, grid.second(b, sent)))
            if b == 0:
                down = [(kept, grid.second(b, hold(sent))) for b, (kept, sent) in enumerate(down)]
                g_up_moved = grid.swap(hold(g_up))
        g_gv = grad(h1, [d_gate, d_v])
        g_qk = grad(h1, [d_q, d_k])
        down = [reduce_second(b, *down[b]) for b in both]
        sums = [reduce_second(b, *sums[b]) for b in both]
        outs = [
            (x1[b] + (down[b][0] + hold(down[b][1]).astype(F32))).astype(BF) for b in both
        ]
        output = mark(jnp.concatenate(outs))
        output_moved = grid.swap(output)
        d_inputs, gain_in_grad = [], 0.0
        for b in both:
            d_h1 = sums[b][0] + hold(sums[b][1]).astype(F32)
            d_ln, part = layer_norm_back(d_h1, rows(scaled_in, b), rows(inverse_in, b), gain_in)
            gain_in_grad = gain_in_grad + part
            d_inputs.append(mark(d_x1[b] + d_ln))
        d_input = mark(jnp.concatenate(d_inputs))
        d_input_moved = grid.swap(d_input)
        g_out_moved = grid.swap(hold(g_out))
        grad_norms = grid.total(jnp.stack([gain_in_grad, gain_mid_grad]))
        g_gv_moved = grid.swap(mark(hold(g_gv)))
        g_qk_moved = grid.swap(hold(g_qk))
        pairs = (
            (output, output_moved), (d_input, d_input_moved), (g_down, g_down_moved),
            (g_up, g_up_moved), (g_out, g_out_moved), (g_gv, g_gv_moved), (g_qk, g_qk_moved),
        )
        output, d_input, g_down, g_up, g_out, g_gv, g_qk = [
            jnp.where(same, value, moved.astype(value.dtype)) for value, moved in pairs
        ]
        g_down, g_up, g_out, g_gv, g_qk = [
            g.astype(F32) for g in (g_down, g_up, g_out, g_gv, g_qk)
        ]
        whole = (micro, 1, piece, width)
        return (
            output.reshape(whole),
            d_input.reshape(whole),
            grad_norms,
            g_qk[:, :dk],
            g_qk[:, dk:],
            g_gv[:, dv:],
            g_gv[:, :dv],
            g_out.T,
            g_up,
            g_down.T,
        )

    return on_device


def solution(mesh):
    grid = Grid(mesh.shape["seq"], mesh.shape["fsdp"])
    rows = P("fsdp", "seq")
    cols = P("seq", "fsdp")
    tok = P(None, "fsdp", "seq", None)
    return jax.shard_map(
        make_on_device(grid),
        mesh=mesh,
        in_specs=(tok, P(), rows, rows, rows, rows, cols, rows, cols, P(None, "fsdp", None), tok),
        out_specs=(tok, tok, P(), rows, rows, rows, rows, cols, rows, cols),
        check_vma=False,
    )
```

```python
import jax
import jax.numpy as jnp
from jax import lax
from jax.experimental import pallas as pl
from jax.experimental.pallas import tpu as pltpu
from jax.sharding import PartitionSpec as P

KEY_HEAD = 256
VAL_HEAD = 512
ROT = KEY_HEAD // 2
eps_norm = 1e-05
eps_group = 1.0
BF = jnp.bfloat16
F32 = jnp.float32
AXES = ("seq", "fsdp")
ANY = pl.BlockSpec(memory_space=pl.ANY)


def nn(left, right):
    return jnp.dot(left, right, preferred_element_type=F32)


def nt(left, right):
    return lax.dot_general(left, right, (((1,), (1,)), ((), ())), preferred_element_type=F32)


def tn(left, right):
    return lax.dot_general(left, right, (((0,), (0,)), ((), ())), preferred_element_type=F32)


def after(value, *first):
    return lax.optimization_barrier((value, *first))[0]


class Grid:
    def __init__(self, n_seq, n_fsdp):
        assert n_seq == 4 and n_fsdp % 2 == 0
        self.n_fsdp, self.nz = n_fsdp, n_fsdp // 2
        self.lines = [[z * 2 + x for z in range(self.nz)] for x in range(2)]
        self.groups = [
            [(y * 2 + c) * n_fsdp + z * 2 + x for z in range(self.nz) for c in range(2)]
            for y in range(2)
            for x in range(2)
        ]

    def send(self, value, move):
        found = []
        for y in range(2):
            for c in range(2):
                for z in range(self.nz):
                    for x in range(2):
                        y2, c2, z2, x2 = move(y, c, z, x)
                        src = (y * 2 + c) * self.n_fsdp + z * 2 + x
                        dst = (y2 * 2 + c2) * self.n_fsdp + z2 * 2 + x2
                        if src != dst:
                            found.append((src, dst))
        return lax.ppermute(value, AXES, found)

    def flip_z(self, value, bit):
        return self.send(value, lambda y, c, z, x: (y, c, z ^ bit, x))

    def flip_c(self, value):
        return self.send(value, lambda y, c, z, x: (y, 1 - c, z, x))

    def flip_y(self, value):
        return self.send(value, lambda y, c, z, x: (1 - y, c, z, x))

    def flip_x(self, value):
        return self.send(value, lambda y, c, z, x: (y, c, z, 1 - x))

    def first(self, b, value):
        return self.flip_y(value) if b == 0 else self.flip_x(value)

    def second(self, b, value):
        return self.flip_x(value) if b == 0 else self.flip_y(value)

    def swap(self, value):
        return self.send(value.astype(BF), lambda y, c, z, x: (y, x, z, c))

    def gather_weight(self, shard):
        return lax.all_gather(shard, AXES, axis=0, tiled=True, axis_index_groups=self.groups)

    def scatter_grad(self, value):
        return lax.psum_scatter(
            value, AXES, scatter_dimension=0, tiled=True, axis_index_groups=self.groups
        )

    def gather_line(self, shard):
        return lax.all_gather(shard, "fsdp", axis=0, tiled=True, axis_index_groups=self.lines)

    def scatter_line(self, value):
        return lax.psum_scatter(
            value, "fsdp", scatter_dimension=0, tiled=True, axis_index_groups=self.lines
        )

    def total(self, value):
        for flip in (self.flip_y, self.flip_x, self.flip_c):
            value = value + flip(value)
        if self.nz & (self.nz - 1):
            return lax.psum(value, "fsdp", axis_index_groups=self.lines)
        bit = 1
        while bit < self.nz:
            value = value + self.flip_z(value, bit)
            bit *= 2
        return value


def call(body, grid, ins, outs, shapes, scratch=(), flops=0, moved=0):
    return pl.pallas_call(
        body,
        out_shape=shapes,
        grid=grid,
        in_specs=ins,
        out_specs=outs,
        scratch_shapes=list(scratch),
        cost_estimate=pl.CostEstimate(
            flops=flops, bytes_accessed=moved, transcendentals=0
        ),
        compiler_params=pltpu.CompilerParams(vmem_limit_bytes=60 << 20),
    )


def shape(rows, cols, dtype=BF):
    return jax.ShapeDtypeStruct((rows, cols), dtype)


def spec(rows, cols, index):
    return pl.BlockSpec((rows, cols), index)


def copies_into(pieces, target, sems):
    copies, row = [], 0
    for i, piece in enumerate(pieces):
        rows = piece.shape[0]
        copies.append(pltpu.make_async_copy(piece, target.at[pl.ds(row, rows)], sems.at[i]))
        row += rows
    return copies


def fetch(pieces, target, sems):
    copies = copies_into(pieces, target, sems)
    for copy in copies:
        copy.start()
    for copy in copies:
        copy.wait()


def fetch_and_keep(j, steps, pieces, target, out, sems):
    keep = pltpu.make_async_copy(target, out, sems.at[len(pieces)])

    @pl.when(j == 0)
    def _():
        fetch(pieces, target, sems)
        keep.start()

    return keep


def assemble(pieces):
    n = len(pieces)

    def body(*refs):
        fetch(refs[:n], refs[n], refs[n + 1])

    rows = sum(p.shape[0] for p in pieces)
    cols = pieces[0].shape[1]
    return pl.pallas_call(
        body,
        out_shape=shape(rows, cols),
        in_specs=[ANY] * n,
        scratch_shapes=[pltpu.SemaphoreType.DMA((n,))],
        cost_estimate=pl.CostEstimate(
            flops=0, bytes_accessed=4 * rows * cols, transcendentals=0
        ),
    )(*pieces)


def rotated(first, second, cos_part, sin_part):
    return (first * cos_part - second * sin_part, second * cos_part + first * sin_part)


def project_turned(pieces, weight, cos_table, sin_table):
    n = len(pieces)
    rows = sum(p.shape[0] for p in pieces)
    width = pieces[0].shape[1]
    cols = weight.shape[1]
    tile, chunk = 512, 512
    steps = cols // tile

    def body(*refs):
        w_ref, cos_ref, sin_ref, out_ref, o_ref, h_ref, sems = refs[n:]
        j = pl.program_id(0)
        keep = fetch_and_keep(j, steps, refs[:n], h_ref, out_ref, sems)

        def step(i, _):
            at = pl.ds(pl.multiple_of(i * chunk, chunk), chunk)
            acc = nn(h_ref[at, :], w_ref[...])
            for s in range(0, tile, KEY_HEAD):
                u, v = rotated(
                    acc[:, s : s + ROT],
                    acc[:, s + ROT : s + KEY_HEAD],
                    cos_ref[at, :],
                    sin_ref[at, :],
                )
                o_ref[at, s : s + ROT] = u.astype(BF)
                o_ref[at, s + ROT : s + KEY_HEAD] = v.astype(BF)
            return 0

        lax.fori_loop(0, rows // chunk, step, 0, unroll=True)

        @pl.when(j == steps - 1)
        def _():
            keep.wait()

    return call(
        body,
        (steps,),
        [ANY] * n
        + [spec(width, tile, lambda j: (0, j))]
        + [spec(rows, ROT, lambda j: (0, 0))] * 2,
        [ANY, spec(rows, tile, lambda j: (0, j))],
        [shape(rows, width), shape(rows, cols)],
        [pltpu.VMEM((rows, width), BF), pltpu.SemaphoreType.DMA((n + 1,))],
        2 * rows * width * cols,
        2 * (2 * rows * width + width * cols + rows * cols),
    )(*pieces, weight, cos_table, sin_table)


def project_plain(h1, weight, gate_cols):
    rows, width = h1.shape
    cols = weight.shape[1]
    tile, chunk = 512, 512
    first = (cols - gate_cols) // tile

    def body(h_ref, w_ref, v_ref, gate_ref):
        j = pl.program_id(0)

        def step(i, _):
            at = pl.ds(pl.multiple_of(i * chunk, chunk), chunk)
            acc = nn(h_ref[at, :], w_ref[...])

            @pl.when(j < first)
            def _():
                v_ref[at, :] = acc.astype(BF)

            @pl.when(j >= first)
            def _():
                gate_ref[at, :] = acc

            return 0

        lax.fori_loop(0, rows // chunk, step, 0, unroll=True)

    return call(
        body,
        (cols // tile,),
        [spec(rows, width, lambda j: (0, 0)), spec(width, tile, lambda j: (0, j))],
        [
            spec(rows, tile, lambda j: (0, jnp.minimum(j, first - 1))),
            spec(rows, tile, lambda j: (0, jnp.maximum(j - first, 0))),
        ],
        [shape(rows, cols - gate_cols), shape(rows, gate_cols, F32)],
        (),
        2 * rows * width * cols,
        2 * (rows * width + width * cols + 2 * rows * cols),
    )(h1, weight)


def decay_chunk(col_ref, row_ref, at, log_gamma):
    pos_n, seg_n = col_ref[at, 0:1], col_ref[at, 1:2]
    pos_m, seg_m = row_ref[0:1, :], row_ref[1:2, :]
    distance = pos_n - pos_m
    allowed = (distance >= 0.0) & (seg_n == seg_m)
    value = jnp.exp(jnp.maximum(distance, 0.0) * log_gamma) * (KEY_HEAD**-0.5)
    return jnp.where(allowed, value, 0.0)


def sigmoid(value):
    return 1.0 / (1.0 + jnp.exp(-value))


def retain(qk, values, gate, col_info, row_info, log_gamma, heads, micro):
    rows = qk.shape[0] // micro
    dv = heads * VAL_HEAD
    chunk = 512

    def body(q_ref, k_ref, v_ref, gate_ref, col_ref, row_ref, lg_ref, gated_ref):
        log_g = lg_ref[pl.program_id(1)]

        def step(i, _):
            at = pl.ds(pl.multiple_of(i * chunk, chunk), chunk)
            decay = decay_chunk(col_ref, row_ref, at, log_g)
            weights = (nt(q_ref[at, :], k_ref[...]) * decay).astype(BF)
            kept = nn(weights, v_ref[...])
            scale = lax.rsqrt(jnp.mean(kept * kept, axis=-1, keepdims=True) + eps_group)
            gate = gate_ref[at, :]
            gated_ref[at, :] = (gate * sigmoid(gate) * (kept * scale)).astype(BF)
            return 0

        lax.fori_loop(0, rows // chunk, step, 0, unroll=True)

    return call(
        body,
        (micro, heads),
        [
            spec(rows, KEY_HEAD, lambda b, h: (b, h)),
            spec(rows, KEY_HEAD, lambda b, h: (b, heads + h)),
            spec(rows, VAL_HEAD, lambda b, h: (b, h)),
            spec(rows, VAL_HEAD, lambda b, h: (b, h)),
            spec(rows, 128, lambda b, h: (b, 0)),
            spec(8, rows, lambda b, h: (b, 0)),
            pl.BlockSpec(memory_space=pltpu.SMEM),
        ],
        spec(rows, VAL_HEAD, lambda b, h: (b, h)),
        shape(micro * rows, dv),
        (),
        2 * micro * rows * rows * heads * (KEY_HEAD + VAL_HEAD),
        10 * micro * rows * dv,
    )(qk, qk, values, gate, col_info, row_info, log_gamma)


ROOT_2_PI = 0.7978845608028654


def feed_up(pieces, weight, hidden):
    n = len(pieces)
    rows = sum(p.shape[0] for p in pieces)
    width = pieces[0].shape[1]
    tile, chunk = 512, 512
    steps = hidden // tile

    def body(*refs):
        w_ref, out_ref, act_ref, slope_ref, h_ref, sems = refs[n:]
        j = pl.program_id(0)
        keep = fetch_and_keep(j, steps, refs[:n], h_ref, out_ref, sems)

        def step(i, _):
            at = pl.ds(pl.multiple_of(i * chunk, chunk), chunk)
            up = nn(h_ref[at, :], w_ref[...])
            square = up * up
            bent = jnp.tanh(ROOT_2_PI * (up + 0.044715 * square * up))
            act_ref[at, :] = (0.5 * up * (1.0 + bent)).astype(BF)
            inner = ROOT_2_PI * (1.0 + 3.0 * 0.044715 * square)
            slope = 0.5 * (1.0 + bent) + 0.5 * up * (1.0 - bent * bent) * inner
            slope_ref[at, :] = slope
            return 0

        lax.fori_loop(0, rows // chunk, step, 0, unroll=True)

        @pl.when(j == steps - 1)
        def _():
            keep.wait()

    return call(
        body,
        (steps,),
        [ANY] * n + [spec(width, tile, lambda j: (0, j))],
        [ANY] + [spec(rows, tile, lambda j: (0, j))] * 2,
        [shape(rows, width), shape(rows, hidden), shape(rows, hidden, F32)],
        [pltpu.VMEM((rows, width), BF), pltpu.SemaphoreType.DMA((n + 1,))],
        2 * rows * width * hidden,
        4 * rows * width + 2 * width * hidden + 6 * rows * hidden,
    )(*pieces, weight)


def in_pairs(flat):
    return [tuple(flat[i : i + 2]) for i in range(0, len(flat), 2)]


def hand_out_specs(micro, rows, width, tile, index):
    shapes = [shape(rows // 2, width), shape(rows // 2, width, F32)] * micro
    return [spec(rows // 2, tile, index)] * len(shapes), shapes


def hand_out(acc, b, outs):
    half = acc.shape[0] // 2
    outs[2 * b][...] = acc[half:].astype(BF)
    outs[2 * b + 1][...] = acc[:half]


def project_back(values, weights):
    n = len(values)
    rows = values[0].shape[0]
    width = weights[0][0].shape[0]
    tile = 512
    each = rows // 2
    sizes = [v.shape[1] for v in values]

    def body(*refs):
        outs = refs[2 * n :]
        for b in range(2):
            at = slice(b * each, (b + 1) * each)
            acc = nt(refs[0][at, :], refs[n][...])
            for i in range(1, n):
                acc = acc + nt(refs[i][at, :], refs[n + i][...])
            hand_out(acc, b, outs)

    out_specs, shapes = hand_out_specs(2, each, width, tile, lambda j: (0, j))
    flat = call(
        body,
        (width // tile,),
        [spec(rows, k, lambda j: (0, 0)) for k in sizes]
        + [spec(tile, k, lambda j, i=i: (j, i)) for k, (_, i) in zip(sizes, weights)],
        out_specs,
        shapes,
        (),
        2 * rows * width * sum(sizes),
        2 * (rows + width) * sum(sizes) + 3 * rows * width,
    )(*values, *[w for w, _ in weights])
    return in_pairs(flat)


def feed_back(cot, slope, weight, hidden):
    rows, width = cot.shape
    tile = 512
    micro, each = 2, rows // 2
    first, second = hidden // tile, width // tile

    def body(cot_ref, down_ref, up_ref, slope_ref, dup_ref, *rest):
        *outs, keep_ref = rest
        j = pl.program_id(0)

        for i in range(first):

            @pl.when(j == i)
            def _(i=i):
                for b in range(micro):
                    at = slice(b * each, (b + 1) * each)
                    d_act = nn(cot_ref[at, :], down_ref[...])
                    d_up = (d_act * slope_ref[at, :]).astype(BF)
                    dup_ref[at, :] = d_up
                    keep_ref[at, i * tile : (i + 1) * tile] = d_up

        @pl.when(j >= first)
        def _():
            acc = nt(keep_ref[...], up_ref[...])
            for b in range(micro):
                hand_out(acc[b * each : (b + 1) * each], b, outs)

    def early(j):
        return jnp.minimum(j, first - 1)

    def late(j):
        return jnp.maximum(j - first, 0)

    out_specs, shapes = hand_out_specs(micro, each, width, tile, lambda j: (0, late(j)))
    d_up, *flat = call(
        body,
        (first + second,),
        [
            spec(rows, width, lambda j: (0, 0)),
            spec(width, tile, lambda j: (0, first + early(j))),
            spec(tile, hidden, lambda j: (late(j), 0)),
            spec(rows, tile, lambda j: (0, early(j))),
        ],
        [spec(rows, tile, lambda j: (0, early(j)))] + out_specs,
        [shape(rows, hidden)] + shapes,
        [pltpu.VMEM((rows, hidden), BF)],
        4 * rows * width * hidden,
        5 * rows * width + 4 * width * hidden + 6 * rows * hidden,
    )(cot, weight, weight, slope)
    return d_up, in_pairs(flat)


def retain_back(d_mix, gate, qk, values, w_out, col_info, row_info, cos_table, sin_table,
                log_gamma, heads, micro):
    rows = d_mix.shape[0] // micro
    width = d_mix.shape[1]
    dk, dv = heads * KEY_HEAD, heads * VAL_HEAD

    def body(mix_ref, wo, gate_ref, q_ref, k_ref, v_ref, col_ref, row_ref, cos_ref,
             sin_ref, lg_ref, dv_ref, dg_ref, dq_ref, dk_ref):
        log_g = lg_ref[pl.program_id(0)]
        d_gated = nn(mix_ref[...], wo[...])
        decay = decay_chunk(col_ref, row_ref, slice(None), log_g)
        weights = (nt(q_ref[...], k_ref[...]) * decay).astype(BF)
        kept = nn(weights, v_ref[...])
        scale = lax.rsqrt(jnp.mean(kept * kept, axis=-1, keepdims=True) + eps_group)
        y_norm = kept * scale
        gate = gate_ref[...]
        sig = sigmoid(gate)
        dg_ref[...] = (d_gated * y_norm * sig * (1.0 + gate * (1.0 - sig))).astype(BF)
        d_y = d_gated * (gate * sig)
        d_ret = (
            scale * (d_y - y_norm * jnp.mean(d_y * y_norm, axis=-1, keepdims=True))
        ).astype(BF)
        d_scores = (nt(d_ret, v_ref[...]) * decay).astype(BF)
        dv_ref[...] = tn(weights, d_ret).astype(BF)
        d_k = tn(d_scores, q_ref[...])
        d_q = nn(d_scores, k_ref[...])
        cos_part, sin_part = cos_ref[...], -sin_ref[...]
        for out, part in ((dq_ref, d_q), (dk_ref, d_k)):
            u, v = rotated(part[:, :ROT], part[:, ROT:], cos_part, sin_part)
            out[:, :ROT] = u.astype(BF)
            out[:, ROT:] = v.astype(BF)

    def per_head(cols, start=0):
        return spec(rows, cols, lambda h, b: (b, start + h))

    def per_row(height, cols):
        return spec(height, cols, lambda h, b: (b, 0))

    total = micro * rows
    return call(
        body,
        (heads, micro),
        [
            per_row(rows, width),
            spec(width, VAL_HEAD, lambda h, b: (0, h)),
            per_head(VAL_HEAD),
            per_head(KEY_HEAD),
            per_head(KEY_HEAD, heads),
            per_head(VAL_HEAD),
            per_row(rows, 128),
            per_row(8, rows),
            per_row(rows, ROT),
            per_row(rows, ROT),
            pl.BlockSpec(memory_space=pltpu.SMEM),
        ],
        [per_head(VAL_HEAD), per_head(VAL_HEAD), per_head(KEY_HEAD), per_head(KEY_HEAD)],
        [shape(total, dv), shape(total, dv), shape(total, dk), shape(total, dk)],
        (),
        2 * total * width * dv + 2 * total * rows * heads * 5 * VAL_HEAD,
        2 * width * dv + 20 * total * dv + 2 * total * width,
    )(
        d_mix, w_out, gate, qk, qk, values, col_info, row_info, cos_table, sin_table, log_gamma
    )


def weight_grad(left, rights):
    rows, width = left.shape
    sizes = [v.shape[1] for v in rights]
    cols = sum(sizes)
    tile = 512

    def body(left_ref, *refs):
        start = 0
        for right, size in zip(refs, sizes):
            refs[-1][:, start : start + size] = tn(left_ref[...], right[...]).astype(BF)
            start += size

    return call(
        body,
        (width // tile,),
        [spec(rows, tile, lambda i: (0, i))] + [spec(rows, k, lambda i: (0, 0)) for k in sizes],
        spec(tile, cols, lambda i: (i, 0)),
        shape(width, cols),
        (),
        2 * rows * width * cols,
        2 * (rows * (width + cols) + width * cols),
    )(left, *rights)


def weight_grad_pieces(pieces, right):
    n = len(pieces)
    rows, cols = right.shape
    width = pieces[0].shape[1]
    tile = 512
    steps = width // tile

    def body(*refs):
        right_ref, out_ref, o_ref, left_ref, sems = refs[n:]
        j = pl.program_id(0)
        keep = fetch_and_keep(j, steps, refs[:n], left_ref, out_ref, sems)
        at = pl.ds(pl.multiple_of(j * tile, tile), tile)
        o_ref[...] = tn(left_ref[:, at], right_ref[...]).astype(BF)

        @pl.when(j == steps - 1)
        def _():
            keep.wait()

    return call(
        body,
        (steps,),
        [ANY] * n + [spec(rows, cols, lambda i: (0, 0))],
        [ANY, spec(tile, cols, lambda i: (i, 0))],
        [shape(rows, width), shape(width, cols)],
        [pltpu.VMEM((rows, width), BF), pltpu.SemaphoreType.DMA((n + 1,))],
        2 * rows * width * cols,
        2 * (rows * (width + cols) + width * cols),
    )(*pieces, right)


def layer_norm_parts(inputs, gain_row):
    center = inputs - jnp.mean(inputs, axis=-1, keepdims=True)
    inverse = lax.rsqrt(jnp.mean(center * center, axis=-1, keepdims=True) + eps_norm)
    scaled = center * inverse
    return (scaled * gain_row, scaled, inverse)


def layer_norm_back(incoming, scaled, inverse, gain_row):
    upstream = incoming * gain_row
    centered_grad = (
        upstream
        - jnp.mean(upstream, axis=-1, keepdims=True)
        - scaled * jnp.mean(upstream * scaled, axis=-1, keepdims=True)
    )
    return (centered_grad * inverse, jnp.sum(incoming * scaled, axis=0))


def make_on_device(grid):
    def on_device(
        tokens, norm_gains, w_query, w_key, w_value, w_gate, w_out, w_up, w_down, segments, d_output
    ):
        micro, _, piece, width = tokens.shape
        assert micro == 2
        own, length = micro * piece, 4 * piece
        dk, dv = w_query.shape[1], w_value.shape[1]
        heads = dk // KEY_HEAD
        hidden = w_up.shape[1]
        seq_id = lax.axis_index("seq")
        fsdp_id = lax.axis_index("fsdp")
        y, c = seq_id // 2, seq_id % 2
        x = fsdp_id % 2
        same = x == c
        both = range(micro)

        last = []

        def hold(value):
            return after(value, *last)

        def mark(value):
            last[:] = [value]
            return value

        def settle(value, moved):
            return mark(jnp.where(same, value, hold(moved).astype(value.dtype)))

        def rows(value, b):
            return value[b * piece : (b + 1) * piece]

        def await_(*values):
            waited = lax.optimization_barrier((*values, *last))[: len(values)]
            last[:] = [waited[0]]
            return list(waited)

        def pair(block, moved):
            return mark(jnp.concatenate([block, hold(moved)], axis=0))

        def reduce_second(b, kept, got):
            got = hold(got).astype(F32)
            kept = kept + got
            return kept[:piece], grid.first(b, mark(kept[piece:].astype(BF)))

        line_qk = grid.gather_line(mark(jnp.concatenate([w_query, w_key], axis=1)))
        w_vgo = mark(jnp.concatenate([hold(w_value), w_gate, w_out.T], axis=1))
        vgo_moved = grid.swap(w_vgo)
        toks = tokens.reshape(own, width)
        toks_moved = grid.swap(toks)
        segs = segments.reshape(micro, length).astype(F32)
        segs_moved = grid.swap(segs)
        ud_cot = mark(
            jnp.concatenate(
                [jnp.concatenate([w_up, hold(w_down).T], axis=1), d_output.reshape(own, width)],
                axis=0,
            )
        )

        ranks = [
            [2 * (y ^ i) + (x ^ j) for i, j in ((0, 0), (1, 0), (0, 1), (1, 1))],
            [2 * (y ^ i) + (x ^ j) for i, j in ((0, 0), (0, 1), (1, 0), (1, 1))],
        ]
        positions = jnp.stack(
            [jnp.concatenate([r * piece + jnp.arange(piece) for r in ranks[b]]) for b in both]
        ).astype(F32)
        frequency = jnp.exp(-jnp.log(10000.0) * 2.0 * jnp.arange(ROT, dtype=F32) / KEY_HEAD)
        angles = hold(positions).reshape(-1, 1) * frequency[None, :]
        cos_table, sin_table = jnp.cos(angles), jnp.sin(angles)
        mark(cos_table)
        head_ids = (y * 2 + x) * heads + jnp.arange(heads, dtype=jnp.int32)
        log_gamma = jnp.log1p(-jnp.exp2(-5.0 - head_ids.astype(F32)))
        gain_in, gain_mid = norm_gains[0], norm_gains[1]

        w_vgo = settle(w_vgo, vgo_moved)
        full_vg = grid.gather_weight(w_vgo[:, : 2 * dv])
        full_o = grid.gather_weight(w_vgo[:, 2 * dv :])
        toks = settle(toks, toks_moved)
        xin = toks.astype(F32)
        normed, scaled_in, inverse_in = layer_norm_parts(xin, gain_in)
        normed = mark(normed.astype(BF))
        h1_own = [rows(normed, b) for b in both]
        h1_first = [grid.first(b, h1_own[b]) for b in both]
        segs = settle(segs, segs_moved)
        h1_second = [grid.second(b, pair(h1_own[b], h1_first[b])) for b in both]
        line_qk = await_(line_qk)[0]
        qk_moved = grid.swap(line_qk)
        ud_cot_moved = grid.swap(after(ud_cot, line_qk))
        h1_second = await_(*h1_second)
        line_qk = settle(line_qk, qk_moved)
        line_other = grid.flip_c(line_qk)
        even, odd = [v.reshape(grid.nz, 1, -1, 2 * dk) for v in (line_qk, hold(line_other))]
        full_qk = jnp.where(
            c == 0,
            jnp.concatenate([even, odd], axis=1),
            jnp.concatenate([odd, even], axis=1),
        ).reshape(width, 2 * dk)
        mark(full_qk)
        h1, qk = project_turned(
            [p for b in both for p in (h1_own[b], h1_first[b], h1_second[b])],
            full_qk, cos_table, sin_table,
        )
        mark(qk)
        ud_cot = settle(ud_cot, ud_cot_moved)
        full_ud = grid.gather_weight(ud_cot[:-own])
        cots = ud_cot[-own:]
        cot_own = [rows(cots, b) for b in both]
        cot_first = [grid.first(b, cot_own[b]) for b in both]
        seg_rows = jnp.stack(
            [
                jnp.concatenate(
                    [lax.dynamic_slice_in_dim(hold(segs)[b], r * piece, piece) for r in ranks[b]]
                )
                for b in both
            ]
        )
        lanes = jnp.arange(128)[None, :]
        col_info = jnp.where(
            lanes == 0,
            positions.reshape(-1, 1),
            jnp.where(lanes == 1, seg_rows.reshape(-1, 1), 0.0),
        )
        row_info = jnp.stack([positions, seg_rows] + [jnp.zeros_like(positions)] * 6, axis=1)
        row_info = mark(row_info.reshape(8 * micro, length))

        values, gate = project_plain(hold(h1), hold(full_vg), dv)
        mark(values)
        cot_second = [grid.second(b, pair(cot_own[b], cot_first[b])) for b in both]
        gated = mark(
            retain(qk, hold(values), gate, col_info, row_info, log_gamma, heads, micro)
        )
        outs = project_back([hold(gated)], [(full_o, 0)])
        mark(outs[0][0])
        moved = [grid.second(b, outs[b][0]) for b in both]
        cot = mark(
            assemble([p for b in both for p in (cot_own[b], cot_first[b], hold(cot_second[b]))])
        )
        sums = [reduce_second(b, outs[b][1], moved[b]) for b in both]
        x1, mid, scaled_mid, inverse_mid, mid_first = [], [], [], [], []
        for b in both:
            x1.append(rows(xin, b) + (sums[b][0] + hold(sums[b][1]).astype(F32)))
            out, scaled, inverse = layer_norm_parts(x1[b], gain_mid)
            mid.append(mark(out.astype(BF)))
            scaled_mid.append(scaled)
            inverse_mid.append(inverse)
            mid_first.append(grid.first(b, mid[b]))
        mid_second = [grid.second(b, pair(mid[b], mid_first[b])) for b in both]
        h2, act, slope = feed_up(
            [p for b in both for p in (mid[b], mid_first[b], hold(mid_second[b]))], full_ud, hidden
        )
        mark(act)

        def grad(left, rights):
            return mark(weight_grad(hold(left), rights))

        g_down = grid.scatter_grad(grad(cot, [act]))
        d_up, outs = feed_back(hold(cot), slope, full_ud, hidden)
        mark(d_up)
        moved = [grid.second(b, outs[b][0]) for b in both]
        g_up = grad(h2, [d_up])
        sums = [reduce_second(b, outs[b][1], moved[b]) for b in both]
        g_up = grid.scatter_grad(hold(g_up))
        d_x1, mix_first, gain_mid_grad = [], [], 0.0
        for b in both:
            d_h2 = sums[b][0] + hold(sums[b][1]).astype(F32)
            d_ln, part = layer_norm_back(d_h2, scaled_mid[b], inverse_mid[b], gain_mid)
            gain_mid_grad = gain_mid_grad + part
            d_x1.append(cot_own[b].astype(F32) + d_ln)
            mix_first.append((mark(d_x1[b].astype(BF)),))
            mix_first[b] = mix_first[b] + (grid.first(b, mix_first[b][0]),)
        g_down = await_(g_down)[0]
        g_down_moved = grid.swap(g_down)
        down = project_back([hold(act)], [(full_ud, 1)])
        mark(down[0][0])
        mix = [(v, f, grid.second(b, pair(v, f))) for b, (v, f) in enumerate(mix_first)]
        g_down = settle(g_down, g_down_moved)
        d_mix, g_out = weight_grad_pieces(
            [p for b in both for p in mix[b][:2] + (hold(mix[b][2]),)], gated
        )
        g_out = grid.scatter_grad(mark(g_out))
        g_up = await_(g_up)[0]
        g_up_moved = grid.swap(g_up)
        down_moved = [grid.second(b, hold(down[b][0])) for b in both]
        d_v, d_gate, d_q, d_k = retain_back(
            hold(d_mix), gate, qk, values, full_o, col_info, row_info, cos_table, sin_table,
            log_gamma, heads, micro,
        )
        mark(d_v)
        g_vg = grid.scatter_grad(grad(h1, [d_v, d_gate]))
        down = [reduce_second(b, down[b][1], down_moved[b]) for b in both]
        outs = project_back(
            [d_q, d_k, d_v, hold(d_gate)],
            [(full_qk, 0), (full_qk, 1), (full_vg, 0), (full_vg, 1)],
        )
        mark(outs[0][0])
        moved = [grid.second(b, outs[b][0]) for b in both]
        g_qk = grid.scatter_grad(grad(h1, [d_q, d_k]))
        output = mark(
            jnp.concatenate(
                [x1[b] + (down[b][0] + hold(down[b][1]).astype(F32)) for b in both]
            ).astype(BF)
        )
        output_moved = grid.swap(output)
        g_up = settle(g_up, g_up_moved)
        sums = [reduce_second(b, outs[b][1], moved[b]) for b in both]
        g_out = await_(g_out)[0]
        g_out_moved = grid.swap(g_out)
        output = settle(output, output_moved)
        d_inputs, gain_in_grad = [], 0.0
        for b in both:
            d_h1 = sums[b][0] + hold(sums[b][1]).astype(F32)
            d_ln, part = layer_norm_back(d_h1, rows(scaled_in, b), rows(inverse_in, b), gain_in)
            gain_in_grad = gain_in_grad + part
            d_inputs.append(mark(d_x1[b] + d_ln))
        d_input = jnp.concatenate(d_inputs)
        d_input_moved = grid.swap(hold(d_input))
        g_out = settle(g_out, g_out_moved)
        d_input = settle(d_input, d_input_moved)
        grad_norms = grid.total(hold(jnp.stack([gain_in_grad, gain_mid_grad])))
        mark(grad_norms)
        g_down, g_up, g_out = [hold(g).astype(F32) for g in (g_down.T, g_up, g_out.T)]
        last[:] = [g_down, g_up, g_out]
        g_vg = await_(g_vg)[0]
        g_vg = mark(settle(g_vg, grid.swap(g_vg)).astype(F32))
        g_qk = await_(g_qk)[0]
        g_qk = settle(g_qk, grid.swap(g_qk)).astype(F32)
        whole = (micro, 1, piece, width)
        return (
            output.reshape(whole),
            d_input.reshape(whole),
            grad_norms,
            g_qk[:, :dk],
            g_qk[:, dk:],
            g_vg[:, :dv],
            g_vg[:, dv:],
            g_out,
            g_up,
            g_down,
        )

    return on_device


def solution(mesh):
    grid = Grid(mesh.shape["seq"], mesh.shape["fsdp"])
    rows = P("fsdp", "seq")
    cols = P("seq", "fsdp")
    tok = P(None, "fsdp", "seq", None)
    return jax.shard_map(
        make_on_device(grid),
        mesh=mesh,
        in_specs=(tok, P(), rows, rows, rows, rows, cols, rows, cols, P(None, "fsdp", None), tok),
        out_specs=(tok, tok, P(), rows, rows, rows, rows, cols, rows, cols),
        check_vma=False,
    )
```

```python
import jax
import jax.numpy as jnp
from jax import lax
from jax.experimental import pallas as pl
from jax.experimental.pallas import tpu as pltpu
from jax.sharding import PartitionSpec as P

KEY_HEAD = 256
VAL_HEAD = 512
ROT = KEY_HEAD // 2
eps_norm = 1e-05
eps_group = 1.0
BF = jnp.bfloat16
F32 = jnp.float32
AXES = ("seq", "fsdp")
ANY = pl.BlockSpec(memory_space=pl.ANY)


def nn(left, right):
    return jnp.dot(left, right, preferred_element_type=F32)


def nt(left, right):
    return lax.dot_general(left, right, (((1,), (1,)), ((), ())), preferred_element_type=F32)


def tn(left, right):
    return lax.dot_general(left, right, (((0,), (0,)), ((), ())), preferred_element_type=F32)


def after(value, *first):
    return lax.optimization_barrier((value, *first))[0]


class Grid:
    def __init__(self, n_seq, n_fsdp):
        assert n_seq == 4 and n_fsdp % 2 == 0
        self.n_fsdp, self.nz = n_fsdp, n_fsdp // 2
        self.lines = [[z * 2 + x for z in range(self.nz)] for x in range(2)]
        self.groups = [
            [(y * 2 + c) * n_fsdp + z * 2 + x for z in range(self.nz) for c in range(2)]
            for y in range(2)
            for x in range(2)
        ]

    def send(self, value, move):
        found = []
        for y in range(2):
            for c in range(2):
                for z in range(self.nz):
                    for x in range(2):
                        y2, c2, z2, x2 = move(y, c, z, x)
                        src = (y * 2 + c) * self.n_fsdp + z * 2 + x
                        dst = (y2 * 2 + c2) * self.n_fsdp + z2 * 2 + x2
                        if src != dst:
                            found.append((src, dst))
        return lax.ppermute(value, AXES, found)

    def flip_z(self, value, bit):
        return self.send(value, lambda y, c, z, x: (y, c, z ^ bit, x))

    def flip_c(self, value):
        return self.send(value, lambda y, c, z, x: (y, 1 - c, z, x))

    def flip_y(self, value):
        return self.send(value, lambda y, c, z, x: (1 - y, c, z, x))

    def flip_x(self, value):
        return self.send(value, lambda y, c, z, x: (y, c, z, 1 - x))

    def first(self, b, value):
        return self.flip_y(value) if b == 0 else self.flip_x(value)

    def second(self, b, value):
        return self.flip_x(value) if b == 0 else self.flip_y(value)

    def swap(self, value):
        return self.send(value.astype(BF), lambda y, c, z, x: (y, x, z, c))

    def gather_weight(self, shard):
        return lax.all_gather(shard, AXES, axis=0, tiled=True, axis_index_groups=self.groups)

    def scatter_grad(self, value):
        return lax.psum_scatter(
            value, AXES, scatter_dimension=0, tiled=True, axis_index_groups=self.groups
        )

    def gather_line(self, shard):
        return lax.all_gather(shard, "fsdp", axis=0, tiled=True, axis_index_groups=self.lines)

    def scatter_line(self, value):
        return lax.psum_scatter(
            value, "fsdp", scatter_dimension=0, tiled=True, axis_index_groups=self.lines
        )

    def total(self, value):
        for flip in (self.flip_y, self.flip_c):
            value = value + flip(value)
        if self.nz & (self.nz - 1):
            value = lax.psum(value, "fsdp", axis_index_groups=self.lines)
        else:
            bit = 1
            while bit < self.nz:
                value = value + self.flip_z(value, bit)
                bit *= 2
        return value + self.flip_x(value)


def call(body, grid, ins, outs, shapes, scratch=(), flops=0, moved=0):
    return pl.pallas_call(
        body,
        out_shape=shapes,
        grid=grid,
        in_specs=ins,
        out_specs=outs,
        scratch_shapes=list(scratch),
        cost_estimate=pl.CostEstimate(
            flops=flops, bytes_accessed=moved, transcendentals=0
        ),
        compiler_params=pltpu.CompilerParams(vmem_limit_bytes=63 << 20),
    )


def shape(rows, cols, dtype=BF):
    return jax.ShapeDtypeStruct((rows, cols), dtype)


def spec(rows, cols, index):
    return pl.BlockSpec((rows, cols), index)


def copies_into(pieces, target, sems):
    copies, row = [], 0
    for i, piece in enumerate(pieces):
        rows = piece.shape[0]
        copies.append(pltpu.make_async_copy(piece, target.at[pl.ds(row, rows)], sems.at[i]))
        row += rows
    return copies


def fetch(pieces, target, sems):
    copies = copies_into(pieces, target, sems)
    for copy in copies:
        copy.start()
    for copy in copies:
        copy.wait()


def fetch_and_keep(j, steps, pieces, target, out, sems):
    keep = pltpu.make_async_copy(target, out, sems.at[len(pieces)])

    @pl.when(j == 0)
    def _():
        fetch(pieces, target, sems)
        keep.start()

    return keep


def assemble(pieces):
    n = len(pieces)

    def body(*refs):
        fetch(refs[:n], refs[n], refs[n + 1])

    rows = sum(p.shape[0] for p in pieces)
    cols = pieces[0].shape[1]
    return pl.pallas_call(
        body,
        out_shape=shape(rows, cols),
        in_specs=[ANY] * n,
        scratch_shapes=[pltpu.SemaphoreType.DMA((n,))],
        cost_estimate=pl.CostEstimate(
            flops=0, bytes_accessed=4 * rows * cols, transcendentals=0
        ),
    )(*pieces)


def rotated(first, second, cos_part, sin_part):
    return (first * cos_part - second * sin_part, second * cos_part + first * sin_part)


def project_turned(pieces, weight, cos_table, sin_table):
    n = len(pieces)
    rows = sum(p.shape[0] for p in pieces)
    width = pieces[0].shape[1]
    cols = weight.shape[1]
    tile, chunk = 512, 512
    steps = cols // tile

    def body(*refs):
        w_ref, cos_ref, sin_ref, out_ref, o_ref, h_ref, sems = refs[n:]
        j = pl.program_id(0)
        keep = fetch_and_keep(j, steps, refs[:n], h_ref, out_ref, sems)

        def step(i, _):
            at = pl.ds(pl.multiple_of(i * chunk, chunk), chunk)
            acc = nn(h_ref[at, :], w_ref[...])
            for s in range(0, tile, KEY_HEAD):
                u, v = rotated(
                    acc[:, s : s + ROT],
                    acc[:, s + ROT : s + KEY_HEAD],
                    cos_ref[at, :],
                    sin_ref[at, :],
                )
                o_ref[at, s : s + ROT] = u.astype(BF)
                o_ref[at, s + ROT : s + KEY_HEAD] = v.astype(BF)
            return 0

        lax.fori_loop(0, rows // chunk, step, 0, unroll=True)

        @pl.when(j == steps - 1)
        def _():
            keep.wait()

    return call(
        body,
        (steps,),
        [ANY] * n
        + [spec(width, tile, lambda j: (0, j))]
        + [spec(rows, ROT, lambda j: (0, 0))] * 2,
        [ANY, spec(rows, tile, lambda j: (0, j))],
        [shape(rows, width), shape(rows, cols)],
        [pltpu.VMEM((rows, width), BF), pltpu.SemaphoreType.DMA((n + 1,))],
        2 * rows * width * cols,
        2 * (2 * rows * width + width * cols + rows * cols),
    )(*pieces, weight, cos_table, sin_table)


def project_plain(h1, weight, gate_cols):
    rows, width = h1.shape
    cols = weight.shape[1]
    tile, chunk = 512, 512
    first = (cols - gate_cols) // tile

    def body(h_ref, w_ref, v_ref, gate_ref):
        j = pl.program_id(0)

        def step(i, _):
            at = pl.ds(pl.multiple_of(i * chunk, chunk), chunk)
            acc = nn(h_ref[at, :], w_ref[...])

            @pl.when(j < first)
            def _():
                v_ref[at, :] = acc.astype(BF)

            @pl.when(j >= first)
            def _():
                gate_ref[at, :] = acc

            return 0

        lax.fori_loop(0, rows // chunk, step, 0, unroll=True)

    return call(
        body,
        (cols // tile,),
        [spec(rows, width, lambda j: (0, 0)), spec(width, tile, lambda j: (0, j))],
        [
            spec(rows, tile, lambda j: (0, jnp.minimum(j, first - 1))),
            spec(rows, tile, lambda j: (0, jnp.maximum(j - first, 0))),
        ],
        [shape(rows, cols - gate_cols), shape(rows, gate_cols, F32)],
        (),
        2 * rows * width * cols,
        2 * (rows * width + width * cols + 2 * rows * cols),
    )(h1, weight)


def decay_chunk(col_ref, row_ref, at, log_gamma):
    pos_n, seg_n = col_ref[at, 0:1], col_ref[at, 1:2]
    pos_m, seg_m = row_ref[0:1, :], row_ref[1:2, :]
    distance = pos_n - pos_m
    allowed = (distance >= 0.0) & (seg_n == seg_m)
    value = jnp.exp(jnp.maximum(distance, 0.0) * log_gamma) * (KEY_HEAD**-0.5)
    return jnp.where(allowed, value, 0.0)


def sigmoid(value):
    return 1.0 / (1.0 + jnp.exp(-value))


def retain(qk, values, gate, col_info, row_info, log_gamma, heads, micro):
    rows = qk.shape[0] // micro
    dv = heads * VAL_HEAD
    chunk = 512

    def body(q_ref, k_ref, v_ref, gate_ref, col_ref, row_ref, lg_ref, gated_ref):
        log_g = lg_ref[pl.program_id(1)]

        def step(i, _):
            at = pl.ds(pl.multiple_of(i * chunk, chunk), chunk)
            decay = decay_chunk(col_ref, row_ref, at, log_g)
            weights = (nt(q_ref[at, :], k_ref[...]) * decay).astype(BF)
            kept = nn(weights, v_ref[...])
            scale = lax.rsqrt(jnp.mean(kept * kept, axis=-1, keepdims=True) + eps_group)
            gate = gate_ref[at, :]
            gated_ref[at, :] = (gate * sigmoid(gate) * (kept * scale)).astype(BF)
            return 0

        lax.fori_loop(0, rows // chunk, step, 0, unroll=True)

    return call(
        body,
        (micro, heads),
        [
            spec(rows, KEY_HEAD, lambda b, h: (b, h)),
            spec(rows, KEY_HEAD, lambda b, h: (b, heads + h)),
            spec(rows, VAL_HEAD, lambda b, h: (b, h)),
            spec(rows, VAL_HEAD, lambda b, h: (b, h)),
            spec(rows, 128, lambda b, h: (b, 0)),
            spec(8, rows, lambda b, h: (b, 0)),
            pl.BlockSpec(memory_space=pltpu.SMEM),
        ],
        spec(rows, VAL_HEAD, lambda b, h: (b, h)),
        shape(micro * rows, dv),
        (),
        2 * micro * rows * rows * heads * (KEY_HEAD + VAL_HEAD),
        10 * micro * rows * dv,
    )(qk, qk, values, gate, col_info, row_info, log_gamma)


ROOT_2_PI = 0.7978845608028654


def feed_up(pieces, weight, hidden):
    n = len(pieces)
    rows = sum(p.shape[0] for p in pieces)
    width = pieces[0].shape[1]
    tile, chunk = 512, 512
    steps = hidden // tile

    def body(*refs):
        w_ref, out_ref, act_ref, slope_ref, h_ref, sems = refs[n:]
        j = pl.program_id(0)
        keep = fetch_and_keep(j, steps, refs[:n], h_ref, out_ref, sems)

        def step(i, _):
            at = pl.ds(pl.multiple_of(i * chunk, chunk), chunk)
            up = nn(h_ref[at, :], w_ref[...])
            square = up * up
            bent = jnp.tanh(ROOT_2_PI * (up + 0.044715 * square * up))
            act_ref[at, :] = (0.5 * up * (1.0 + bent)).astype(BF)
            inner = ROOT_2_PI * (1.0 + 3.0 * 0.044715 * square)
            slope = 0.5 * (1.0 + bent) + 0.5 * up * (1.0 - bent * bent) * inner
            slope_ref[at, :] = slope
            return 0

        lax.fori_loop(0, rows // chunk, step, 0, unroll=True)

        @pl.when(j == steps - 1)
        def _():
            keep.wait()

    return call(
        body,
        (steps,),
        [ANY] * n + [spec(width, tile, lambda j: (0, j))],
        [ANY] + [spec(rows, tile, lambda j: (0, j))] * 2,
        [shape(rows, width), shape(rows, hidden), shape(rows, hidden, F32)],
        [pltpu.VMEM((rows, width), BF), pltpu.SemaphoreType.DMA((n + 1,))],
        2 * rows * width * hidden,
        4 * rows * width + 2 * width * hidden + 6 * rows * hidden,
    )(*pieces, weight)


def in_pairs(flat):
    return [tuple(flat[i : i + 2]) for i in range(0, len(flat), 2)]


def hand_out_specs(micro, rows, width, tile, index):
    shapes = [shape(rows // 2, width), shape(rows // 2, width, F32)] * micro
    return [spec(rows // 2, tile, index)] * len(shapes), shapes


def hand_out(acc, b, outs):
    half = acc.shape[0] // 2
    outs[2 * b][...] = acc[half:].astype(BF)
    outs[2 * b + 1][...] = acc[:half]


def project_back(values, weights):
    n = len(values)
    rows = values[0].shape[0]
    width = weights[0][0].shape[0]
    tile = 512
    each = rows // 2
    sizes = [v.shape[1] for v in values]

    def body(*refs):
        outs = refs[2 * n :]
        for b in range(2):
            at = slice(b * each, (b + 1) * each)
            acc = nt(refs[0][at, :], refs[n][...])
            for i in range(1, n):
                acc = acc + nt(refs[i][at, :], refs[n + i][...])
            hand_out(acc, b, outs)

    out_specs, shapes = hand_out_specs(2, each, width, tile, lambda j: (0, j))
    flat = call(
        body,
        (width // tile,),
        [spec(rows, k, lambda j: (0, 0)) for k in sizes]
        + [spec(tile, k, lambda j, i=i: (j, i)) for k, (_, i) in zip(sizes, weights)],
        out_specs,
        shapes,
        (),
        2 * rows * width * sum(sizes),
        2 * (rows + width) * sum(sizes) + 3 * rows * width,
    )(*values, *[w for w, _ in weights])
    return in_pairs(flat)


def feed_back(cot, slope, weight, hidden):
    rows, width = cot.shape
    tile = 512
    micro, each = 2, rows // 2
    first, second = hidden // tile, width // tile

    def body(cot_ref, down_ref, up_ref, slope_ref, dup_ref, *rest):
        *outs, keep_ref = rest
        j = pl.program_id(0)

        for i in range(first):

            @pl.when(j == i)
            def _(i=i):
                for b in range(micro):
                    at = slice(b * each, (b + 1) * each)
                    d_act = nn(cot_ref[at, :], down_ref[...])
                    d_up = (d_act * slope_ref[at, :]).astype(BF)
                    dup_ref[at, :] = d_up
                    keep_ref[at, i * tile : (i + 1) * tile] = d_up

        @pl.when(j >= first)
        def _():
            acc = nt(keep_ref[...], up_ref[...])
            for b in range(micro):
                hand_out(acc[b * each : (b + 1) * each], b, outs)

    def early(j):
        return jnp.minimum(j, first - 1)

    def late(j):
        return jnp.maximum(j - first, 0)

    out_specs, shapes = hand_out_specs(micro, each, width, tile, lambda j: (0, late(j)))
    d_up, *flat = call(
        body,
        (first + second,),
        [
            spec(rows, width, lambda j: (0, 0)),
            spec(width, tile, lambda j: (0, first + early(j))),
            spec(tile, hidden, lambda j: (late(j), 0)),
            spec(rows, tile, lambda j: (0, early(j))),
        ],
        [spec(rows, tile, lambda j: (0, early(j)))] + out_specs,
        [shape(rows, hidden)] + shapes,
        [pltpu.VMEM((rows, hidden), BF)],
        4 * rows * width * hidden,
        5 * rows * width + 4 * width * hidden + 6 * rows * hidden,
    )(cot, weight, weight, slope)
    return d_up, in_pairs(flat)


def retain_back(d_mix, gate, qk, values, w_out, col_info, row_info, cos_table, sin_table,
                log_gamma, heads, micro):
    rows = d_mix.shape[0] // micro
    width = d_mix.shape[1]
    dk, dv = heads * KEY_HEAD, heads * VAL_HEAD

    def body(mix_ref, wo, gate_ref, q_ref, k_ref, v_ref, col_ref, row_ref, cos_ref,
             sin_ref, lg_ref, dv_ref, dg_ref, dq_ref, dk_ref):
        log_g = lg_ref[pl.program_id(0)]
        d_gated = nn(mix_ref[...], wo[...])
        decay = decay_chunk(col_ref, row_ref, slice(None), log_g)
        weights = (nt(q_ref[...], k_ref[...]) * decay).astype(BF)
        kept = nn(weights, v_ref[...])
        scale = lax.rsqrt(jnp.mean(kept * kept, axis=-1, keepdims=True) + eps_group)
        y_norm = kept * scale
        gate = gate_ref[...]
        sig = sigmoid(gate)
        dg_ref[...] = (d_gated * y_norm * sig * (1.0 + gate * (1.0 - sig))).astype(BF)
        d_y = d_gated * (gate * sig)
        d_ret = (
            scale * (d_y - y_norm * jnp.mean(d_y * y_norm, axis=-1, keepdims=True))
        ).astype(BF)
        d_scores = (nt(d_ret, v_ref[...]) * decay).astype(BF)
        dv_ref[...] = tn(weights, d_ret).astype(BF)
        d_k = tn(d_scores, q_ref[...])
        d_q = nn(d_scores, k_ref[...])
        cos_part, sin_part = cos_ref[...], -sin_ref[...]
        for out, part in ((dq_ref, d_q), (dk_ref, d_k)):
            u, v = rotated(part[:, :ROT], part[:, ROT:], cos_part, sin_part)
            out[:, :ROT] = u.astype(BF)
            out[:, ROT:] = v.astype(BF)

    def per_head(cols, start=0):
        return spec(rows, cols, lambda h, b: (b, start + h))

    def per_row(height, cols):
        return spec(height, cols, lambda h, b: (b, 0))

    total = micro * rows
    return call(
        body,
        (heads, micro),
        [
            per_row(rows, width),
            spec(width, VAL_HEAD, lambda h, b: (0, h)),
            per_head(VAL_HEAD),
            per_head(KEY_HEAD),
            per_head(KEY_HEAD, heads),
            per_head(VAL_HEAD),
            per_row(rows, 128),
            per_row(8, rows),
            per_row(rows, ROT),
            per_row(rows, ROT),
            pl.BlockSpec(memory_space=pltpu.SMEM),
        ],
        [per_head(VAL_HEAD), per_head(VAL_HEAD), per_head(KEY_HEAD), per_head(KEY_HEAD)],
        [shape(total, dv), shape(total, dv), shape(total, dk), shape(total, dk)],
        (),
        2 * total * width * dv + 2 * total * rows * heads * 5 * VAL_HEAD,
        2 * width * dv + 20 * total * dv + 2 * total * width,
    )(
        d_mix, w_out, gate, qk, qk, values, col_info, row_info, cos_table, sin_table, log_gamma
    )


def weight_grad(left, rights):
    rows, width = left.shape
    sizes = [v.shape[1] for v in rights]
    cols = sum(sizes)
    tile = 512

    def body(left_ref, *refs):
        start = 0
        for right, size in zip(refs, sizes):
            refs[-1][:, start : start + size] = tn(left_ref[...], right[...]).astype(BF)
            start += size

    return call(
        body,
        (width // tile,),
        [spec(rows, tile, lambda i: (0, i))] + [spec(rows, k, lambda i: (0, 0)) for k in sizes],
        spec(tile, cols, lambda i: (i, 0)),
        shape(width, cols),
        (),
        2 * rows * width * cols,
        2 * (rows * (width + cols) + width * cols),
    )(left, *rights)


def weight_grad_pieces(pieces, right):
    n = len(pieces)
    rows, cols = right.shape
    width = pieces[0].shape[1]
    tile = 512
    steps = width // tile

    def body(*refs):
        right_ref, out_ref, o_ref, left_ref, sems = refs[n:]
        j = pl.program_id(0)
        keep = fetch_and_keep(j, steps, refs[:n], left_ref, out_ref, sems)
        at = pl.ds(pl.multiple_of(j * tile, tile), tile)
        o_ref[...] = tn(left_ref[:, at], right_ref[...]).astype(BF)

        @pl.when(j == steps - 1)
        def _():
            keep.wait()

    return call(
        body,
        (steps,),
        [ANY] * n + [spec(rows, cols, lambda i: (0, 0))],
        [ANY, spec(tile, cols, lambda i: (i, 0))],
        [shape(rows, width), shape(width, cols)],
        [pltpu.VMEM((rows, width), BF), pltpu.SemaphoreType.DMA((n + 1,))],
        2 * rows * width * cols,
        2 * (rows * (width + cols) + width * cols),
    )(*pieces, right)


def layer_norm_parts(inputs, gain_row):
    center = inputs - jnp.mean(inputs, axis=-1, keepdims=True)
    inverse = lax.rsqrt(jnp.mean(center * center, axis=-1, keepdims=True) + eps_norm)
    scaled = center * inverse
    return (scaled * gain_row, scaled, inverse)


def layer_norm_back(incoming, scaled, inverse, gain_row):
    upstream = incoming * gain_row
    centered_grad = (
        upstream
        - jnp.mean(upstream, axis=-1, keepdims=True)
        - scaled * jnp.mean(upstream * scaled, axis=-1, keepdims=True)
    )
    return (centered_grad * inverse, jnp.sum(incoming * scaled, axis=0))


def make_on_device(grid):
    def on_device(
        tokens, norm_gains, w_query, w_key, w_value, w_gate, w_out, w_up, w_down, segments, d_output
    ):
        micro, _, piece, width = tokens.shape
        assert micro == 2
        own, length = micro * piece, 4 * piece
        dk, dv = w_query.shape[1], w_value.shape[1]
        heads = dk // KEY_HEAD
        hidden = w_up.shape[1]
        seq_id = lax.axis_index("seq")
        fsdp_id = lax.axis_index("fsdp")
        y, c = seq_id // 2, seq_id % 2
        x = fsdp_id % 2
        same = x == c
        both = range(micro)

        last = []

        def hold(value):
            return after(value, *last)

        def mark(value):
            last[:] = [value]
            return value

        def settle(value, moved):
            return mark(jnp.where(same, value, hold(moved).astype(value.dtype)))

        def rows(value, b):
            return value[b * piece : (b + 1) * piece]

        def await_(*values):
            waited = lax.optimization_barrier((*values, *last))[: len(values)]
            last[:] = [waited[0]]
            return list(waited)

        def pair(block, moved):
            return mark(jnp.concatenate([block, hold(moved)], axis=0))

        def reduce_second(b, kept, got):
            got = hold(got)
            sent = (kept[piece:] + got[piece:].astype(F32)).astype(BF)
            return kept[:piece] + got[:piece].astype(F32), grid.first(b, mark(sent))

        line_qk = grid.gather_line(mark(jnp.concatenate([w_query, w_key], axis=1)))
        w_vgo = mark(jnp.concatenate([hold(w_value), w_gate, w_out.T], axis=1))
        vgo_moved = grid.swap(w_vgo)
        toks = tokens.reshape(own, width)
        toks_moved = grid.swap(toks)
        segs = segments.reshape(micro, length).astype(F32)
        segs_moved = grid.swap(segs)
        ud_cot = mark(
            jnp.concatenate(
                [jnp.concatenate([w_up, hold(w_down).T], axis=1), d_output.reshape(own, width)],
                axis=0,
            )
        )

        ranks = [
            [2 * (y ^ i) + (x ^ j) for i, j in ((0, 0), (1, 0), (0, 1), (1, 1))],
            [2 * (y ^ i) + (x ^ j) for i, j in ((0, 0), (0, 1), (1, 0), (1, 1))],
        ]
        positions = jnp.stack(
            [jnp.concatenate([r * piece + jnp.arange(piece) for r in ranks[b]]) for b in both]
        ).astype(F32)
        frequency = jnp.exp(-jnp.log(10000.0) * 2.0 * jnp.arange(ROT, dtype=F32) / KEY_HEAD)
        angles = hold(positions).reshape(-1, 1) * frequency[None, :]
        cos_table, sin_table = jnp.cos(angles), jnp.sin(angles)
        mark(cos_table)
        head_ids = (y * 2 + x) * heads + jnp.arange(heads, dtype=jnp.int32)
        log_gamma = jnp.log1p(-jnp.exp2(-5.0 - head_ids.astype(F32)))
        gain_in, gain_mid = norm_gains[0], norm_gains[1]

        w_vgo = settle(w_vgo, vgo_moved)
        full_vg = grid.gather_weight(w_vgo[:, : 2 * dv])
        full_o = grid.gather_weight(w_vgo[:, 2 * dv :])
        toks = settle(toks, toks_moved)
        xin = toks.astype(F32)
        normed, scaled_in, inverse_in = layer_norm_parts(xin, gain_in)
        normed = mark(normed.astype(BF))
        h1_own = [rows(normed, b) for b in both]
        h1_first = [grid.first(b, h1_own[b]) for b in both]
        line_qk = await_(line_qk)[0]
        qk_moved = grid.swap(line_qk)
        segs = settle(segs, segs_moved)
        seg_rows = jnp.stack(
            [
                jnp.concatenate(
                    [lax.dynamic_slice_in_dim(segs[b], r * piece, piece) for r in ranks[b]]
                )
                for b in both
            ]
        )
        lanes = jnp.arange(128)[None, :]
        col_info = jnp.where(
            lanes == 0,
            positions.reshape(-1, 1),
            jnp.where(lanes == 1, seg_rows.reshape(-1, 1), 0.0),
        )
        row_info = jnp.stack([positions, seg_rows] + [jnp.zeros_like(positions)] * 6, axis=1)
        row_info = mark(row_info.reshape(8 * micro, length))
        h1_second = [grid.second(b, pair(h1_own[b], h1_first[b])) for b in both]
        ud_cot_moved = grid.swap(after(ud_cot, line_qk))
        h1_second = await_(*h1_second)
        line_qk = settle(line_qk, qk_moved)
        line_other = grid.flip_c(line_qk)
        even, odd = [v.reshape(grid.nz, 1, -1, 2 * dk) for v in (line_qk, hold(line_other))]
        full_qk = jnp.where(
            c == 0,
            jnp.concatenate([even, odd], axis=1),
            jnp.concatenate([odd, even], axis=1),
        ).reshape(width, 2 * dk)
        mark(full_qk)
        h1, qk = project_turned(
            [p for b in both for p in (h1_own[b], h1_first[b], h1_second[b])],
            full_qk, cos_table, sin_table,
        )
        mark(qk)
        ud_cot = settle(ud_cot, ud_cot_moved)
        full_ud = grid.gather_weight(ud_cot[:-own])
        cots = ud_cot[-own:]
        cot_own = [rows(cots, b) for b in both]
        cot_first = [grid.first(b, cot_own[b]) for b in both]
        values, gate = project_plain(hold(h1), hold(full_vg), dv)
        mark(values)
        cot_second = [grid.second(b, pair(cot_own[b], cot_first[b])) for b in both]
        gated = mark(
            retain(qk, hold(values), gate, col_info, row_info, log_gamma, heads, micro)
        )
        outs = project_back([hold(gated)], [(full_o, 0)])
        mark(outs[0][0])
        moved = [grid.second(b, outs[b][0]) for b in both]
        cot = mark(
            assemble([p for b in both for p in (cot_own[b], cot_first[b], hold(cot_second[b]))])
        )
        sums = [reduce_second(b, outs[b][1], moved[b]) for b in both]
        x1, mid, scaled_mid, inverse_mid, mid_first = [], [], [], [], []
        for b in both:
            x1.append(rows(xin, b) + (sums[b][0] + hold(sums[b][1]).astype(F32)))
            out, scaled, inverse = layer_norm_parts(x1[b], gain_mid)
            mid.append(mark(out.astype(BF)))
            scaled_mid.append(scaled)
            inverse_mid.append(inverse)
            mid_first.append(grid.first(b, mid[b]))
        mid_second = [grid.second(b, pair(mid[b], mid_first[b])) for b in both]
        h2, act, slope = feed_up(
            [p for b in both for p in (mid[b], mid_first[b], hold(mid_second[b]))], full_ud, hidden
        )
        mark(act)

        def grad(left, rights):
            return mark(weight_grad(hold(left), rights))

        g_down = grid.scatter_grad(grad(cot, [act]))
        d_up, outs = feed_back(hold(cot), slope, full_ud, hidden)
        mark(d_up)
        moved = [grid.second(b, outs[b][0]) for b in both]
        g_up = grad(h2, [d_up])
        sums = [reduce_second(b, outs[b][1], moved[b]) for b in both]
        g_up = grid.scatter_grad(hold(g_up))
        d_x1, mix_first, gain_mid_grad = [], [], 0.0
        for b in both:
            d_h2 = sums[b][0] + hold(sums[b][1]).astype(F32)
            d_ln, part = layer_norm_back(d_h2, scaled_mid[b], inverse_mid[b], gain_mid)
            gain_mid_grad = gain_mid_grad + part
            d_x1.append(cot_own[b].astype(F32) + d_ln)
            mix_first.append((mark(d_x1[b].astype(BF)),))
            mix_first[b] = mix_first[b] + (grid.first(b, mix_first[b][0]),)
        g_down = await_(g_down)[0]
        down = project_back([hold(act)], [(full_ud, 1)])
        mark(down[0][0])
        mix = [(v, f, grid.second(b, pair(v, f))) for b, (v, f) in enumerate(mix_first)]
        d_mix, g_out = weight_grad_pieces(
            [p for b in both for p in mix[b][:2] + (hold(mix[b][2]),)], gated
        )
        g_out = grid.scatter_grad(mark(g_out))
        g_ud = mark(jnp.concatenate([hold(g_up), g_down], axis=1))
        g_ud_moved = grid.swap(g_ud)
        down_moved = [grid.second(b, hold(down[b][0])) for b in both]
        d_v, d_gate, d_q, d_k = retain_back(
            hold(d_mix), gate, qk, values, full_o, col_info, row_info, cos_table, sin_table,
            log_gamma, heads, micro,
        )
        mark(d_v)
        g_vg = grid.scatter_grad(grad(h1, [d_v, d_gate]))
        down = [reduce_second(b, down[b][1], down_moved[b]) for b in both]
        outs = project_back(
            [d_q, d_k, d_v, hold(d_gate)],
            [(full_qk, 0), (full_qk, 1), (full_vg, 0), (full_vg, 1)],
        )
        mark(outs[0][0])
        moved = [grid.second(b, outs[b][0]) for b in both]
        g_qk = grid.scatter_grad(grad(h1, [d_q, d_k]))
        output = mark(
            jnp.concatenate(
                [x1[b] + (down[b][0] + hold(down[b][1]).astype(F32)) for b in both]
            ).astype(BF)
        )
        output_moved = grid.swap(output)
        g_ud = settle(g_ud, g_ud_moved)
        sums = [reduce_second(b, outs[b][1], moved[b]) for b in both]
        g_out = await_(g_out)[0]
        g_out_moved = grid.swap(g_out)
        output = settle(output, output_moved)
        d_inputs, gain_in_grad = [], 0.0
        for b in both:
            d_h1 = sums[b][0] + hold(sums[b][1]).astype(F32)
            d_ln, part = layer_norm_back(d_h1, rows(scaled_in, b), rows(inverse_in, b), gain_in)
            gain_in_grad = gain_in_grad + part
            d_inputs.append(mark(d_x1[b] + d_ln))
        d_input = jnp.concatenate(d_inputs)
        d_input_moved = grid.swap(hold(d_input))
        g_out = settle(g_out, g_out_moved)
        grad_norms = grid.total(hold(jnp.stack([gain_in_grad, gain_mid_grad])))
        mark(grad_norms)
        d_input = settle(d_input, d_input_moved)
        g_down, g_up, g_out = [
            hold(g).astype(F32) for g in (g_ud[:, hidden:].T, g_ud[:, :hidden], g_out.T)
        ]
        last[:] = [g_down, g_up, g_out]
        g_vg = await_(g_vg)[0]
        g_vg = mark(settle(g_vg, grid.swap(g_vg)).astype(F32))
        g_qk = await_(g_qk)[0]
        g_qk = settle(g_qk, grid.swap(g_qk)).astype(F32)
        whole = (micro, 1, piece, width)
        return (
            output.reshape(whole),
            d_input.reshape(whole),
            grad_norms,
            g_qk[:, :dk],
            g_qk[:, dk:],
            g_vg[:, :dv],
            g_vg[:, dv:],
            g_out,
            g_up,
            g_down,
        )

    return on_device


def solution(mesh):
    grid = Grid(mesh.shape["seq"], mesh.shape["fsdp"])
    rows = P("fsdp", "seq")
    cols = P("seq", "fsdp")
    tok = P(None, "fsdp", "seq", None)
    return jax.shard_map(
        make_on_device(grid),
        mesh=mesh,
        in_specs=(tok, P(), rows, rows, rows, rows, cols, rows, cols, P(None, "fsdp", None), tok),
        out_specs=(tok, tok, P(), rows, rows, rows, rows, cols, rows, cols),
        check_vma=False,
    )
```

```python
import jax
import jax.numpy as jnp
from jax import lax
from jax.experimental import pallas as pl
from jax.experimental.pallas import tpu as pltpu
from jax.sharding import PartitionSpec as P

KEY_HEAD = 256
VAL_HEAD = 512
ROT = KEY_HEAD // 2
eps_norm = 1e-05
eps_group = 1.0
BF = jnp.bfloat16
F32 = jnp.float32
AXES = ("seq", "fsdp")
ANY = pl.BlockSpec(memory_space=pl.ANY)


def nn(left, right):
    return jnp.dot(left, right, preferred_element_type=F32)


def nt(left, right):
    return lax.dot_general(left, right, (((1,), (1,)), ((), ())), preferred_element_type=F32)


def tn(left, right):
    return lax.dot_general(left, right, (((0,), (0,)), ((), ())), preferred_element_type=F32)


def after(value, *first):
    return lax.optimization_barrier((value, *first))[0]


class Grid:
    def __init__(self, n_seq, n_fsdp):
        assert n_seq == 4 and n_fsdp % 2 == 0
        self.n_fsdp, self.nz = n_fsdp, n_fsdp // 2
        self.lines = [[z * 2 + x for z in range(self.nz)] for x in range(2)]
        self.groups = [
            [(y * 2 + c) * n_fsdp + z * 2 + x for z in range(self.nz) for c in range(2)]
            for y in range(2)
            for x in range(2)
        ]

    def send(self, value, move):
        found = []
        for y in range(2):
            for c in range(2):
                for z in range(self.nz):
                    for x in range(2):
                        y2, c2, z2, x2 = move(y, c, z, x)
                        src = (y * 2 + c) * self.n_fsdp + z * 2 + x
                        dst = (y2 * 2 + c2) * self.n_fsdp + z2 * 2 + x2
                        if src != dst:
                            found.append((src, dst))
        return lax.ppermute(value, AXES, found)

    def flip_z(self, value, bit):
        return self.send(value, lambda y, c, z, x: (y, c, z ^ bit, x))

    def flip_c(self, value):
        return self.send(value, lambda y, c, z, x: (y, 1 - c, z, x))

    def flip_y(self, value):
        return self.send(value, lambda y, c, z, x: (1 - y, c, z, x))

    def flip_x(self, value):
        return self.send(value, lambda y, c, z, x: (y, c, z, 1 - x))

    def first(self, b, value):
        return self.flip_y(value) if b == 0 else self.flip_x(value)

    def second(self, b, value):
        return self.flip_x(value) if b == 0 else self.flip_y(value)

    def swap(self, value):
        return self.send(value.astype(BF), lambda y, c, z, x: (y, x, z, c))

    def gather_weight(self, shard):
        return lax.all_gather(shard, AXES, axis=0, tiled=True, axis_index_groups=self.groups)

    def scatter_grad(self, value):
        return lax.psum_scatter(
            value, AXES, scatter_dimension=0, tiled=True, axis_index_groups=self.groups
        )

    def gather_line(self, shard):
        return lax.all_gather(shard, "fsdp", axis=0, tiled=True, axis_index_groups=self.lines)

    def scatter_line(self, value):
        return lax.psum_scatter(
            value, "fsdp", scatter_dimension=0, tiled=True, axis_index_groups=self.lines
        )

    def total(self, value):
        for flip in (self.flip_y, self.flip_c):
            value = value + flip(value)
        if self.nz & (self.nz - 1):
            value = lax.psum(value, "fsdp", axis_index_groups=self.lines)
        else:
            bit = 1
            while bit < self.nz:
                value = value + self.flip_z(value, bit)
                bit *= 2
        return value + self.flip_x(value)


def call(body, grid, ins, outs, shapes, scratch=(), flops=0, moved=0):
    return pl.pallas_call(
        body,
        out_shape=shapes,
        grid=grid,
        in_specs=ins,
        out_specs=outs,
        scratch_shapes=list(scratch),
        cost_estimate=pl.CostEstimate(
            flops=flops, bytes_accessed=moved, transcendentals=0
        ),
        compiler_params=pltpu.CompilerParams(vmem_limit_bytes=63 << 20),
    )


def shape(rows, cols, dtype=BF):
    return jax.ShapeDtypeStruct((rows, cols), dtype)


def spec(rows, cols, index):
    return pl.BlockSpec((rows, cols), index)


def copies_into(pieces, target, sems):
    copies, row = [], 0
    for i, piece in enumerate(pieces):
        rows = piece.shape[0]
        copies.append(pltpu.make_async_copy(piece, target.at[pl.ds(row, rows)], sems.at[i]))
        row += rows
    return copies


def fetch(pieces, target, sems):
    copies = copies_into(pieces, target, sems)
    for copy in copies:
        copy.start()
    for copy in copies:
        copy.wait()


def fetch_and_keep(j, steps, pieces, target, out, sems):
    keep = pltpu.make_async_copy(target, out, sems.at[len(pieces)])

    @pl.when(j == 0)
    def _():
        fetch(pieces, target, sems)
        keep.start()

    return keep


def assemble(pieces):
    n = len(pieces)

    def body(*refs):
        fetch(refs[:n], refs[n], refs[n + 1])

    rows = sum(p.shape[0] for p in pieces)
    cols = pieces[0].shape[1]
    return pl.pallas_call(
        body,
        out_shape=shape(rows, cols),
        in_specs=[ANY] * n,
        scratch_shapes=[pltpu.SemaphoreType.DMA((n,))],
        cost_estimate=pl.CostEstimate(
            flops=0, bytes_accessed=4 * rows * cols, transcendentals=0
        ),
    )(*pieces)


def rotated(first, second, cos_part, sin_part):
    return (first * cos_part - second * sin_part, second * cos_part + first * sin_part)


def project_turned(pieces, weight, cos_table, sin_table):
    n = len(pieces)
    rows = sum(p.shape[0] for p in pieces)
    width = pieces[0].shape[1]
    cols = weight.shape[1]
    tile, chunk = 512, 512
    steps = cols // tile

    def body(*refs):
        w_ref, cos_ref, sin_ref, out_ref, o_ref, h_ref, sems = refs[n:]
        j = pl.program_id(0)
        keep = fetch_and_keep(j, steps, refs[:n], h_ref, out_ref, sems)

        def step(i, _):
            at = pl.ds(pl.multiple_of(i * chunk, chunk), chunk)
            acc = nn(h_ref[at, :], w_ref[...])
            for s in range(0, tile, KEY_HEAD):
                u, v = rotated(
                    acc[:, s : s + ROT],
                    acc[:, s + ROT : s + KEY_HEAD],
                    cos_ref[at, :],
                    sin_ref[at, :],
                )
                o_ref[at, s : s + ROT] = u.astype(BF)
                o_ref[at, s + ROT : s + KEY_HEAD] = v.astype(BF)
            return 0

        lax.fori_loop(0, rows // chunk, step, 0, unroll=True)

        @pl.when(j == steps - 1)
        def _():
            keep.wait()

    return call(
        body,
        (steps,),
        [ANY] * n
        + [spec(width, tile, lambda j: (0, j))]
        + [spec(rows, ROT, lambda j: (0, 0))] * 2,
        [ANY, spec(rows, tile, lambda j: (0, j))],
        [shape(rows, width), shape(rows, cols)],
        [pltpu.VMEM((rows, width), BF), pltpu.SemaphoreType.DMA((n + 1,))],
        2 * rows * width * cols,
        2 * (2 * rows * width + width * cols + rows * cols),
    )(*pieces, weight, cos_table, sin_table)


def project_plain(h1, weight, gate_cols):
    rows, width = h1.shape
    cols = weight.shape[1]
    tile, chunk = 512, 512
    first = (cols - gate_cols) // tile

    def body(h_ref, w_ref, v_ref, gate_ref):
        j = pl.program_id(0)

        def step(i, _):
            at = pl.ds(pl.multiple_of(i * chunk, chunk), chunk)
            acc = nn(h_ref[at, :], w_ref[...])

            @pl.when(j < first)
            def _():
                v_ref[at, :] = acc.astype(BF)

            @pl.when(j >= first)
            def _():
                gate_ref[at, :] = acc

            return 0

        lax.fori_loop(0, rows // chunk, step, 0, unroll=True)

    return call(
        body,
        (cols // tile,),
        [spec(rows, width, lambda j: (0, 0)), spec(width, tile, lambda j: (0, j))],
        [
            spec(rows, tile, lambda j: (0, jnp.minimum(j, first - 1))),
            spec(rows, tile, lambda j: (0, jnp.maximum(j - first, 0))),
        ],
        [shape(rows, cols - gate_cols), shape(rows, gate_cols, F32)],
        (),
        2 * rows * width * cols,
        2 * (rows * width + width * cols + 2 * rows * cols),
    )(h1, weight)


def decay_chunk(col_ref, row_ref, at, log_gamma):
    pos_n, seg_n = col_ref[at, 0:1], col_ref[at, 1:2]
    pos_m, seg_m = row_ref[0:1, :], row_ref[1:2, :]
    distance = pos_n - pos_m
    allowed = (distance >= 0.0) & (seg_n == seg_m)
    value = jnp.exp(jnp.maximum(distance, 0.0) * log_gamma) * (KEY_HEAD**-0.5)
    return jnp.where(allowed, value, 0.0)


def sigmoid(value):
    return 1.0 / (1.0 + jnp.exp(-value))


def retain(qk, values, gate, col_info, row_info, log_gamma, heads, micro):
    rows = qk.shape[0] // micro
    dv = heads * VAL_HEAD
    chunk = 512

    def body(q_ref, k_ref, v_ref, gate_ref, col_ref, row_ref, lg_ref, gated_ref):
        log_g = lg_ref[pl.program_id(1)]

        def step(i, _):
            at = pl.ds(pl.multiple_of(i * chunk, chunk), chunk)
            decay = decay_chunk(col_ref, row_ref, at, log_g)
            weights = (nt(q_ref[at, :], k_ref[...]) * decay).astype(BF)
            kept = nn(weights, v_ref[...])
            scale = lax.rsqrt(jnp.mean(kept * kept, axis=-1, keepdims=True) + eps_group)
            gate = gate_ref[at, :]
            gated_ref[at, :] = (gate * sigmoid(gate) * (kept * scale)).astype(BF)
            return 0

        lax.fori_loop(0, rows // chunk, step, 0, unroll=True)

    return call(
        body,
        (micro, heads),
        [
            spec(rows, KEY_HEAD, lambda b, h: (b, h)),
            spec(rows, KEY_HEAD, lambda b, h: (b, heads + h)),
            spec(rows, VAL_HEAD, lambda b, h: (b, h)),
            spec(rows, VAL_HEAD, lambda b, h: (b, h)),
            spec(rows, 128, lambda b, h: (b, 0)),
            spec(8, rows, lambda b, h: (b, 0)),
            pl.BlockSpec(memory_space=pltpu.SMEM),
        ],
        spec(rows, VAL_HEAD, lambda b, h: (b, h)),
        shape(micro * rows, dv),
        (),
        2 * micro * rows * rows * heads * (KEY_HEAD + VAL_HEAD),
        10 * micro * rows * dv,
    )(qk, qk, values, gate, col_info, row_info, log_gamma)


ROOT_2_PI = 0.7978845608028654


def feed_up(pieces, weight, hidden):
    n = len(pieces)
    rows = sum(p.shape[0] for p in pieces)
    width = pieces[0].shape[1]
    tile, chunk = 512, 512
    steps = hidden // tile

    def body(*refs):
        w_ref, out_ref, act_ref, slope_ref, h_ref, sems = refs[n:]
        j = pl.program_id(0)
        keep = fetch_and_keep(j, steps, refs[:n], h_ref, out_ref, sems)

        def step(i, _):
            at = pl.ds(pl.multiple_of(i * chunk, chunk), chunk)
            up = nn(h_ref[at, :], w_ref[...])
            square = up * up
            bent = jnp.tanh(ROOT_2_PI * (up + 0.044715 * square * up))
            act_ref[at, :] = (0.5 * up * (1.0 + bent)).astype(BF)
            inner = ROOT_2_PI * (1.0 + 3.0 * 0.044715 * square)
            slope = 0.5 * (1.0 + bent) + 0.5 * up * (1.0 - bent * bent) * inner
            slope_ref[at, :] = slope
            return 0

        lax.fori_loop(0, rows // chunk, step, 0, unroll=True)

        @pl.when(j == steps - 1)
        def _():
            keep.wait()

    return call(
        body,
        (steps,),
        [ANY] * n + [spec(width, tile, lambda j: (0, j))],
        [ANY] + [spec(rows, tile, lambda j: (0, j))] * 2,
        [shape(rows, width), shape(rows, hidden), shape(rows, hidden, F32)],
        [pltpu.VMEM((rows, width), BF), pltpu.SemaphoreType.DMA((n + 1,))],
        2 * rows * width * hidden,
        4 * rows * width + 2 * width * hidden + 6 * rows * hidden,
    )(*pieces, weight)


def project_back(values, weights, cuts, dtype):
    n, m = len(values), len(cuts)
    rows = values[0].shape[0]
    width = weights[0][0].shape[0]
    tile = 512
    sizes = [v.shape[1] for v in values]

    def body(*refs):
        acc = 0.0
        for i in range(n):
            some = jnp.concatenate([refs[i][at : at + k, :] for at, k in cuts], axis=0)
            acc = acc + nt(some, refs[n + i][...])
        start = 0
        for out, (_, k) in zip(refs[2 * n :], cuts):
            out[...] = acc[start : start + k].astype(dtype)
            start += k

    taken = sum(k for _, k in cuts)
    return call(
        body,
        (width // tile,),
        [spec(rows, k, lambda j: (0, 0)) for k in sizes]
        + [spec(tile, k, lambda j, i=i: (j, i)) for k, (_, i) in zip(sizes, weights)],
        [spec(k, tile, lambda j: (0, j)) for _, k in cuts],
        [shape(k, width, dtype) for _, k in cuts],
        (),
        2 * taken * width * sum(sizes),
        2 * (rows + width) * sum(sizes) + 3 * taken * width,
    )(*values, *[w for w, _ in weights])


def feed_back(cot, slopes, w_up, w_down):
    rows, width = cot.shape
    hidden = w_up.shape[1]
    tile = 512
    half = rows // 2
    first, second = hidden // tile, width // tile

    def body(cot_ref, down_ref, up_ref, slope_a, slope_b, dup_ref, sent_0, sent_1, keep_ref):
        j = pl.program_id(0)

        for i in range(first):

            @pl.when(j == i)
            def _(i=i):
                for at, slope_ref in ((0, slope_a), (half, slope_b)):
                    d_act = nn(cot_ref[at : at + half, :], down_ref[...])
                    d_up = (d_act * slope_ref[...]).astype(BF)
                    dup_ref[at : at + half, :] = d_up
                    if at:
                        keep_ref[:, i * tile : (i + 1) * tile] = d_up

        @pl.when(j >= first)
        def _():
            acc = nt(keep_ref[...], up_ref[...]).astype(BF)
            sent_0[...] = acc[: half // 2]
            sent_1[...] = acc[half // 2 :]

    def early(j):
        return jnp.minimum(j, first - 1)

    def late(j):
        return jnp.maximum(j - first, 0)

    return call(
        body,
        (first + second,),
        [
            spec(rows, width, lambda j: (0, 0)),
            spec(width, tile, lambda j: (0, early(j))),
            spec(tile, hidden, lambda j: (late(j), 0)),
            spec(half, tile, lambda j: (0, early(j))),
            spec(half, tile, lambda j: (0, early(j))),
        ],
        [spec(rows, tile, lambda j: (0, early(j)))]
        + [spec(half // 2, tile, lambda j: (0, late(j)))] * 2,
        [shape(rows, hidden), shape(half // 2, width), shape(half // 2, width)],
        [pltpu.VMEM((half, hidden), BF)],
        3 * rows * width * hidden,
        4 * rows * width + 4 * width * hidden + 6 * rows * hidden,
    )(cot, w_down, w_up, *slopes)


def retain_back(d_mix, gate, qk, values, w_out, col_info, row_info, cos_table, sin_table,
                log_gamma, heads, micro):
    rows = d_mix.shape[0] // micro
    width = d_mix.shape[1]
    dk, dv = heads * KEY_HEAD, heads * VAL_HEAD

    def body(mix_ref, wo, gate_ref, q_ref, k_ref, v_ref, col_ref, row_ref, cos_ref,
             sin_ref, lg_ref, dv_ref, dg_ref, dq_ref, dk_ref):
        log_g = lg_ref[pl.program_id(0)]
        d_gated = nn(mix_ref[...], wo[...])
        decay = decay_chunk(col_ref, row_ref, slice(None), log_g)
        weights = (nt(q_ref[...], k_ref[...]) * decay).astype(BF)
        kept = nn(weights, v_ref[...])
        scale = lax.rsqrt(jnp.mean(kept * kept, axis=-1, keepdims=True) + eps_group)
        y_norm = kept * scale
        gate = gate_ref[...]
        sig = sigmoid(gate)
        dg_ref[...] = (d_gated * y_norm * sig * (1.0 + gate * (1.0 - sig))).astype(BF)
        d_y = d_gated * (gate * sig)
        d_ret = (
            scale * (d_y - y_norm * jnp.mean(d_y * y_norm, axis=-1, keepdims=True))
        ).astype(BF)
        d_scores = (nt(d_ret, v_ref[...]) * decay).astype(BF)
        dv_ref[...] = tn(weights, d_ret).astype(BF)
        d_k = tn(d_scores, q_ref[...])
        d_q = nn(d_scores, k_ref[...])
        cos_part, sin_part = cos_ref[...], -sin_ref[...]
        for out, part in ((dq_ref, d_q), (dk_ref, d_k)):
            u, v = rotated(part[:, :ROT], part[:, ROT:], cos_part, sin_part)
            out[:, :ROT] = u.astype(BF)
            out[:, ROT:] = v.astype(BF)

    def per_head(cols, start=0):
        return spec(rows, cols, lambda h, b: (b, start + h))

    def per_row(height, cols):
        return spec(height, cols, lambda h, b: (b, 0))

    total = micro * rows
    return call(
        body,
        (heads, micro),
        [
            per_row(rows, width),
            spec(width, VAL_HEAD, lambda h, b: (0, h)),
            per_head(VAL_HEAD),
            per_head(KEY_HEAD),
            per_head(KEY_HEAD, heads),
            per_head(VAL_HEAD),
            per_row(rows, 128),
            per_row(8, rows),
            per_row(rows, ROT),
            per_row(rows, ROT),
            pl.BlockSpec(memory_space=pltpu.SMEM),
        ],
        [per_head(VAL_HEAD), per_head(VAL_HEAD), per_head(KEY_HEAD), per_head(KEY_HEAD)],
        [shape(total, dv), shape(total, dv), shape(total, dk), shape(total, dk)],
        (),
        2 * total * width * dv + 2 * total * rows * heads * 5 * VAL_HEAD,
        2 * width * dv + 20 * total * dv + 2 * total * width,
    )(
        d_mix, w_out, gate, qk, qk, values, col_info, row_info, cos_table, sin_table, log_gamma
    )


def weight_grad(left, rights):
    rows, width = left.shape
    sizes = [v.shape[1] for v in rights]
    cols = sum(sizes)
    tile = 512

    def body(left_ref, *refs):
        start = 0
        for right, size in zip(refs, sizes):
            refs[-1][:, start : start + size] = tn(left_ref[...], right[...]).astype(BF)
            start += size

    return call(
        body,
        (width // tile,),
        [spec(rows, tile, lambda i: (0, i))] + [spec(rows, k, lambda i: (0, 0)) for k in sizes],
        spec(tile, cols, lambda i: (i, 0)),
        shape(width, cols),
        (),
        2 * rows * width * cols,
        2 * (rows * (width + cols) + width * cols),
    )(left, *rights)


def weight_grad_rows(rows, pairs):
    n = len(pairs)
    width, cols = pairs[0][0][0].shape[1], pairs[0][1][0].shape[1]
    tile = 512

    def body(*refs):
        acc = tn(refs[0][...], refs[n][...])
        for i in range(1, n):
            acc = acc + tn(refs[i][...], refs[n + i][...])
        refs[-1][...] = acc.astype(BF)

    return call(
        body,
        (width // tile,),
        [spec(rows, tile, lambda i, b=b: (b, i)) for (_, b), _ in pairs]
        + [spec(rows, cols, lambda i, b=b: (b, 0)) for _, (_, b) in pairs],
        spec(tile, cols, lambda i: (i, 0)),
        shape(width, cols),
        (),
        2 * n * rows * width * cols,
        2 * (n * rows * (width + cols) + width * cols),
    )(*[left for (left, _), _ in pairs], *[right for _, (right, _) in pairs])


def weight_grad_pieces(pieces, right):
    n = len(pieces)
    rows, cols = right.shape
    width = pieces[0].shape[1]
    tile = 512
    steps = width // tile

    def body(*refs):
        right_ref, out_ref, o_ref, left_ref, sems = refs[n:]
        j = pl.program_id(0)
        keep = fetch_and_keep(j, steps, refs[:n], left_ref, out_ref, sems)
        at = pl.ds(pl.multiple_of(j * tile, tile), tile)
        o_ref[...] = tn(left_ref[:, at], right_ref[...]).astype(BF)

        @pl.when(j == steps - 1)
        def _():
            keep.wait()

    return call(
        body,
        (steps,),
        [ANY] * n + [spec(rows, cols, lambda i: (0, 0))],
        [ANY, spec(tile, cols, lambda i: (i, 0))],
        [shape(rows, width), shape(width, cols)],
        [pltpu.VMEM((rows, width), BF), pltpu.SemaphoreType.DMA((n + 1,))],
        2 * rows * width * cols,
        2 * (rows * (width + cols) + width * cols),
    )(*pieces, right)


def layer_norm_parts(inputs, gain_row):
    center = inputs - jnp.mean(inputs, axis=-1, keepdims=True)
    inverse = lax.rsqrt(jnp.mean(center * center, axis=-1, keepdims=True) + eps_norm)
    scaled = center * inverse
    return (scaled * gain_row, scaled, inverse)


def layer_norm_back(incoming, scaled, inverse, gain_row):
    upstream = incoming * gain_row
    centered_grad = (
        upstream
        - jnp.mean(upstream, axis=-1, keepdims=True)
        - scaled * jnp.mean(upstream * scaled, axis=-1, keepdims=True)
    )
    return (centered_grad * inverse, jnp.sum(incoming * scaled, axis=0))


def make_on_device(grid):
    def on_device(
        tokens, norm_gains, w_query, w_key, w_value, w_gate, w_out, w_up, w_down, segments, d_output
    ):
        micro, _, piece, width = tokens.shape
        assert micro == 2
        own, length = micro * piece, 4 * piece
        dk, dv = w_query.shape[1], w_value.shape[1]
        heads = dk // KEY_HEAD
        hidden = w_up.shape[1]
        seq_id = lax.axis_index("seq")
        fsdp_id = lax.axis_index("fsdp")
        y, c = seq_id // 2, seq_id % 2
        x = fsdp_id % 2
        same = x == c
        both = range(micro)

        last = []

        def hold(value):
            return after(value, *last)

        def mark(value):
            last[:] = [value]
            return value

        def settle(value, moved):
            return mark(jnp.where(same, value, hold(moved).astype(value.dtype)))

        def rows(value, b):
            return value[b * piece : (b + 1) * piece]

        def await_(*values):
            waited = lax.optimization_barrier((*values, *last))[: len(values)]
            last[:] = [waited[0]]
            return list(waited)

        def pair(block, moved):
            return mark(jnp.concatenate([block, hold(moved)], axis=0))

        def reduce_second(b, kept, got):
            got = hold(got)
            sent = (kept[piece:] + got[piece:].astype(F32)).astype(BF)
            return kept[:piece] + got[:piece].astype(F32), grid.first(b, mark(sent))

        line_qk = grid.gather_line(mark(jnp.concatenate([w_query, w_key], axis=1)))
        w_vgo = mark(jnp.concatenate([hold(w_value), w_gate, w_out.T], axis=1))
        vgo_moved = grid.swap(w_vgo)
        toks = tokens.reshape(own, width)
        toks_moved = grid.swap(toks)
        segs = segments.reshape(micro, length).astype(F32)
        segs_moved = grid.swap(segs)
        ud_cot = mark(
            jnp.concatenate(
                [jnp.concatenate([w_up, hold(w_down).T], axis=1), d_output.reshape(own, width)],
                axis=0,
            )
        )

        ranks = [
            [2 * (y ^ i) + (x ^ j) for i, j in ((0, 0), (1, 0), (0, 1), (1, 1))],
            [2 * (y ^ i) + (x ^ j) for i, j in ((0, 0), (0, 1), (1, 0), (1, 1))],
        ]
        positions = jnp.stack(
            [jnp.concatenate([r * piece + jnp.arange(piece) for r in ranks[b]]) for b in both]
        ).astype(F32)
        frequency = jnp.exp(-jnp.log(10000.0) * 2.0 * jnp.arange(ROT, dtype=F32) / KEY_HEAD)
        angles = hold(positions).reshape(-1, 1) * frequency[None, :]
        cos_table, sin_table = jnp.cos(angles), jnp.sin(angles)
        mark(cos_table)
        head_ids = (y * 2 + x) * heads + jnp.arange(heads, dtype=jnp.int32)
        log_gamma = jnp.log1p(-jnp.exp2(-5.0 - head_ids.astype(F32)))
        gain_in, gain_mid = norm_gains[0], norm_gains[1]

        w_vgo = settle(w_vgo, vgo_moved)
        full_vg = grid.gather_weight(w_vgo[:, : 2 * dv])
        full_o = grid.gather_weight(w_vgo[:, 2 * dv :])
        toks = settle(toks, toks_moved)
        xin = toks.astype(F32)
        normed, scaled_in, inverse_in = layer_norm_parts(xin, gain_in)
        normed = mark(normed.astype(BF))
        h1_own = [rows(normed, b) for b in both]
        h1_first = [grid.first(b, h1_own[b]) for b in both]
        line_qk = await_(line_qk)[0]
        qk_moved = grid.swap(line_qk)
        segs = settle(segs, segs_moved)
        seg_rows = jnp.stack(
            [
                jnp.concatenate(
                    [lax.dynamic_slice_in_dim(segs[b], r * piece, piece) for r in ranks[b]]
                )
                for b in both
            ]
        )
        lanes = jnp.arange(128)[None, :]
        col_info = jnp.where(
            lanes == 0,
            positions.reshape(-1, 1),
            jnp.where(lanes == 1, seg_rows.reshape(-1, 1), 0.0),
        )
        row_info = jnp.stack([positions, seg_rows] + [jnp.zeros_like(positions)] * 6, axis=1)
        row_info = mark(row_info.reshape(8 * micro, length))
        h1_second = [grid.second(b, pair(h1_own[b], h1_first[b])) for b in both]
        ud_cot_moved = grid.swap(after(ud_cot, line_qk))
        h1_second = await_(*h1_second)
        line_qk = settle(line_qk, qk_moved)
        line_other = grid.flip_c(line_qk)
        even, odd = [v.reshape(grid.nz, 1, -1, 2 * dk) for v in (line_qk, hold(line_other))]
        full_qk = jnp.where(
            c == 0,
            jnp.concatenate([even, odd], axis=1),
            jnp.concatenate([odd, even], axis=1),
        ).reshape(width, 2 * dk)
        mark(full_qk)
        h1, qk = project_turned(
            [p for b in both for p in (h1_own[b], h1_first[b], h1_second[b])],
            full_qk, cos_table, sin_table,
        )
        mark(qk)
        ud_cot = settle(ud_cot, ud_cot_moved)
        full_u = grid.gather_weight(ud_cot[:-own, :hidden])
        full_d = grid.gather_weight(ud_cot[:-own, hidden:])
        cots = ud_cot[-own:]
        cot_own = [rows(cots, b) for b in both]
        cot_first = [grid.first(b, cot_own[b]) for b in both]
        values, gate = project_plain(hold(h1), hold(full_vg), dv)
        mark(values)
        cot_second = [grid.second(b, pair(cot_own[b], cot_first[b])) for b in both]
        gated = mark(
            retain(qk, hold(values), gate, col_info, row_info, log_gamma, heads, micro)
        )
        halves = [[(b * length + i * 2 * piece, 2 * piece) for b in both] for i in range(2)]

        def exchange_rows(values, weights):
            sent = project_back(values, weights, halves[1], BF)
            mark(sent[0])
            moved = [grid.second(b, sent[b]) for b in both]
            kept = project_back([hold(values[0]), *values[1:]], weights, halves[0], F32)
            mark(kept[0])
            return kept, moved

        kept, moved = exchange_rows([hold(gated)], [(full_o, 0)])
        cot = mark(
            assemble(
                [p for b in both for p in (cot_own[b], cot_first[b])]
                + [hold(cot_second[b]) for b in both]
            )
        )
        sums = [reduce_second(b, kept[b], moved[b]) for b in both]
        x1, mid, scaled_mid, inverse_mid, mid_first = [], [], [], [], []
        for b in both:
            x1.append(rows(xin, b) + (sums[b][0] + hold(sums[b][1]).astype(F32)))
            out, scaled, inverse = layer_norm_parts(x1[b], gain_mid)
            mid.append(mark(out.astype(BF)))
            scaled_mid.append(scaled)
            inverse_mid.append(inverse)
            mid_first.append(grid.first(b, mid[b]))
        mid_second = [grid.second(b, pair(mid[b], mid_first[b])) for b in both]
        h2, act, slope = [], [], []
        for some in ([v for b in both for v in (mid[b], mid_first[b])], mid_second):
            out = feed_up([hold(v) for v in some], full_u, hidden)
            mark(out[1])
            for held, value in zip((h2, act, slope), out):
                held.append(value)

        def grad(left, rights):
            return mark(weight_grad(hold(left), rights))

        def grad_rows(lefts, rights):
            return mark(weight_grad_rows(length, list(zip(lefts, rights))))

        g_down = grid.scatter_grad(
            grad_rows([(hold(cot), 0), (cot, 1)], [(act[0], 0), (act[1], 0)])
        )
        d_up, *sent = feed_back(hold(cot), slope, full_u, full_d)
        mark(d_up)
        moved = [grid.second(b, sent[b]) for b in both]
        quarters = [(0, 2 * piece), (2 * piece, 2 * piece)]
        kept = project_back([hold(d_up)], [(full_u, 0)], quarters, F32)
        mark(kept[0])
        g_up = grad_rows([(hold(h2[0]), 0), (h2[1], 0)], [(d_up, 0), (d_up, 1)])
        sums = [reduce_second(b, kept[b], moved[b]) for b in both]
        g_up = grid.scatter_grad(hold(g_up))
        d_x1, mix_first, gain_mid_grad = [], [], 0.0
        for b in both:
            d_h2 = sums[b][0] + hold(sums[b][1]).astype(F32)
            d_ln, part = layer_norm_back(d_h2, scaled_mid[b], inverse_mid[b], gain_mid)
            gain_mid_grad = gain_mid_grad + part
            d_x1.append(cot_own[b].astype(F32) + d_ln)
            mix_first.append((mark(d_x1[b].astype(BF)),))
            mix_first[b] = mix_first[b] + (grid.first(b, mix_first[b][0]),)
        g_down = await_(g_down)[0]
        mix = [(v, f, grid.second(b, pair(v, f))) for b, (v, f) in enumerate(mix_first)]
        down = [
            project_back([hold(v)], [(full_d, 0)], quarters, dtype)
            for v, dtype in ((act[0], F32), (act[1], BF))
        ]
        last[:] = [down[0][0], down[1][0]]
        d_mix, g_out = weight_grad_pieces(
            [p for b in both for p in mix[b][:2] + (hold(mix[b][2]),)], gated
        )
        g_out = grid.scatter_grad(mark(g_out))
        g_ud = mark(jnp.concatenate([hold(g_up), g_down], axis=1))
        g_ud_moved = grid.swap(g_ud)
        down_moved = [grid.second(b, hold(down[1][b])) for b in both]
        d_v, d_gate, d_q, d_k = retain_back(
            hold(d_mix), gate, qk, values, full_o, col_info, row_info, cos_table, sin_table,
            log_gamma, heads, micro,
        )
        mark(d_v)
        g_vg = grid.scatter_grad(grad(h1, [d_v, d_gate]))
        down = [reduce_second(b, down[0][b], down_moved[b]) for b in both]
        kept, moved = exchange_rows(
            [hold(d_q), d_k, d_v, d_gate],
            [(full_qk, 0), (full_qk, 1), (full_vg, 0), (full_vg, 1)],
        )
        g_qk = grid.scatter_grad(grad(h1, [d_q, d_k]))
        output = mark(
            jnp.concatenate(
                [x1[b] + (down[b][0] + hold(down[b][1]).astype(F32)) for b in both]
            ).astype(BF)
        )
        output_moved = grid.swap(output)
        g_ud = settle(g_ud, g_ud_moved)
        sums = [reduce_second(b, kept[b], moved[b]) for b in both]
        g_out = await_(g_out)[0]
        g_out_moved = grid.swap(g_out)
        output = settle(output, output_moved)
        d_inputs, gain_in_grad = [], 0.0
        for b in both:
            d_h1 = sums[b][0] + hold(sums[b][1]).astype(F32)
            d_ln, part = layer_norm_back(d_h1, rows(scaled_in, b), rows(inverse_in, b), gain_in)
            gain_in_grad = gain_in_grad + part
            d_inputs.append(mark(d_x1[b] + d_ln))
        d_input = jnp.concatenate(d_inputs)
        d_input_moved = grid.swap(hold(d_input))
        g_out = settle(g_out, g_out_moved)
        grad_norms = grid.total(hold(jnp.stack([gain_in_grad, gain_mid_grad])))
        mark(grad_norms)
        d_input = settle(d_input, d_input_moved)
        g_down, g_up, g_out = [
            hold(g).astype(F32) for g in (g_ud[:, hidden:].T, g_ud[:, :hidden], g_out.T)
        ]
        last[:] = [g_down, g_up, g_out]
        g_vg = await_(g_vg)[0]
        g_vg = mark(settle(g_vg, grid.swap(g_vg)).astype(F32))
        g_qk = await_(g_qk)[0]
        g_qk = settle(g_qk, grid.swap(g_qk)).astype(F32)
        whole = (micro, 1, piece, width)
        return (
            output.reshape(whole),
            d_input.reshape(whole),
            grad_norms,
            g_qk[:, :dk],
            g_qk[:, dk:],
            g_vg[:, :dv],
            g_vg[:, dv:],
            g_out,
            g_up,
            g_down,
        )

    return on_device


def solution(mesh):
    grid = Grid(mesh.shape["seq"], mesh.shape["fsdp"])
    rows = P("fsdp", "seq")
    cols = P("seq", "fsdp")
    tok = P(None, "fsdp", "seq", None)
    return jax.shard_map(
        make_on_device(grid),
        mesh=mesh,
        in_specs=(tok, P(), rows, rows, rows, rows, cols, rows, cols, P(None, "fsdp", None), tok),
        out_specs=(tok, tok, P(), rows, rows, rows, rows, cols, rows, cols),
        check_vma=False,
    )
```

```python
import jax
import jax.numpy as jnp
from jax import lax
from jax.experimental import pallas as pl
from jax.experimental.pallas import tpu as pltpu
from jax.sharding import PartitionSpec as P

KEY_HEAD = 256
VAL_HEAD = 512
ROT = KEY_HEAD // 2
eps_norm = 1e-05
eps_group = 1.0
BF = jnp.bfloat16
F32 = jnp.float32
AXES = ("seq", "fsdp")
ANY = pl.BlockSpec(memory_space=pl.ANY)


def nn(left, right):
    return jnp.dot(left, right, preferred_element_type=F32)


def nt(left, right):
    return lax.dot_general(left, right, (((1,), (1,)), ((), ())), preferred_element_type=F32)


def tn(left, right):
    return lax.dot_general(left, right, (((0,), (0,)), ((), ())), preferred_element_type=F32)


def after(value, *first):
    return lax.optimization_barrier((value, *first))[0]


class Grid:
    def __init__(self, n_seq, n_fsdp):
        assert n_seq == 4 and n_fsdp % 2 == 0
        self.n_fsdp, self.nz = n_fsdp, n_fsdp // 2
        self.lines = [[z * 2 + x for z in range(self.nz)] for x in range(2)]
        self.groups = [
            [(y * 2 + c) * n_fsdp + z * 2 + x for z in range(self.nz) for c in range(2)]
            for y in range(2)
            for x in range(2)
        ]

    def send(self, value, move):
        found = []
        for y in range(2):
            for c in range(2):
                for z in range(self.nz):
                    for x in range(2):
                        y2, c2, z2, x2 = move(y, c, z, x)
                        src = (y * 2 + c) * self.n_fsdp + z * 2 + x
                        dst = (y2 * 2 + c2) * self.n_fsdp + z2 * 2 + x2
                        if src != dst:
                            found.append((src, dst))
        return lax.ppermute(value, AXES, found)

    def flip_z(self, value, bit):
        return self.send(value, lambda y, c, z, x: (y, c, z ^ bit, x))

    def flip_c(self, value):
        return self.send(value, lambda y, c, z, x: (y, 1 - c, z, x))

    def flip_y(self, value):
        return self.send(value, lambda y, c, z, x: (1 - y, c, z, x))

    def flip_x(self, value):
        return self.send(value, lambda y, c, z, x: (y, c, z, 1 - x))

    def first(self, b, value):
        return self.flip_y(value) if b == 0 else self.flip_x(value)

    def second(self, b, value):
        return self.flip_x(value) if b == 0 else self.flip_y(value)

    def swap(self, value):
        return self.send(value.astype(BF), lambda y, c, z, x: (y, x, z, c))

    def gather_weight(self, shard):
        return lax.all_gather(shard, AXES, axis=0, tiled=True, axis_index_groups=self.groups)

    def scatter_grad(self, value):
        return lax.psum_scatter(
            value, AXES, scatter_dimension=0, tiled=True, axis_index_groups=self.groups
        )

    def gather_line(self, shard):
        return lax.all_gather(shard, "fsdp", axis=0, tiled=True, axis_index_groups=self.lines)

    def scatter_line(self, value):
        return lax.psum_scatter(
            value, "fsdp", scatter_dimension=0, tiled=True, axis_index_groups=self.lines
        )

    def total(self, value):
        for flip in (self.flip_y, self.flip_c):
            value = value + flip(value)
        if self.nz & (self.nz - 1):
            value = lax.psum(value, "fsdp", axis_index_groups=self.lines)
        else:
            bit = 1
            while bit < self.nz:
                value = value + self.flip_z(value, bit)
                bit *= 2
        return value + self.flip_x(value)


def call(body, grid, ins, outs, shapes, scratch=(), flops=0, moved=0):
    return pl.pallas_call(
        body,
        out_shape=shapes,
        grid=grid,
        in_specs=ins,
        out_specs=outs,
        scratch_shapes=list(scratch),
        cost_estimate=pl.CostEstimate(
            flops=flops, bytes_accessed=moved, transcendentals=0
        ),
        compiler_params=pltpu.CompilerParams(vmem_limit_bytes=63 << 20),
    )


def shape(rows, cols, dtype=BF):
    return jax.ShapeDtypeStruct((rows, cols), dtype)


def spec(rows, cols, index):
    return pl.BlockSpec((rows, cols), index)


def copies_into(pieces, target, sems):
    copies, row = [], 0
    for i, piece in enumerate(pieces):
        rows = piece.shape[0]
        copies.append(pltpu.make_async_copy(piece, target.at[pl.ds(row, rows)], sems.at[i]))
        row += rows
    return copies


def fetch(pieces, target, sems):
    copies = copies_into(pieces, target, sems)
    for copy in copies:
        copy.start()
    for copy in copies:
        copy.wait()


def fetch_and_keep(j, steps, pieces, target, out, sems):
    keep = pltpu.make_async_copy(target, out, sems.at[len(pieces)])

    @pl.when(j == 0)
    def _():
        fetch(pieces, target, sems)
        keep.start()

    return keep


def assemble(pieces):
    n = len(pieces)

    def body(*refs):
        fetch(refs[:n], refs[n], refs[n + 1])

    rows = sum(p.shape[0] for p in pieces)
    cols = pieces[0].shape[1]
    return pl.pallas_call(
        body,
        out_shape=shape(rows, cols),
        in_specs=[ANY] * n,
        scratch_shapes=[pltpu.SemaphoreType.DMA((n,))],
        cost_estimate=pl.CostEstimate(
            flops=0, bytes_accessed=4 * rows * cols, transcendentals=0
        ),
    )(*pieces)


def rotated(first, second, cos_part, sin_part):
    return (first * cos_part - second * sin_part, second * cos_part + first * sin_part)


def project_turned(pieces, weight, cos_table, sin_table):
    n = len(pieces)
    rows = sum(p.shape[0] for p in pieces)
    width = pieces[0].shape[1]
    cols = weight.shape[1]
    tile, chunk = 512, 512
    steps = cols // tile

    def body(*refs):
        w_ref, cos_ref, sin_ref, out_ref, o_ref, h_ref, sems = refs[n:]
        j = pl.program_id(0)
        keep = fetch_and_keep(j, steps, refs[:n], h_ref, out_ref, sems)

        def step(i, _):
            at = pl.ds(pl.multiple_of(i * chunk, chunk), chunk)
            acc = nn(h_ref[at, :], w_ref[...])
            for s in range(0, tile, KEY_HEAD):
                u, v = rotated(
                    acc[:, s : s + ROT],
                    acc[:, s + ROT : s + KEY_HEAD],
                    cos_ref[at, :],
                    sin_ref[at, :],
                )
                o_ref[at, s : s + ROT] = u.astype(BF)
                o_ref[at, s + ROT : s + KEY_HEAD] = v.astype(BF)
            return 0

        lax.fori_loop(0, rows // chunk, step, 0, unroll=True)

        @pl.when(j == steps - 1)
        def _():
            keep.wait()

    return call(
        body,
        (steps,),
        [ANY] * n
        + [spec(width, tile, lambda j: (0, j))]
        + [spec(rows, ROT, lambda j: (0, 0))] * 2,
        [ANY, spec(rows, tile, lambda j: (0, j))],
        [shape(rows, width), shape(rows, cols)],
        [pltpu.VMEM((rows, width), BF), pltpu.SemaphoreType.DMA((n + 1,))],
        2 * rows * width * cols,
        2 * (2 * rows * width + width * cols + rows * cols),
    )(*pieces, weight, cos_table, sin_table)


def project_plain(h1, weight, gate_cols):
    rows, width = h1.shape
    cols = weight.shape[1]
    tile, chunk = 512, 512
    first = (cols - gate_cols) // tile

    def body(h_ref, w_ref, v_ref, gate_ref):
        j = pl.program_id(0)

        def step(i, _):
            at = pl.ds(pl.multiple_of(i * chunk, chunk), chunk)
            acc = nn(h_ref[at, :], w_ref[...])

            @pl.when(j < first)
            def _():
                v_ref[at, :] = acc.astype(BF)

            @pl.when(j >= first)
            def _():
                gate_ref[at, :] = acc

            return 0

        lax.fori_loop(0, rows // chunk, step, 0, unroll=True)

    return call(
        body,
        (cols // tile,),
        [spec(rows, width, lambda j: (0, 0)), spec(width, tile, lambda j: (0, j))],
        [
            spec(rows, tile, lambda j: (0, jnp.minimum(j, first - 1))),
            spec(rows, tile, lambda j: (0, jnp.maximum(j - first, 0))),
        ],
        [shape(rows, cols - gate_cols), shape(rows, gate_cols, F32)],
        (),
        2 * rows * width * cols,
        2 * (rows * width + width * cols + 2 * rows * cols),
    )(h1, weight)


def decay_chunk(col_ref, row_ref, at, log_gamma):
    pos_n, seg_n = col_ref[at, 0:1], col_ref[at, 1:2]
    pos_m, seg_m = row_ref[0:1, :], row_ref[1:2, :]
    distance = pos_n - pos_m
    allowed = (distance >= 0.0) & (seg_n == seg_m)
    value = jnp.exp(jnp.maximum(distance, 0.0) * log_gamma) * (KEY_HEAD**-0.5)
    return jnp.where(allowed, value, 0.0)


def sigmoid(value):
    return 1.0 / (1.0 + jnp.exp(-value))


def retain(qk, values, gate, col_info, row_info, log_gamma, heads, micro):
    rows = qk.shape[0] // micro
    dv = heads * VAL_HEAD
    chunk = 512

    def body(q_ref, k_ref, v_ref, gate_ref, col_ref, row_ref, lg_ref, gated_ref):
        log_g = lg_ref[pl.program_id(1)]

        def step(i, _):
            at = pl.ds(pl.multiple_of(i * chunk, chunk), chunk)
            decay = decay_chunk(col_ref, row_ref, at, log_g)
            weights = (nt(q_ref[at, :], k_ref[...]) * decay).astype(BF)
            kept = nn(weights, v_ref[...])
            scale = lax.rsqrt(jnp.mean(kept * kept, axis=-1, keepdims=True) + eps_group)
            gate = gate_ref[at, :]
            gated_ref[at, :] = (gate * sigmoid(gate) * (kept * scale)).astype(BF)
            return 0

        lax.fori_loop(0, rows // chunk, step, 0, unroll=True)

    return call(
        body,
        (micro, heads),
        [
            spec(rows, KEY_HEAD, lambda b, h: (b, h)),
            spec(rows, KEY_HEAD, lambda b, h: (b, heads + h)),
            spec(rows, VAL_HEAD, lambda b, h: (b, h)),
            spec(rows, VAL_HEAD, lambda b, h: (b, h)),
            spec(rows, 128, lambda b, h: (b, 0)),
            spec(8, rows, lambda b, h: (b, 0)),
            pl.BlockSpec(memory_space=pltpu.SMEM),
        ],
        spec(rows, VAL_HEAD, lambda b, h: (b, h)),
        shape(micro * rows, dv),
        (),
        2 * micro * rows * rows * heads * (KEY_HEAD + VAL_HEAD),
        10 * micro * rows * dv,
    )(qk, qk, values, gate, col_info, row_info, log_gamma)


ROOT_2_PI = 0.7978845608028654


def feed_up(pieces, weight, hidden):
    n = len(pieces)
    rows = sum(p.shape[0] for p in pieces)
    width = pieces[0].shape[1]
    tile, chunk = 512, 512
    steps = hidden // tile

    def body(*refs):
        w_ref, out_ref, act_ref, slope_ref, h_ref, sems = refs[n:]
        j = pl.program_id(0)
        keep = fetch_and_keep(j, steps, refs[:n], h_ref, out_ref, sems)

        def step(i, _):
            at = pl.ds(pl.multiple_of(i * chunk, chunk), chunk)
            up = nn(h_ref[at, :], w_ref[...])
            square = up * up
            bent = jnp.tanh(ROOT_2_PI * (up + 0.044715 * square * up))
            act_ref[at, :] = (0.5 * up * (1.0 + bent)).astype(BF)
            inner = ROOT_2_PI * (1.0 + 3.0 * 0.044715 * square)
            slope = 0.5 * (1.0 + bent) + 0.5 * up * (1.0 - bent * bent) * inner
            slope_ref[at, :] = slope
            return 0

        lax.fori_loop(0, rows // chunk, step, 0, unroll=True)

        @pl.when(j == steps - 1)
        def _():
            keep.wait()

    return call(
        body,
        (steps,),
        [ANY] * n + [spec(width, tile, lambda j: (0, j))],
        [ANY] + [spec(rows, tile, lambda j: (0, j))] * 2,
        [shape(rows, width), shape(rows, hidden), shape(rows, hidden, F32)],
        [pltpu.VMEM((rows, width), BF), pltpu.SemaphoreType.DMA((n + 1,))],
        2 * rows * width * hidden,
        4 * rows * width + 2 * width * hidden + 6 * rows * hidden,
    )(*pieces, weight)


def project_back(values, weights, cuts, dtype):
    n, m = len(values), len(cuts)
    rows = values[0].shape[0]
    width = weights[0][0].shape[0]
    tile = 512
    sizes = [v.shape[1] for v in values]

    def body(*refs):
        acc = 0.0
        for i in range(n):
            some = jnp.concatenate([refs[i][at : at + k, :] for at, k in cuts], axis=0)
            acc = acc + nt(some, refs[n + i][...])
        start = 0
        for out, (_, k) in zip(refs[2 * n :], cuts):
            out[...] = acc[start : start + k].astype(dtype)
            start += k

    taken = sum(k for _, k in cuts)
    return call(
        body,
        (width // tile,),
        [spec(rows, k, lambda j: (0, 0)) for k in sizes]
        + [spec(tile, k, lambda j, i=i: (j, i)) for k, (_, i) in zip(sizes, weights)],
        [spec(k, tile, lambda j: (0, j)) for _, k in cuts],
        [shape(k, width, dtype) for _, k in cuts],
        (),
        2 * taken * width * sum(sizes),
        2 * (rows + width) * sum(sizes) + 3 * taken * width,
    )(*values, *[w for w, _ in weights])


def feed_back(cot, slopes, w_up, w_down):
    rows, width = cot.shape
    hidden = w_up.shape[1]
    tile = 512
    half = rows // 2
    first, second = hidden // tile, width // tile

    def body(cot_ref, down_ref, up_ref, slope_a, slope_b, dup_ref, sent_0, sent_1, keep_ref):
        j = pl.program_id(0)

        for i in range(first):

            @pl.when(j == i)
            def _(i=i):
                for at, slope_ref in ((0, slope_a), (half, slope_b)):
                    d_act = nn(cot_ref[at : at + half, :], down_ref[...])
                    d_up = (d_act * slope_ref[...]).astype(BF)
                    dup_ref[at : at + half, :] = d_up
                    if at:
                        keep_ref[:, i * tile : (i + 1) * tile] = d_up

        @pl.when(j >= first)
        def _():
            acc = nt(keep_ref[...], up_ref[...]).astype(BF)
            sent_0[...] = acc[: half // 2]
            sent_1[...] = acc[half // 2 :]

    def early(j):
        return jnp.minimum(j, first - 1)

    def late(j):
        return jnp.maximum(j - first, 0)

    return call(
        body,
        (first + second,),
        [
            spec(rows, width, lambda j: (0, 0)),
            spec(width, tile, lambda j: (0, early(j))),
            spec(tile, hidden, lambda j: (late(j), 0)),
            spec(half, tile, lambda j: (0, early(j))),
            spec(half, tile, lambda j: (0, early(j))),
        ],
        [spec(rows, tile, lambda j: (0, early(j)))]
        + [spec(half // 2, tile, lambda j: (0, late(j)))] * 2,
        [shape(rows, hidden), shape(half // 2, width), shape(half // 2, width)],
        [pltpu.VMEM((half, hidden), BF)],
        3 * rows * width * hidden,
        4 * rows * width + 4 * width * hidden + 6 * rows * hidden,
    )(cot, w_down, w_up, *slopes)


def retain_back(d_mix, gate, qk, values, w_out, col_info, row_info, cos_table, sin_table,
                log_gamma, heads, micro):
    rows = d_mix.shape[0] // micro
    width = d_mix.shape[1]
    dk, dv = heads * KEY_HEAD, heads * VAL_HEAD

    def body(mix_ref, wo, gate_ref, q_ref, k_ref, v_ref, col_ref, row_ref, cos_ref,
             sin_ref, lg_ref, dv_ref, dg_ref, dq_ref, dk_ref):
        log_g = lg_ref[pl.program_id(0)]
        d_gated = nn(mix_ref[...], wo[...])
        decay = decay_chunk(col_ref, row_ref, slice(None), log_g)
        weights = (nt(q_ref[...], k_ref[...]) * decay).astype(BF)
        kept = nn(weights, v_ref[...])
        scale = lax.rsqrt(jnp.mean(kept * kept, axis=-1, keepdims=True) + eps_group)
        y_norm = kept * scale
        gate = gate_ref[...]
        sig = sigmoid(gate)
        dg_ref[...] = (d_gated * y_norm * sig * (1.0 + gate * (1.0 - sig))).astype(BF)
        d_y = d_gated * (gate * sig)
        d_ret = (
            scale * (d_y - y_norm * jnp.mean(d_y * y_norm, axis=-1, keepdims=True))
        ).astype(BF)
        d_scores = (nt(d_ret, v_ref[...]) * decay).astype(BF)
        dv_ref[...] = tn(weights, d_ret).astype(BF)
        d_k = tn(d_scores, q_ref[...])
        d_q = nn(d_scores, k_ref[...])
        cos_part, sin_part = cos_ref[...], -sin_ref[...]
        for out, part in ((dq_ref, d_q), (dk_ref, d_k)):
            u, v = rotated(part[:, :ROT], part[:, ROT:], cos_part, sin_part)
            out[:, :ROT] = u.astype(BF)
            out[:, ROT:] = v.astype(BF)

    def per_head(cols, start=0):
        return spec(rows, cols, lambda h, b: (b, start + h))

    def per_row(height, cols):
        return spec(height, cols, lambda h, b: (b, 0))

    total = micro * rows
    return call(
        body,
        (heads, micro),
        [
            per_row(rows, width),
            spec(width, VAL_HEAD, lambda h, b: (0, h)),
            per_head(VAL_HEAD),
            per_head(KEY_HEAD),
            per_head(KEY_HEAD, heads),
            per_head(VAL_HEAD),
            per_row(rows, 128),
            per_row(8, rows),
            per_row(rows, ROT),
            per_row(rows, ROT),
            pl.BlockSpec(memory_space=pltpu.SMEM),
        ],
        [per_head(VAL_HEAD), per_head(VAL_HEAD), per_head(KEY_HEAD), per_head(KEY_HEAD)],
        [shape(total, dv), shape(total, dv), shape(total, dk), shape(total, dk)],
        (),
        2 * total * width * dv + 2 * total * rows * heads * 5 * VAL_HEAD,
        2 * width * dv + 20 * total * dv + 2 * total * width,
    )(
        d_mix, w_out, gate, qk, qk, values, col_info, row_info, cos_table, sin_table, log_gamma
    )


def weight_grad(left, rights):
    rows, width = left.shape
    sizes = [v.shape[1] for v in rights]
    cols = sum(sizes)
    tile = 512

    def body(left_ref, *refs):
        start = 0
        for right, size in zip(refs, sizes):
            refs[-1][:, start : start + size] = tn(left_ref[...], right[...]).astype(BF)
            start += size

    return call(
        body,
        (width // tile,),
        [spec(rows, tile, lambda i: (0, i))] + [spec(rows, k, lambda i: (0, 0)) for k in sizes],
        spec(tile, cols, lambda i: (i, 0)),
        shape(width, cols),
        (),
        2 * rows * width * cols,
        2 * (rows * (width + cols) + width * cols),
    )(left, *rights)


def weight_grad_part(index, left, rights, blocks, received=None):
    rows, width = left.shape
    sizes = [v.shape[1] for v in rights]
    cols, tile = sum(sizes), width // (2 * blocks)
    more = [] if received is None else [received]

    def body(_, left_ref, *refs):
        o_ref = refs[-1]
        start = 0
        for right, size in zip(refs, sizes):
            at = slice(start, start + size)
            acc = tn(left_ref[...], right[...])
            if more:
                acc = acc + refs[-2][:, at].astype(F32)
            o_ref[:, at] = acc.astype(BF)
            start += size

    return pl.pallas_call(
        body,
        out_shape=shape(blocks * tile, cols),
        grid_spec=pltpu.PrefetchScalarGridSpec(
            num_scalar_prefetch=1,
            grid=(blocks,),
            in_specs=[spec(rows, tile, lambda i, at: (0, 2 * i + at[0]))]
            + [spec(rows, k, lambda i, at: (0, 0)) for k in sizes]
            + [spec(tile, cols, lambda i, at: (i, 0)) for _ in more],
            out_specs=spec(tile, cols, lambda i, at: (i, 0)),
        ),
        cost_estimate=pl.CostEstimate(
            flops=rows * width * cols,
            bytes_accessed=2 * rows * (width + cols) + 2 * width * cols,
            transcendentals=0,
        ),
        compiler_params=pltpu.CompilerParams(vmem_limit_bytes=63 << 20),
    )(index, left, *rights, *more)


def weight_grad_rows(rows, pairs):
    n = len(pairs)
    width, cols = pairs[0][0][0].shape[1], pairs[0][1][0].shape[1]
    tile = 512

    def body(*refs):
        acc = tn(refs[0][...], refs[n][...])
        for i in range(1, n):
            acc = acc + tn(refs[i][...], refs[n + i][...])
        refs[-1][...] = acc.astype(BF)

    return call(
        body,
        (width // tile,),
        [spec(rows, tile, lambda i, b=b: (b, i)) for (_, b), _ in pairs]
        + [spec(rows, cols, lambda i, b=b: (b, 0)) for _, (_, b) in pairs],
        spec(tile, cols, lambda i: (i, 0)),
        shape(width, cols),
        (),
        2 * n * rows * width * cols,
        2 * (n * rows * (width + cols) + width * cols),
    )(*[left for (left, _), _ in pairs], *[right for _, (right, _) in pairs])


def weight_grad_pieces(pieces, right):
    n = len(pieces)
    rows, cols = right.shape
    width = pieces[0].shape[1]
    tile = 512
    steps = width // tile

    def body(*refs):
        right_ref, out_ref, o_ref, left_ref, sems = refs[n:]
        j = pl.program_id(0)
        keep = fetch_and_keep(j, steps, refs[:n], left_ref, out_ref, sems)
        at = pl.ds(pl.multiple_of(j * tile, tile), tile)
        o_ref[...] = tn(left_ref[:, at], right_ref[...]).astype(BF)

        @pl.when(j == steps - 1)
        def _():
            keep.wait()

    return call(
        body,
        (steps,),
        [ANY] * n + [spec(rows, cols, lambda i: (0, 0))],
        [ANY, spec(tile, cols, lambda i: (i, 0))],
        [shape(rows, width), shape(width, cols)],
        [pltpu.VMEM((rows, width), BF), pltpu.SemaphoreType.DMA((n + 1,))],
        2 * rows * width * cols,
        2 * (rows * (width + cols) + width * cols),
    )(*pieces, right)


def layer_norm_parts(inputs, gain_row):
    center = inputs - jnp.mean(inputs, axis=-1, keepdims=True)
    inverse = lax.rsqrt(jnp.mean(center * center, axis=-1, keepdims=True) + eps_norm)
    scaled = center * inverse
    return (scaled * gain_row, scaled, inverse)


def layer_norm_back(incoming, scaled, inverse, gain_row):
    upstream = incoming * gain_row
    centered_grad = (
        upstream
        - jnp.mean(upstream, axis=-1, keepdims=True)
        - scaled * jnp.mean(upstream * scaled, axis=-1, keepdims=True)
    )
    return (centered_grad * inverse, jnp.sum(incoming * scaled, axis=0))


def make_on_device(grid):
    def on_device(
        tokens, norm_gains, w_query, w_key, w_value, w_gate, w_out, w_up, w_down, segments, d_output
    ):
        micro, _, piece, width = tokens.shape
        assert micro == 2
        own, length = micro * piece, 4 * piece
        dk, dv = w_query.shape[1], w_value.shape[1]
        heads = dk // KEY_HEAD
        hidden = w_up.shape[1]
        seq_id = lax.axis_index("seq")
        fsdp_id = lax.axis_index("fsdp")
        y, c = seq_id // 2, seq_id % 2
        x = fsdp_id % 2
        same = x == c
        both = range(micro)

        last = []

        def hold(value):
            return after(value, *last)

        def mark(value):
            last[:] = [value]
            return value

        def settle(value, moved):
            return mark(jnp.where(same, value, hold(moved).astype(value.dtype)))

        def rows(value, b):
            return value[b * piece : (b + 1) * piece]

        def await_(*values):
            waited = lax.optimization_barrier((*values, *last))[: len(values)]
            last[:] = [waited[0]]
            return list(waited)

        def pair(block, moved):
            return mark(jnp.concatenate([block, hold(moved)], axis=0))

        def reduce_second(b, kept, got):
            got = hold(got)
            sent = (kept[piece:] + got[piece:].astype(F32)).astype(BF)
            return kept[:piece] + got[:piece].astype(F32), grid.first(b, mark(sent))

        line_qk = grid.gather_line(mark(jnp.concatenate([w_query, w_key], axis=1)))
        w_vgo = mark(jnp.concatenate([hold(w_value), w_gate, w_out.T], axis=1))
        vgo_moved = grid.swap(w_vgo)
        toks = tokens.reshape(own, width)
        toks_moved = grid.swap(toks)
        segs = segments.reshape(micro, length).astype(F32)
        segs_moved = grid.swap(segs)
        ud_cot = mark(
            jnp.concatenate(
                [jnp.concatenate([w_up, hold(w_down).T], axis=1), d_output.reshape(own, width)],
                axis=0,
            )
        )

        ranks = [
            [2 * (y ^ i) + (x ^ j) for i, j in ((0, 0), (1, 0), (0, 1), (1, 1))],
            [2 * (y ^ i) + (x ^ j) for i, j in ((0, 0), (0, 1), (1, 0), (1, 1))],
        ]
        positions = jnp.stack(
            [jnp.concatenate([r * piece + jnp.arange(piece) for r in ranks[b]]) for b in both]
        ).astype(F32)
        frequency = jnp.exp(-jnp.log(10000.0) * 2.0 * jnp.arange(ROT, dtype=F32) / KEY_HEAD)
        angles = hold(positions).reshape(-1, 1) * frequency[None, :]
        cos_table, sin_table = jnp.cos(angles), jnp.sin(angles)
        mark(cos_table)
        head_ids = (y * 2 + x) * heads + jnp.arange(heads, dtype=jnp.int32)
        log_gamma = jnp.log1p(-jnp.exp2(-5.0 - head_ids.astype(F32)))
        gain_in, gain_mid = norm_gains[0], norm_gains[1]

        w_vgo = settle(w_vgo, vgo_moved)
        full_vg = grid.gather_weight(w_vgo[:, : 2 * dv])
        full_o = grid.gather_weight(w_vgo[:, 2 * dv :])
        toks = settle(toks, toks_moved)
        xin = toks.astype(F32)
        normed, scaled_in, inverse_in = layer_norm_parts(xin, gain_in)
        normed = mark(normed.astype(BF))
        h1_own = [rows(normed, b) for b in both]
        h1_first = [grid.first(b, h1_own[b]) for b in both]
        line_qk = await_(line_qk)[0]
        qk_moved = grid.swap(line_qk)
        segs = settle(segs, segs_moved)
        seg_rows = jnp.stack(
            [
                jnp.concatenate(
                    [lax.dynamic_slice_in_dim(segs[b], r * piece, piece) for r in ranks[b]]
                )
                for b in both
            ]
        )
        lanes = jnp.arange(128)[None, :]
        col_info = jnp.where(
            lanes == 0,
            positions.reshape(-1, 1),
            jnp.where(lanes == 1, seg_rows.reshape(-1, 1), 0.0),
        )
        row_info = jnp.stack([positions, seg_rows] + [jnp.zeros_like(positions)] * 6, axis=1)
        row_info = mark(row_info.reshape(8 * micro, length))
        h1_second = [grid.second(b, pair(h1_own[b], h1_first[b])) for b in both]
        ud_cot_moved = grid.swap(after(ud_cot, line_qk))
        h1_second = await_(*h1_second)
        line_qk = settle(line_qk, qk_moved)
        line_other = grid.flip_c(line_qk)
        even, odd = [v.reshape(grid.nz, 1, -1, 2 * dk) for v in (line_qk, hold(line_other))]
        full_qk = jnp.where(
            c == 0,
            jnp.concatenate([even, odd], axis=1),
            jnp.concatenate([odd, even], axis=1),
        ).reshape(width, 2 * dk)
        mark(full_qk)
        h1, qk = project_turned(
            [p for b in both for p in (h1_own[b], h1_first[b], h1_second[b])],
            full_qk, cos_table, sin_table,
        )
        mark(qk)
        ud_cot = settle(ud_cot, ud_cot_moved)
        full_u = grid.gather_weight(ud_cot[:-own, :hidden])
        full_d = grid.gather_weight(ud_cot[:-own, hidden:])
        cots = ud_cot[-own:]
        cot_own = [rows(cots, b) for b in both]
        cot_first = [grid.first(b, cot_own[b]) for b in both]
        values, gate = project_plain(hold(h1), hold(full_vg), dv)
        mark(values)
        cot_second = [grid.second(b, pair(cot_own[b], cot_first[b])) for b in both]
        gated = mark(
            retain(qk, hold(values), gate, col_info, row_info, log_gamma, heads, micro)
        )
        halves = [[(b * length + i * 2 * piece, 2 * piece) for b in both] for i in range(2)]

        def exchange_rows(values, weights):
            sent = project_back(values, weights, halves[1], BF)
            mark(sent[0])
            moved = [grid.second(b, sent[b]) for b in both]
            kept = project_back([hold(values[0]), *values[1:]], weights, halves[0], F32)
            mark(kept[0])
            return kept, moved

        kept, moved = exchange_rows([hold(gated)], [(full_o, 0)])
        cot = mark(
            assemble(
                [p for b in both for p in (cot_own[b], cot_first[b])]
                + [hold(cot_second[b]) for b in both]
            )
        )
        sums = [reduce_second(b, kept[b], moved[b]) for b in both]
        x1, mid, scaled_mid, inverse_mid, mid_first = [], [], [], [], []
        for b in both:
            x1.append(rows(xin, b) + (sums[b][0] + hold(sums[b][1]).astype(F32)))
            out, scaled, inverse = layer_norm_parts(x1[b], gain_mid)
            mid.append(mark(out.astype(BF)))
            scaled_mid.append(scaled)
            inverse_mid.append(inverse)
            mid_first.append(grid.first(b, mid[b]))
        mid_second = [grid.second(b, pair(mid[b], mid_first[b])) for b in both]
        h2, act, slope = [], [], []
        for some in ([v for b in both for v in (mid[b], mid_first[b])], mid_second):
            out = feed_up([hold(v) for v in some], full_u, hidden)
            mark(out[1])
            for held, value in zip((h2, act, slope), out):
                held.append(value)

        def grad(left, rights):
            return mark(weight_grad(hold(left), rights))

        def grad_rows(lefts, rights):
            return mark(weight_grad_rows(length, list(zip(lefts, rights))))

        g_down = grid.scatter_grad(
            grad_rows([(hold(cot), 0), (cot, 1)], [(act[0], 0), (act[1], 0)])
        )
        d_up, *sent = feed_back(hold(cot), slope, full_u, full_d)
        mark(d_up)
        moved = [grid.second(b, sent[b]) for b in both]
        quarters = [(0, 2 * piece), (2 * piece, 2 * piece)]
        kept = project_back([hold(d_up)], [(full_u, 0)], quarters, F32)
        mark(kept[0])
        g_up = grad_rows([(hold(h2[0]), 0), (h2[1], 0)], [(d_up, 0), (d_up, 1)])
        sums = [reduce_second(b, kept[b], moved[b]) for b in both]
        g_up = grid.scatter_grad(hold(g_up))
        d_x1, mix_first, gain_mid_grad = [], [], 0.0
        for b in both:
            d_h2 = sums[b][0] + hold(sums[b][1]).astype(F32)
            d_ln, part = layer_norm_back(d_h2, scaled_mid[b], inverse_mid[b], gain_mid)
            gain_mid_grad = gain_mid_grad + part
            d_x1.append(cot_own[b].astype(F32) + d_ln)
            mix_first.append((mark(d_x1[b].astype(BF)),))
            mix_first[b] = mix_first[b] + (grid.first(b, mix_first[b][0]),)
        g_down = await_(g_down)[0]
        mix = [(v, f, grid.second(b, pair(v, f))) for b, (v, f) in enumerate(mix_first)]
        down = [
            project_back([hold(v)], [(full_d, 0)], quarters, dtype)
            for v, dtype in ((act[0], F32), (act[1], BF))
        ]
        last[:] = [down[0][0], down[1][0]]
        d_mix, g_out = weight_grad_pieces(
            [p for b in both for p in mix[b][:2] + (hold(mix[b][2]),)], gated
        )
        g_out = grid.scatter_grad(mark(g_out))
        g_ud = mark(jnp.concatenate([hold(g_up), g_down], axis=1))
        down_moved = [grid.second(b, hold(down[1][b])) for b in both]
        d_v, d_gate, d_q, d_k = retain_back(
            hold(d_mix), gate, qk, values, full_o, col_info, row_info, cos_table, sin_table,
            log_gamma, heads, micro,
        )
        mark(d_v)
        def line_part(index, left, rights, received=None):
            if width // grid.n_fsdp % 128 == 0:
                index = index.astype(jnp.int32).reshape(1)
                return weight_grad_part(index, left, rights, grid.nz, received)
            value = weight_grad(left, rights)
            value = value.reshape(grid.nz, 2, -1, value.shape[-1])
            value = lax.dynamic_index_in_dim(value, index, 1, False)
            value = value.reshape(-1, value.shape[-1]).astype(F32)
            return (value if received is None else value + received.astype(F32)).astype(BF)

        def line_start(rights):
            return grid.flip_c(mark(line_part(1 - c, hold(h1), rights)))

        def line_finish(rights, moved):
            return grid.scatter_line(mark(line_part(c, h1, rights, hold(moved))))

        down_moved = await_(*down_moved)
        vg_moved = line_start([d_v, d_gate])
        down = [reduce_second(b, down[0][b], down_moved[b]) for b in both]
        g_ud_moved = grid.swap(hold(g_ud))
        g_vg = line_finish([d_v, d_gate], vg_moved)
        back = [d_q, d_k, d_v, d_gate]
        back_weights = [(full_qk, 0), (full_qk, 1), (full_vg, 0), (full_vg, 1)]
        sent = project_back([hold(back[0]), *back[1:]], back_weights, halves[1], BF)
        mark(sent[0])
        g_ud_moved = await_(g_ud_moved)[0]
        moved = [grid.second(b, hold(sent[b])) for b in both]
        kept = project_back([hold(back[0]), *back[1:]], back_weights, halves[0], F32)
        mark(kept[0])
        *moved, g_out = await_(*moved, g_out)
        qk_moved = line_start([d_q, d_k])
        sums = [reduce_second(b, kept[b], moved[b]) for b in both]
        g_qk = line_finish([d_q, d_k], qk_moved)
        output = mark(
            jnp.concatenate(
                [x1[b] + (down[b][0] + hold(down[b][1]).astype(F32)) for b in both]
            ).astype(BF)
        )
        output_moved = grid.swap(output)
        d_inputs, gain_in_grad = [], 0.0
        for b in both:
            d_h1 = sums[b][0] + hold(sums[b][1]).astype(F32)
            d_ln, part_grad = layer_norm_back(
                d_h1, rows(scaled_in, b), rows(inverse_in, b), gain_in
            )
            gain_in_grad = gain_in_grad + part_grad
            d_inputs.append(mark(d_x1[b] + d_ln))
        d_input = jnp.concatenate(d_inputs)
        d_input_moved = grid.swap(hold(d_input))
        g_vg = await_(g_vg)[0]
        vg_moved = grid.swap(g_vg)
        output = settle(output, output_moved)
        grad_norms = grid.total(hold(jnp.stack([gain_in_grad, gain_mid_grad])))
        mark(grad_norms)
        g_out_moved = grid.swap(hold(g_out))
        g_ud = settle(g_ud, g_ud_moved)
        d_input = settle(d_input, d_input_moved)
        g_out = settle(g_out, g_out_moved)
        g_down, g_up, g_out = [
            hold(g).astype(F32) for g in (g_ud[:, hidden:].T, g_ud[:, :hidden], g_out.T)
        ]
        last[:] = [g_down, g_up, g_out]
        g_vg = mark(settle(g_vg, vg_moved).astype(F32))
        g_qk = await_(g_qk)[0]
        g_qk = settle(g_qk, grid.swap(g_qk)).astype(F32)
        whole = (micro, 1, piece, width)
        return (
            output.reshape(whole),
            d_input.reshape(whole),
            grad_norms,
            g_qk[:, :dk],
            g_qk[:, dk:],
            g_vg[:, :dv],
            g_vg[:, dv:],
            g_out,
            g_up,
            g_down,
        )

    return on_device


def solution(mesh):
    grid = Grid(mesh.shape["seq"], mesh.shape["fsdp"])
    rows = P("fsdp", "seq")
    cols = P("seq", "fsdp")
    tok = P(None, "fsdp", "seq", None)
    return jax.shard_map(
        make_on_device(grid),
        mesh=mesh,
        in_specs=(tok, P(), rows, rows, rows, rows, cols, rows, cols, P(None, "fsdp", None), tok),
        out_specs=(tok, tok, P(), rows, rows, rows, rows, cols, rows, cols),
        check_vma=False,
    )
```

```python
import jax
import jax.numpy as jnp
from jax import lax
from jax.experimental import pallas as pl
from jax.experimental.pallas import tpu as pltpu
from jax.sharding import PartitionSpec as P

KEY_HEAD = 256
VAL_HEAD = 512
ROT = KEY_HEAD // 2
eps_norm = 1e-05
eps_group = 1.0
BF = jnp.bfloat16
F32 = jnp.float32
AXES = ("seq", "fsdp")
ANY = pl.BlockSpec(memory_space=pl.ANY)


def nn(left, right):
    return jnp.dot(left, right, preferred_element_type=F32)


def nt(left, right):
    return lax.dot_general(left, right, (((1,), (1,)), ((), ())), preferred_element_type=F32)


def tn(left, right):
    return lax.dot_general(left, right, (((0,), (0,)), ((), ())), preferred_element_type=F32)


def after(value, *first):
    return lax.optimization_barrier((value, *first))[0]


class Grid:
    def __init__(self, n_seq, n_fsdp):
        assert n_seq == 4 and n_fsdp % 2 == 0
        self.n_fsdp, self.nz = n_fsdp, n_fsdp // 2
        self.lines = [[z * 2 + x for z in range(self.nz)] for x in range(2)]
        self.groups = [
            [(y * 2 + c) * n_fsdp + z * 2 + x for z in range(self.nz) for c in range(2)]
            for y in range(2)
            for x in range(2)
        ]

    def send(self, value, move):
        found = []
        for y in range(2):
            for c in range(2):
                for z in range(self.nz):
                    for x in range(2):
                        y2, c2, z2, x2 = move(y, c, z, x)
                        src = (y * 2 + c) * self.n_fsdp + z * 2 + x
                        dst = (y2 * 2 + c2) * self.n_fsdp + z2 * 2 + x2
                        if src != dst:
                            found.append((src, dst))
        return lax.ppermute(value, AXES, found)

    def flip_z(self, value, bit):
        return self.send(value, lambda y, c, z, x: (y, c, z ^ bit, x))

    def flip_c(self, value):
        return self.send(value, lambda y, c, z, x: (y, 1 - c, z, x))

    def flip_y(self, value):
        return self.send(value, lambda y, c, z, x: (1 - y, c, z, x))

    def flip_x(self, value):
        return self.send(value, lambda y, c, z, x: (y, c, z, 1 - x))

    def first(self, b, value):
        return self.flip_y(value) if b == 0 else self.flip_x(value)

    def second(self, b, value):
        return self.flip_x(value) if b == 0 else self.flip_y(value)

    def swap(self, value):
        return self.send(value.astype(BF), lambda y, c, z, x: (y, x, z, c))

    def gather_weight(self, shard):
        return lax.all_gather(shard, AXES, axis=0, tiled=True, axis_index_groups=self.groups)

    def scatter_grad(self, value):
        return lax.psum_scatter(
            value, AXES, scatter_dimension=0, tiled=True, axis_index_groups=self.groups
        )

    def gather_line(self, shard):
        return lax.all_gather(shard, "fsdp", axis=0, tiled=True, axis_index_groups=self.lines)

    def scatter_line(self, value):
        return lax.psum_scatter(
            value, "fsdp", scatter_dimension=0, tiled=True, axis_index_groups=self.lines
        )

    def total_but_x(self, value):
        for flip in (self.flip_y, self.flip_c):
            value = value + flip(value)
        if self.nz & (self.nz - 1):
            value = lax.psum(value, "fsdp", axis_index_groups=self.lines)
        else:
            bit = 1
            while bit < self.nz:
                value = value + self.flip_z(value, bit)
                bit *= 2
        return value


def call(body, grid, ins, outs, shapes, scratch=(), flops=0, moved=0):
    return pl.pallas_call(
        body,
        out_shape=shapes,
        grid=grid,
        in_specs=ins,
        out_specs=outs,
        scratch_shapes=list(scratch),
        cost_estimate=pl.CostEstimate(
            flops=flops, bytes_accessed=moved, transcendentals=0
        ),
        compiler_params=pltpu.CompilerParams(vmem_limit_bytes=63 << 20),
    )


def shape(rows, cols, dtype=BF):
    return jax.ShapeDtypeStruct((rows, cols), dtype)


def spec(rows, cols, index):
    return pl.BlockSpec((rows, cols), index)


def copies_into(pieces, target, sems):
    copies, row = [], 0
    for i, piece in enumerate(pieces):
        rows = piece.shape[0]
        copies.append(pltpu.make_async_copy(piece, target.at[pl.ds(row, rows)], sems.at[i]))
        row += rows
    return copies


def fetch(pieces, target, sems):
    copies = copies_into(pieces, target, sems)
    for copy in copies:
        copy.start()
    for copy in copies:
        copy.wait()


def fetch_and_keep(j, steps, pieces, target, out, sems):
    keep = pltpu.make_async_copy(target, out, sems.at[len(pieces)])

    @pl.when(j == 0)
    def _():
        fetch(pieces, target, sems)
        keep.start()

    return keep


def assemble(pieces):
    n = len(pieces)

    def body(*refs):
        fetch(refs[:n], refs[n], refs[n + 1])

    rows = sum(p.shape[0] for p in pieces)
    cols = pieces[0].shape[1]
    return pl.pallas_call(
        body,
        out_shape=shape(rows, cols),
        in_specs=[ANY] * n,
        scratch_shapes=[pltpu.SemaphoreType.DMA((n,))],
        cost_estimate=pl.CostEstimate(
            flops=0, bytes_accessed=4 * rows * cols, transcendentals=0
        ),
    )(*pieces)


def rotated(first, second, cos_part, sin_part):
    return (first * cos_part - second * sin_part, second * cos_part + first * sin_part)


def project_turned(pieces, weight, cos_table, sin_table):
    n = len(pieces)
    rows = sum(p.shape[0] for p in pieces)
    width = pieces[0].shape[1]
    cols = weight.shape[1]
    tile, chunk = 512, 512
    steps = cols // tile

    def body(*refs):
        w_ref, cos_ref, sin_ref, out_ref, o_ref, h_ref, sems = refs[n:]
        j = pl.program_id(0)
        keep = fetch_and_keep(j, steps, refs[:n], h_ref, out_ref, sems)

        def step(i, _):
            at = pl.ds(pl.multiple_of(i * chunk, chunk), chunk)
            acc = nn(h_ref[at, :], w_ref[...])
            for s in range(0, tile, KEY_HEAD):
                u, v = rotated(
                    acc[:, s : s + ROT],
                    acc[:, s + ROT : s + KEY_HEAD],
                    cos_ref[at, :],
                    sin_ref[at, :],
                )
                o_ref[at, s : s + ROT] = u.astype(BF)
                o_ref[at, s + ROT : s + KEY_HEAD] = v.astype(BF)
            return 0

        lax.fori_loop(0, rows // chunk, step, 0, unroll=True)

        @pl.when(j == steps - 1)
        def _():
            keep.wait()

    return call(
        body,
        (steps,),
        [ANY] * n
        + [spec(width, tile, lambda j: (0, j))]
        + [spec(rows, ROT, lambda j: (0, 0))] * 2,
        [ANY, spec(rows, tile, lambda j: (0, j))],
        [shape(rows, width), shape(rows, cols)],
        [pltpu.VMEM((rows, width), BF), pltpu.SemaphoreType.DMA((n + 1,))],
        2 * rows * width * cols,
        2 * (2 * rows * width + width * cols + rows * cols),
    )(*pieces, weight, cos_table, sin_table)


def project_plain(h1, weight, gate_cols):
    rows, width = h1.shape
    cols = weight.shape[1]
    tile, chunk = 512, 512
    first = (cols - gate_cols) // tile

    def body(h_ref, w_ref, v_ref, gate_ref):
        j = pl.program_id(0)

        def step(i, _):
            at = pl.ds(pl.multiple_of(i * chunk, chunk), chunk)
            acc = nn(h_ref[at, :], w_ref[...])

            @pl.when(j < first)
            def _():
                v_ref[at, :] = acc.astype(BF)

            @pl.when(j >= first)
            def _():
                gate_ref[at, :] = acc

            return 0

        lax.fori_loop(0, rows // chunk, step, 0, unroll=True)

    return call(
        body,
        (cols // tile,),
        [spec(rows, width, lambda j: (0, 0)), spec(width, tile, lambda j: (0, j))],
        [
            spec(rows, tile, lambda j: (0, jnp.minimum(j, first - 1))),
            spec(rows, tile, lambda j: (0, jnp.maximum(j - first, 0))),
        ],
        [shape(rows, cols - gate_cols), shape(rows, gate_cols, F32)],
        (),
        2 * rows * width * cols,
        2 * (rows * width + width * cols + 2 * rows * cols),
    )(h1, weight)


def decay_chunk(col_ref, row_ref, at, log_gamma):
    pos_n, seg_n = col_ref[at, 0:1], col_ref[at, 1:2]
    pos_m, seg_m = row_ref[0:1, :], row_ref[1:2, :]
    distance = pos_n - pos_m
    allowed = (distance >= 0.0) & (seg_n == seg_m)
    value = jnp.exp(jnp.maximum(distance, 0.0) * log_gamma) * (KEY_HEAD**-0.5)
    return jnp.where(allowed, value, 0.0)


def sigmoid(value):
    return 1.0 / (1.0 + jnp.exp(-value))


def retain(qk, values, gate, col_info, row_info, log_gamma, heads, micro):
    rows = qk.shape[0] // micro
    dv = heads * VAL_HEAD
    chunk = 512

    def body(q_ref, k_ref, v_ref, gate_ref, col_ref, row_ref, lg_ref, gated_ref):
        log_g = lg_ref[pl.program_id(1)]

        def step(i, _):
            at = pl.ds(pl.multiple_of(i * chunk, chunk), chunk)
            decay = decay_chunk(col_ref, row_ref, at, log_g)
            weights = (nt(q_ref[at, :], k_ref[...]) * decay).astype(BF)
            kept = nn(weights, v_ref[...])
            scale = lax.rsqrt(jnp.mean(kept * kept, axis=-1, keepdims=True) + eps_group)
            gate = gate_ref[at, :]
            gated_ref[at, :] = (gate * sigmoid(gate) * (kept * scale)).astype(BF)
            return 0

        lax.fori_loop(0, rows // chunk, step, 0, unroll=True)

    return call(
        body,
        (micro, heads),
        [
            spec(rows, KEY_HEAD, lambda b, h: (b, h)),
            spec(rows, KEY_HEAD, lambda b, h: (b, heads + h)),
            spec(rows, VAL_HEAD, lambda b, h: (b, h)),
            spec(rows, VAL_HEAD, lambda b, h: (b, h)),
            spec(rows, 128, lambda b, h: (b, 0)),
            spec(8, rows, lambda b, h: (b, 0)),
            pl.BlockSpec(memory_space=pltpu.SMEM),
        ],
        spec(rows, VAL_HEAD, lambda b, h: (b, h)),
        shape(micro * rows, dv),
        (),
        2 * micro * rows * rows * heads * (KEY_HEAD + VAL_HEAD),
        10 * micro * rows * dv,
    )(qk, qk, values, gate, col_info, row_info, log_gamma)


ROOT_2_PI = 0.7978845608028654


def feed_up(pieces, weight, hidden):
    n = len(pieces)
    rows = sum(p.shape[0] for p in pieces)
    width = pieces[0].shape[1]
    tile, chunk = 512, 512
    steps = hidden // tile

    def body(*refs):
        w_ref, out_ref, act_ref, slope_ref, h_ref, sems = refs[n:]
        j = pl.program_id(0)
        keep = fetch_and_keep(j, steps, refs[:n], h_ref, out_ref, sems)

        def step(i, _):
            at = pl.ds(pl.multiple_of(i * chunk, chunk), chunk)
            up = nn(h_ref[at, :], w_ref[...])
            square = up * up
            bent = jnp.tanh(ROOT_2_PI * (up + 0.044715 * square * up))
            act_ref[at, :] = (0.5 * up * (1.0 + bent)).astype(BF)
            inner = ROOT_2_PI * (1.0 + 3.0 * 0.044715 * square)
            slope = 0.5 * (1.0 + bent) + 0.5 * up * (1.0 - bent * bent) * inner
            slope_ref[at, :] = slope
            return 0

        lax.fori_loop(0, rows // chunk, step, 0, unroll=True)

        @pl.when(j == steps - 1)
        def _():
            keep.wait()

    return call(
        body,
        (steps,),
        [ANY] * n + [spec(width, tile, lambda j: (0, j))],
        [ANY] + [spec(rows, tile, lambda j: (0, j))] * 2,
        [shape(rows, width), shape(rows, hidden), shape(rows, hidden, F32)],
        [pltpu.VMEM((rows, width), BF), pltpu.SemaphoreType.DMA((n + 1,))],
        2 * rows * width * hidden,
        4 * rows * width + 2 * width * hidden + 6 * rows * hidden,
    )(*pieces, weight)


def project_back(values, weights, cuts, dtype):
    n, m = len(values), len(cuts)
    rows = values[0].shape[0]
    width = weights[0][0].shape[0]
    tile = 512
    sizes = [v.shape[1] for v in values]

    def body(*refs):
        acc = 0.0
        for i in range(n):
            some = jnp.concatenate([refs[i][at : at + k, :] for at, k in cuts], axis=0)
            acc = acc + nt(some, refs[n + i][...])
        start = 0
        for out, (_, k) in zip(refs[2 * n :], cuts):
            out[...] = acc[start : start + k].astype(dtype)
            start += k

    taken = sum(k for _, k in cuts)
    return call(
        body,
        (width // tile,),
        [spec(rows, k, lambda j: (0, 0)) for k in sizes]
        + [spec(tile, k, lambda j, i=i: (j, i)) for k, (_, i) in zip(sizes, weights)],
        [spec(k, tile, lambda j: (0, j)) for _, k in cuts],
        [shape(k, width, dtype) for _, k in cuts],
        (),
        2 * taken * width * sum(sizes),
        2 * (rows + width) * sum(sizes) + 3 * taken * width,
    )(*values, *[w for w, _ in weights])


def feed_back(cot, slopes, w_up, w_down):
    rows, width = cot.shape
    hidden = w_up.shape[1]
    tile = 512
    half = rows // 2
    first, second = hidden // tile, width // tile

    def body(cot_ref, down_ref, up_ref, slope_a, slope_b, dup_ref, sent_0, sent_1, keep_ref):
        j = pl.program_id(0)

        for i in range(first):

            @pl.when(j == i)
            def _(i=i):
                for at, slope_ref in ((0, slope_a), (half, slope_b)):
                    d_act = nn(cot_ref[at : at + half, :], down_ref[...])
                    d_up = (d_act * slope_ref[...]).astype(BF)
                    dup_ref[at : at + half, :] = d_up
                    if at:
                        keep_ref[:, i * tile : (i + 1) * tile] = d_up

        @pl.when(j >= first)
        def _():
            acc = nt(keep_ref[...], up_ref[...]).astype(BF)
            sent_0[...] = acc[: half // 2]
            sent_1[...] = acc[half // 2 :]

    def early(j):
        return jnp.minimum(j, first - 1)

    def late(j):
        return jnp.maximum(j - first, 0)

    return call(
        body,
        (first + second,),
        [
            spec(rows, width, lambda j: (0, 0)),
            spec(width, tile, lambda j: (0, early(j))),
            spec(tile, hidden, lambda j: (late(j), 0)),
            spec(half, tile, lambda j: (0, early(j))),
            spec(half, tile, lambda j: (0, early(j))),
        ],
        [spec(rows, tile, lambda j: (0, early(j)))]
        + [spec(half // 2, tile, lambda j: (0, late(j)))] * 2,
        [shape(rows, hidden), shape(half // 2, width), shape(half // 2, width)],
        [pltpu.VMEM((half, hidden), BF)],
        3 * rows * width * hidden,
        4 * rows * width + 4 * width * hidden + 6 * rows * hidden,
    )(cot, w_down, w_up, *slopes)


def retain_back(d_mix, gate, qk, values, w_out, col_info, row_info, cos_table, sin_table,
                log_gamma, heads, micro):
    rows = d_mix.shape[0] // micro
    width = d_mix.shape[1]
    dk, dv = heads * KEY_HEAD, heads * VAL_HEAD

    def body(mix_ref, wo, gate_ref, q_ref, k_ref, v_ref, col_ref, row_ref, cos_ref,
             sin_ref, lg_ref, dv_ref, dg_ref, dq_ref, dk_ref):
        log_g = lg_ref[pl.program_id(0)]
        d_gated = nn(mix_ref[...], wo[...])
        decay = decay_chunk(col_ref, row_ref, slice(None), log_g)
        weights = (nt(q_ref[...], k_ref[...]) * decay).astype(BF)
        kept = nn(weights, v_ref[...])
        scale = lax.rsqrt(jnp.mean(kept * kept, axis=-1, keepdims=True) + eps_group)
        y_norm = kept * scale
        gate = gate_ref[...]
        sig = sigmoid(gate)
        dg_ref[...] = (d_gated * y_norm * sig * (1.0 + gate * (1.0 - sig))).astype(BF)
        d_y = d_gated * (gate * sig)
        d_ret = (
            scale * (d_y - y_norm * jnp.mean(d_y * y_norm, axis=-1, keepdims=True))
        ).astype(BF)
        d_scores = (nt(d_ret, v_ref[...]) * decay).astype(BF)
        dv_ref[...] = tn(weights, d_ret).astype(BF)
        d_k = tn(d_scores, q_ref[...])
        d_q = nn(d_scores, k_ref[...])
        cos_part, sin_part = cos_ref[...], -sin_ref[...]
        for out, part in ((dq_ref, d_q), (dk_ref, d_k)):
            u, v = rotated(part[:, :ROT], part[:, ROT:], cos_part, sin_part)
            out[:, :ROT] = u.astype(BF)
            out[:, ROT:] = v.astype(BF)

    def per_head(cols, start=0):
        return spec(rows, cols, lambda h, b: (b, start + h))

    def per_row(height, cols):
        return spec(height, cols, lambda h, b: (b, 0))

    total = micro * rows
    return call(
        body,
        (heads, micro),
        [
            per_row(rows, width),
            spec(width, VAL_HEAD, lambda h, b: (0, h)),
            per_head(VAL_HEAD),
            per_head(KEY_HEAD),
            per_head(KEY_HEAD, heads),
            per_head(VAL_HEAD),
            per_row(rows, 128),
            per_row(8, rows),
            per_row(rows, ROT),
            per_row(rows, ROT),
            pl.BlockSpec(memory_space=pltpu.SMEM),
        ],
        [per_head(VAL_HEAD), per_head(VAL_HEAD), per_head(KEY_HEAD), per_head(KEY_HEAD)],
        [shape(total, dv), shape(total, dv), shape(total, dk), shape(total, dk)],
        (),
        2 * total * width * dv + 2 * total * rows * heads * 5 * VAL_HEAD,
        2 * width * dv + 20 * total * dv + 2 * total * width,
    )(
        d_mix, w_out, gate, qk, qk, values, col_info, row_info, cos_table, sin_table, log_gamma
    )


def weight_grad(left, rights):
    rows, width = left.shape
    sizes = [v.shape[1] for v in rights]
    cols = sum(sizes)
    tile = 512

    def body(left_ref, *refs):
        start = 0
        for right, size in zip(refs, sizes):
            refs[-1][:, start : start + size] = tn(left_ref[...], right[...]).astype(BF)
            start += size

    return call(
        body,
        (width // tile,),
        [spec(rows, tile, lambda i: (0, i))] + [spec(rows, k, lambda i: (0, 0)) for k in sizes],
        spec(tile, cols, lambda i: (i, 0)),
        shape(width, cols),
        (),
        2 * rows * width * cols,
        2 * (rows * (width + cols) + width * cols),
    )(left, *rights)


def weight_grad_part(index, left, rights, blocks, received=None):
    rows, width = left.shape
    sizes = [v.shape[1] for v in rights]
    cols, tile = sum(sizes), width // (2 * blocks)
    more = [] if received is None else [received]

    def body(_, left_ref, *refs):
        o_ref = refs[-1]
        start = 0
        for right, size in zip(refs, sizes):
            at = slice(start, start + size)
            acc = tn(left_ref[...], right[...])
            if more:
                acc = acc + refs[-2][:, at].astype(F32)
            o_ref[:, at] = acc.astype(BF)
            start += size

    return pl.pallas_call(
        body,
        out_shape=shape(blocks * tile, cols),
        grid_spec=pltpu.PrefetchScalarGridSpec(
            num_scalar_prefetch=1,
            grid=(blocks,),
            in_specs=[spec(rows, tile, lambda i, at: (0, 2 * i + at[0]))]
            + [spec(rows, k, lambda i, at: (0, 0)) for k in sizes]
            + [spec(tile, cols, lambda i, at: (i, 0)) for _ in more],
            out_specs=spec(tile, cols, lambda i, at: (i, 0)),
        ),
        cost_estimate=pl.CostEstimate(
            flops=rows * width * cols,
            bytes_accessed=2 * rows * (width + cols) + 2 * width * cols,
            transcendentals=0,
        ),
        compiler_params=pltpu.CompilerParams(vmem_limit_bytes=63 << 20),
    )(index, left, *rights, *more)


def weight_grad_rows(rows, pairs, earlier=None):
    n = len(pairs)
    width, cols = pairs[0][0][0].shape[1], pairs[0][1][0].shape[1]
    tile = 512
    more = [] if earlier is None else [earlier]

    def body(*refs):
        acc = tn(refs[0][...], refs[n][...])
        for i in range(1, n):
            acc = acc + tn(refs[i][...], refs[n + i][...])
        if more:
            acc = acc + refs[-2][...].astype(F32)
        refs[-1][...] = acc.astype(BF)

    return call(
        body,
        (width // tile,),
        [spec(rows, tile, lambda i, b=b: (b, i)) for (_, b), _ in pairs]
        + [spec(rows, cols, lambda i, b=b: (b, 0)) for _, (_, b) in pairs]
        + [spec(tile, cols, lambda i: (i, 0)) for _ in more],
        spec(tile, cols, lambda i: (i, 0)),
        shape(width, cols),
        (),
        2 * n * rows * width * cols,
        2 * (n * rows * (width + cols) + width * cols),
    )(*[left for (left, _), _ in pairs], *[right for _, (right, _) in pairs], *more)


def weight_grad_pieces(pieces, right):
    n = len(pieces)
    rows, cols = right.shape
    width = pieces[0].shape[1]
    tile = 512
    steps = width // tile

    def body(*refs):
        right_ref, out_ref, o_ref, left_ref, sems = refs[n:]
        j = pl.program_id(0)
        keep = fetch_and_keep(j, steps, refs[:n], left_ref, out_ref, sems)
        at = pl.ds(pl.multiple_of(j * tile, tile), tile)
        o_ref[...] = tn(left_ref[:, at], right_ref[...]).astype(BF)

        @pl.when(j == steps - 1)
        def _():
            keep.wait()

    return call(
        body,
        (steps,),
        [ANY] * n + [spec(rows, cols, lambda i: (0, 0))],
        [ANY, spec(tile, cols, lambda i: (i, 0))],
        [shape(rows, width), shape(width, cols)],
        [pltpu.VMEM((rows, width), BF), pltpu.SemaphoreType.DMA((n + 1,))],
        2 * rows * width * cols,
        2 * (rows * (width + cols) + width * cols),
    )(*pieces, right)


def layer_norm_parts(inputs, gain_row):
    center = inputs - jnp.mean(inputs, axis=-1, keepdims=True)
    inverse = lax.rsqrt(jnp.mean(center * center, axis=-1, keepdims=True) + eps_norm)
    scaled = center * inverse
    return (scaled * gain_row, scaled, inverse)


def layer_norm_back(incoming, scaled, inverse, gain_row):
    upstream = incoming * gain_row
    centered_grad = (
        upstream
        - jnp.mean(upstream, axis=-1, keepdims=True)
        - scaled * jnp.mean(upstream * scaled, axis=-1, keepdims=True)
    )
    return (centered_grad * inverse, jnp.sum(incoming * scaled, axis=0))


def make_on_device(grid):
    def on_device(
        tokens, norm_gains, w_query, w_key, w_value, w_gate, w_out, w_up, w_down, segments, d_output
    ):
        micro, _, piece, width = tokens.shape
        assert micro == 2
        own, length = micro * piece, 4 * piece
        dk, dv = w_query.shape[1], w_value.shape[1]
        heads = dk // KEY_HEAD
        hidden = w_up.shape[1]
        seq_id = lax.axis_index("seq")
        fsdp_id = lax.axis_index("fsdp")
        y, c = seq_id // 2, seq_id % 2
        x = fsdp_id % 2
        same = x == c
        both = range(micro)

        last = []

        def hold(value):
            return after(value, *last)

        def mark(value):
            last[:] = [value]
            return value

        def settle(value, moved):
            return mark(jnp.where(same, value, hold(moved).astype(value.dtype)))

        def rows(value, b):
            return value[b * piece : (b + 1) * piece]

        def await_(*values):
            waited = lax.optimization_barrier((*values, *last))[: len(values)]
            last[:] = [waited[0]]
            return list(waited)

        def pair(block, moved):
            return mark(jnp.concatenate([block, hold(moved)], axis=0))

        def reduce_second(b, kept, got):
            got = hold(got)
            sent = (kept[piece:] + got[piece:].astype(F32)).astype(BF)
            return kept[:piece] + got[:piece].astype(F32), grid.first(b, mark(sent))

        line_qk = grid.gather_line(mark(jnp.concatenate([w_query, w_key], axis=1)))
        w_vgo = mark(jnp.concatenate([hold(w_value), w_gate, w_out.T], axis=1))
        vgo_moved = grid.swap(w_vgo)
        toks = tokens.reshape(own, width)
        toks_moved = grid.swap(toks)
        segs = segments.reshape(micro, length).astype(F32)
        segs_moved = grid.swap(segs)
        w_ud = mark(jnp.concatenate([w_up, hold(w_down).T], axis=1))
        cots = d_output.reshape(own, width)

        ranks = [
            [2 * (y ^ i) + (x ^ j) for i, j in ((0, 0), (1, 0), (0, 1), (1, 1))],
            [2 * (y ^ i) + (x ^ j) for i, j in ((0, 0), (0, 1), (1, 0), (1, 1))],
        ]
        positions = jnp.stack(
            [jnp.concatenate([r * piece + jnp.arange(piece) for r in ranks[b]]) for b in both]
        ).astype(F32)
        frequency = jnp.exp(-jnp.log(10000.0) * 2.0 * jnp.arange(ROT, dtype=F32) / KEY_HEAD)
        angles = hold(positions).reshape(-1, 1) * frequency[None, :]
        cos_table, sin_table = jnp.cos(angles), jnp.sin(angles)
        mark(cos_table)
        head_ids = (y * 2 + x) * heads + jnp.arange(heads, dtype=jnp.int32)
        log_gamma = jnp.log1p(-jnp.exp2(-5.0 - head_ids.astype(F32)))
        gain_in, gain_mid = norm_gains[0], norm_gains[1]

        w_vgo = settle(w_vgo, vgo_moved)
        full_vg = grid.gather_weight(w_vgo[:, : 2 * dv])
        full_o = grid.gather_weight(w_vgo[:, 2 * dv :])
        toks = settle(toks, toks_moved)
        xin = toks.astype(F32)
        normed, scaled_in, inverse_in = layer_norm_parts(xin, gain_in)
        normed = mark(normed.astype(BF))
        h1_own = [rows(normed, b) for b in both]
        h1_first = [grid.first(b, h1_own[b]) for b in both]
        line_qk = await_(line_qk)[0]
        qk_moved = grid.swap(line_qk)
        segs = settle(segs, segs_moved)
        seg_rows = jnp.stack(
            [
                jnp.concatenate(
                    [lax.dynamic_slice_in_dim(segs[b], r * piece, piece) for r in ranks[b]]
                )
                for b in both
            ]
        )
        lanes = jnp.arange(128)[None, :]
        col_info = jnp.where(
            lanes == 0,
            positions.reshape(-1, 1),
            jnp.where(lanes == 1, seg_rows.reshape(-1, 1), 0.0),
        )
        row_info = jnp.stack([positions, seg_rows] + [jnp.zeros_like(positions)] * 6, axis=1)
        row_info = mark(row_info.reshape(8 * micro, length))
        h1_second = [grid.second(b, pair(h1_own[b], h1_first[b])) for b in both]
        cots_moved = grid.swap(after(cots, line_qk))
        ud_moved = grid.swap(after(w_ud, line_qk))
        h1_second = await_(*h1_second)
        line_qk = settle(line_qk, qk_moved)
        line_other = grid.flip_c(line_qk)
        even, odd = [v.reshape(grid.nz, 1, -1, 2 * dk) for v in (line_qk, hold(line_other))]
        full_qk = jnp.where(
            c == 0,
            jnp.concatenate([even, odd], axis=1),
            jnp.concatenate([odd, even], axis=1),
        ).reshape(width, 2 * dk)
        mark(full_qk)
        h1, qk = project_turned(
            [p for b in both for p in (h1_own[b], h1_first[b], h1_second[b])],
            full_qk, cos_table, sin_table,
        )
        mark(qk)
        cots = settle(cots, cots_moved)
        cot_own = [rows(cots, b) for b in both]
        cot_first = [grid.first(b, cot_own[b]) for b in both]
        w_ud = settle(w_ud, ud_moved)
        full_u = grid.gather_weight(w_ud[:, :hidden])
        full_d = grid.gather_weight(w_ud[:, hidden:])
        cot_second = [grid.second(b, pair(cot_own[b], cot_first[b])) for b in both]
        values, gate = project_plain(hold(h1), hold(full_vg), dv)
        mark(values)
        gated = mark(
            retain(qk, hold(values), gate, col_info, row_info, log_gamma, heads, micro)
        )
        halves = [[(b * length + i * 2 * piece, 2 * piece) for b in both] for i in range(2)]

        def exchange_rows(values, weights):
            sent = project_back(values, weights, halves[1], BF)
            mark(sent[0])
            moved = [grid.second(b, sent[b]) for b in both]
            kept = project_back([hold(values[0]), *values[1:]], weights, halves[0], F32)
            mark(kept[0])
            return kept, moved

        kept, moved = exchange_rows([hold(gated)], [(full_o, 0)])
        cot = mark(
            assemble(
                [p for b in both for p in (cot_own[b], cot_first[b])]
                + [hold(cot_second[b]) for b in both]
            )
        )
        sums = [reduce_second(b, kept[b], moved[b]) for b in both]
        x1, mid, scaled_mid, inverse_mid, mid_first = [], [], [], [], []
        for b in both:
            x1.append(rows(xin, b) + (sums[b][0] + hold(sums[b][1]).astype(F32)))
            out, scaled, inverse = layer_norm_parts(x1[b], gain_mid)
            mid.append(mark(out.astype(BF)))
            scaled_mid.append(scaled)
            inverse_mid.append(inverse)
            mid_first.append(grid.first(b, mid[b]))
        mid_second = [grid.second(b, pair(mid[b], mid_first[b])) for b in both]
        h2, act, slope = [], [], []
        g_down = None
        for i, some in enumerate(
            ([v for b in both for v in (mid[b], mid_first[b])], mid_second)
        ):
            out = feed_up([hold(v) for v in some], full_u, hidden)
            mark(out[1])
            for held, value in zip((h2, act, slope), out):
                held.append(value)
            g_down = mark(weight_grad_rows(length, [((hold(cot), i), (act[i], 0))], g_down))

        def grad(left, rights):
            return mark(weight_grad(hold(left), rights))

        def grad_rows(lefts, rights):
            return mark(weight_grad_rows(length, list(zip(lefts, rights))))

        g_down = grid.scatter_grad(g_down)
        d_up, *sent = feed_back(hold(cot), slope, full_u, full_d)
        mark(d_up)
        moved = [grid.second(b, sent[b]) for b in both]
        quarters = [(0, 2 * piece), (2 * piece, 2 * piece)]
        kept = project_back([hold(d_up)], [(full_u, 0)], quarters, F32)
        mark(kept[0])
        g_up = grad_rows([(hold(h2[0]), 0), (h2[1], 0)], [(d_up, 0), (d_up, 1)])
        sums = [reduce_second(b, kept[b], moved[b]) for b in both]
        g_up = grid.scatter_grad(hold(g_up))
        d_x1, mix_first, gain_mid_grad = [], [], 0.0
        for b in both:
            d_h2 = sums[b][0] + hold(sums[b][1]).astype(F32)
            d_ln, part = layer_norm_back(d_h2, scaled_mid[b], inverse_mid[b], gain_mid)
            gain_mid_grad = gain_mid_grad + part
            d_x1.append(cot_own[b].astype(F32) + d_ln)
            mix_first.append((mark(d_x1[b].astype(BF)),))
            mix_first[b] = mix_first[b] + (grid.first(b, mix_first[b][0]),)
        g_down = await_(g_down)[0]
        mix = [(v, f, grid.second(b, pair(v, f))) for b, (v, f) in enumerate(mix_first)]
        down = [
            project_back([hold(v)], [(full_d, 0)], quarters, dtype)
            for v, dtype in ((act[0], F32), (act[1], BF))
        ]
        last[:] = [down[0][0], down[1][0]]
        d_mix, g_out = weight_grad_pieces(
            [p for b in both for p in mix[b][:2] + (hold(mix[b][2]),)], gated
        )
        g_out = grid.scatter_grad(mark(g_out))
        g_up = await_(g_up)[0]
        down_moved = [grid.second(b, hold(down[1][b])) for b in both]
        d_v, d_gate, d_q, d_k = retain_back(
            hold(d_mix), gate, qk, values, full_o, col_info, row_info, cos_table, sin_table,
            log_gamma, heads, micro,
        )
        mark(d_v)
        def line_part(index, left, rights, received=None):
            if width // grid.n_fsdp % 128 == 0:
                index = index.astype(jnp.int32).reshape(1)
                return weight_grad_part(index, left, rights, grid.nz, received)
            value = weight_grad(left, rights)
            value = value.reshape(grid.nz, 2, -1, value.shape[-1])
            value = lax.dynamic_index_in_dim(value, index, 1, False)
            value = value.reshape(-1, value.shape[-1]).astype(F32)
            return (value if received is None else value + received.astype(F32)).astype(BF)

        def line_start(rights):
            return grid.flip_c(mark(line_part(1 - c, hold(h1), rights)))

        def line_finish(rights, moved):
            return grid.scatter_line(mark(line_part(c, h1, rights, hold(moved))))

        down_moved = await_(*down_moved)
        vg_moved = line_start([d_v, d_gate])
        down = [reduce_second(b, down[0][b], down_moved[b]) for b in both]
        g_vg = line_finish([d_v, d_gate], vg_moved)
        g_ud = mark(jnp.concatenate([hold(g_up), g_down], axis=1))
        g_ud_moved = grid.swap(g_ud)
        back = [d_q, d_k, d_v, d_gate]
        back_weights = [(full_qk, 0), (full_qk, 1), (full_vg, 0), (full_vg, 1)]
        sent = project_back([hold(back[0]), *back[1:]], back_weights, halves[1], BF)
        mark(sent[0])
        g_ud_moved = await_(g_ud_moved)[0]
        moved = [grid.second(b, hold(sent[b])) for b in both]
        kept = project_back([hold(back[0]), *back[1:]], back_weights, halves[0], F32)
        mark(kept[0])
        *moved, g_out = await_(*moved, g_out)
        qk_moved = line_start([d_q, d_k])
        sums = [reduce_second(b, kept[b], moved[b]) for b in both]
        g_qk = line_finish([d_q, d_k], qk_moved)
        output = mark(
            jnp.concatenate(
                [x1[b] + (down[b][0] + hold(down[b][1]).astype(F32)) for b in both]
            ).astype(BF)
        )
        output_moved = grid.swap(output)
        d_inputs, gain_in_grad = [], 0.0
        for b in both:
            d_h1 = sums[b][0] + hold(sums[b][1]).astype(F32)
            d_ln, part_grad = layer_norm_back(
                d_h1, rows(scaled_in, b), rows(inverse_in, b), gain_in
            )
            gain_in_grad = gain_in_grad + part_grad
            d_inputs.append(mark(d_x1[b] + d_ln))
        d_input = jnp.concatenate(d_inputs)
        d_input_moved = grid.swap(hold(d_input))
        g_vg = await_(g_vg)[0]
        vg_moved = grid.swap(g_vg)
        output = settle(output, output_moved)
        norms = mark(grid.total_but_x(hold(jnp.stack([gain_in_grad, gain_mid_grad]))))
        g_vg = settle(g_vg, vg_moved)
        grad_norms = mark(norms + grid.flip_x(hold(norms)))
        g_out_moved = grid.swap(hold(g_out))
        g_ud = settle(g_ud, g_ud_moved)
        d_input = settle(d_input, d_input_moved)
        g_out = settle(g_out, g_out_moved)
        g_down, g_up, g_out = [
            hold(g).astype(F32) for g in (g_ud[:, hidden:].T, g_ud[:, :hidden], g_out.T)
        ]
        last[:] = [g_down, g_up, g_out]
        g_vg = mark(hold(g_vg).astype(F32))
        g_qk = await_(g_qk)[0]
        g_qk = settle(g_qk, grid.swap(g_qk)).astype(F32)
        whole = (micro, 1, piece, width)
        return (
            output.reshape(whole),
            d_input.reshape(whole),
            grad_norms,
            g_qk[:, :dk],
            g_qk[:, dk:],
            g_vg[:, :dv],
            g_vg[:, dv:],
            g_out,
            g_up,
            g_down,
        )

    return on_device


def solution(mesh):
    grid = Grid(mesh.shape["seq"], mesh.shape["fsdp"])
    rows = P("fsdp", "seq")
    cols = P("seq", "fsdp")
    tok = P(None, "fsdp", "seq", None)
    return jax.shard_map(
        make_on_device(grid),
        mesh=mesh,
        in_specs=(tok, P(), rows, rows, rows, rows, cols, rows, cols, P(None, "fsdp", None), tok),
        out_specs=(tok, tok, P(), rows, rows, rows, rows, cols, rows, cols),
        check_vma=False,
    )
```
